32 devices in a mesh: clip: 4 (over y, x), seq: 8 (over z, core).
Axes of the slice: x: 2, y: 2, z: 4, core: 2. Of those that a mesh axis runs over, the one named last changes fastest.
Arguments:
- frames: bfloat16 [2, 4, 1536, 1280], P(None, 'clip', 'seq'), may hold values from -6 to 6
- clip_ids: int32 [2, 4, 1536], P(None, 'clip'), may hold values from 0 to 1, never falling along the last dimension, each value on 1 to 1500 neighbouring positions
- query_weight: bfloat16 [1280, 1280], P(('clip', 'seq')), may hold values from -0.25 to 0.25
- key_weight: bfloat16 [1280, 1280], P(('clip', 'seq')), may hold values from -0.25 to 0.25
- value_weight: bfloat16 [1280, 1280], P(('clip', 'seq')), may hold values from -0.15625 to 0.15625
- output_weight: bfloat16 [1280, 1280], P(('clip', 'seq')), may hold values from -0.625 to 0.625
- inner_weight: bfloat16 [1280, 5120], P(('clip', 'seq')), may hold values from -0.15625 to 0.15625
- outer_weight: bfloat16 [5120, 1280], P(('clip', 'seq')), may hold values from -0.078125 to 0.078125
- query_bias: bfloat16 [1280], P(('clip', 'seq')), may hold values from -1.75 to 1.75
- value_bias: bfloat16 [1280], P(('clip', 'seq')), may hold values from -1.75 to 1.75
- output_bias: bfloat16 [1280], P(('clip', 'seq')), may hold values from -1.75 to 1.75
- inner_bias: bfloat16 [5120], P(('clip', 'seq')), may hold values from -3 to 3
- outer_bias: bfloat16 [1280], P(('clip', 'seq')), may hold values from -1.75 to 1.75
- first_gain: bfloat16 [1280], P(('clip', 'seq')), may hold values from 0.25 to 1.75
- first_shift: bfloat16 [1280], P(('clip', 'seq')), may hold values from -1.75 to 1.75
- second_gain: bfloat16 [1280], P(('clip', 'seq')), may hold values from 0.25 to 1.75
- second_shift: bfloat16 [1280], P(('clip', 'seq')), may hold values from -1.75 to 1.75
- out_cotangent: bfloat16 [2, 4, 1536, 1280], P(None, 'clip', 'seq'), may hold values from -6 to 6
Outputs:
- layer_out: bfloat16 [2, 4, 1536, 1280], P(None, 'clip', 'seq')
- frames_grad: float32 [2, 4, 1536, 1280], P(None, 'clip', 'seq')
- query_weight_grad: float32 [1280, 1280], P(('clip', 'seq'))
- key_weight_grad: float32 [1280, 1280], P(('clip', 'seq'))
- value_weight_grad: float32 [1280, 1280], P(('clip', 'seq'))
- output_weight_grad: float32 [1280, 1280], P(('clip', 'seq'))
- inner_weight_grad: float32 [1280, 5120], P(('clip', 'seq'))
- outer_weight_grad: float32 [5120, 1280], P(('clip', 'seq'))
- query_bias_grad: float32 [1280], P(('clip', 'seq'))
- value_bias_grad: float32 [1280], P(('clip', 'seq'))
- output_bias_grad: float32 [1280], P(('clip', 'seq'))
- inner_bias_grad: float32 [5120], P(('clip', 'seq'))
- outer_bias_grad: float32 [1280], P(('clip', 'seq'))
- first_gain_grad: float32 [1280], P(('clip', 'seq'))
- first_shift_grad: float32 [1280], P(('clip', 'seq'))
- second_gain_grad: float32 [1280], P(('clip', 'seq'))
- second_shift_grad: float32 [1280], P(('clip', 'seq'))
The draws below stay inside these ranges and needn't reach their ends.
Inputs may be any that keep to these rules, and one draw needn't show every extreme that they name: `clip_ids`: within each group's frames of one micro-batch the clip numbers never fall; there are 2 clips, each of 1 to 1500 frames.
All inputs are finite; a program needn't handle non-finite values.
Results may differ from the reference program's by a relative error of at most 0.017.
Values may be sent and summed in bfloat16 or wider, within the bound.
A program may use at most 320 MiB of HBM per device.

```python
import math
import jax
import jax.numpy as jnp
import numpy as np
from jax import lax

D = 1280
H = 16
HD = 80
FF = 5120
MICRO = 2
CLIP_MAX = 1500
GROUPS = 4
GROUP = 1536
CLIPS_ROW = 2


def level_of(own_key, extent, cuts, smallest, top_value):
    def one(position, blocks):
        steps = jax.random.uniform(jax.random.fold_in(jax.random.fold_in(own_key, 6), position), (blocks,), jnp.float32, smallest / len(cuts), top_value / len(cuts))
        return jnp.repeat(jnp.exp(steps), extent[position] // blocks).reshape((-1,) + (1,) * (len(extent) - position - 1))

    factor_of = one(*cuts[0])
    for cut in cuts[1:]:
        factor_of = factor_of * one(*cut)
    return factor_of


def profile(amount, total, most, lean):
    weights = [(1 << 20) // math.isqrt(standing ** lean) + 1 for standing in range(2, amount + 1)]
    rest, holding = total - most - (amount - 1), [1] * (amount - 1)
    while rest > 0:
        movable = [i for i in range(amount - 1) if holding[i] < most]
        pool, remaining = sum([weights[i] for i in movable]), rest
        for i in movable:
            addition = min(most - holding[i], max(1, remaining * weights[i] // pool), rest)
            holding[i] = holding[i] + addition
            rest = rest - addition
    return np.array([most] + holding)


def uneven(stream_key, amount, total, reach, slope):
    if amount == 2:
        one = jax.random.randint(stream_key, (), max(1, total - reach), min(reach, total - 1) + 1)
        return jnp.stack([one, total - one])
    tallies = jnp.asarray(profile(amount, total, reach, slope), jnp.int32)
    twos = (amount - 1) // 2
    giver, receiver = tallies[1:1 + 2 * twos:2], tallies[2:2 + 2 * twos:2]
    slack = jnp.minimum(giver - 1, reach - receiver)
    passed = jax.random.randint(jax.random.fold_in(stream_key, 1), (twos,), 0, 1 << 20) % (slack + 1)
    tallies = tallies.at[1:1 + 2 * twos:2].set(giver - passed).at[2:2 + 2 * twos:2].set(receiver + passed)
    return tallies[jax.random.permutation(jax.random.fold_in(stream_key, 2), amount)]


def gaussian(rng, extent, deviation, bound, cuts=(), dtype=jnp.bfloat16):
    result = deviation * jax.random.normal(rng, extent, jnp.float32)
    if cuts:
        result = result * level_of(rng, extent, cuts, -0.22, 0.18)
    return jnp.clip(result, -bound, bound).astype(dtype)


def setup_inputs(seed: int = 0) -> dict:
    splits = jax.random.split(jax.random.key(seed), 19)
    frames = gaussian(splits[0], (MICRO, GROUPS, GROUP, D), 1.0, 6.0, ((1, 4), (2, 8)))
    clip_ids = jax.vmap(lambda own: jnp.searchsorted(jnp.cumsum(uneven(own, CLIPS_ROW, GROUP, CLIP_MAX, 1)), jnp.arange(GROUP), side="right"))(jax.random.split(splits[1], MICRO * GROUPS)).reshape((MICRO, GROUPS, GROUP)).astype(jnp.int32)
    query_weight = gaussian(splits[2], (D, D), (D // 2) ** -0.5, 0.25, ((0, 32),))
    key_weight = gaussian(splits[3], (D, D), (D // 2) ** -0.5, 0.25, ((0, 32),))
    value_weight = gaussian(splits[4], (D, D), D ** -0.5, 0.15625, ((0, 32),))
    output_weight = gaussian(splits[5], (D, D), HD ** -0.5, 0.625, ((0, 32),))
    inner_weight = gaussian(splits[6], (D, FF), D ** -0.5, 0.15625, ((0, 32),))
    outer_weight = gaussian(splits[7], (FF, D), FF ** -0.5, 0.078125, ((0, 32),))
    query_bias = gaussian(splits[8], (D,), 0.3, 1.75, ((0, 32),))
    value_bias = gaussian(splits[9], (D,), 0.3, 1.75, ((0, 32),))
    output_bias = gaussian(splits[10], (D,), 0.3, 1.75, ((0, 32),))
    inner_bias = gaussian(splits[11], (FF,), 0.5, 3.0, ((0, 32),))
    outer_bias = gaussian(splits[12], (D,), 0.3, 1.75, ((0, 32),))
    first_gain = jnp.clip(1.0 + 0.15 * jax.random.normal(splits[13], (D,), jnp.float32), 0.25, 1.75).astype(jnp.bfloat16)
    first_shift = gaussian(splits[14], (D,), 0.3, 1.75, ((0, 32),))
    second_gain = jnp.clip(1.0 + 0.15 * jax.random.normal(splits[15], (D,), jnp.float32), 0.25, 1.75).astype(jnp.bfloat16)
    second_shift = gaussian(splits[16], (D,), 0.3, 1.75, ((0, 32),))
    out_cotangent = gaussian(splits[17], (MICRO, GROUPS, GROUP, D), 1.0, 6.0, ((1, 4), (2, 8)))
    return {"frames": frames, "clip_ids": clip_ids, "query_weight": query_weight, "key_weight": key_weight, "value_weight": value_weight, "output_weight": output_weight, "inner_weight": inner_weight, "outer_weight": outer_weight, "query_bias": query_bias, "value_bias": value_bias, "output_bias": output_bias, "inner_bias": inner_bias, "outer_bias": outer_bias, "first_gain": first_gain, "first_shift": first_shift, "second_gain": second_gain, "second_shift": second_shift, "out_cotangent": out_cotangent}


epsilon = 1e-05
masked_score = -1e+30

@jax.custom_vjp
def low(v):
    return lax.optimization_barrier(v.astype(jnp.bfloat16)).astype(jnp.float32)

@jax.custom_vjp
def low_back(v):
    return v

def low_keep(v):
    return (low(v), None)

def low_pass(kept, grad):
    return (grad,)

def back_keep(v):
    return (v, None)

def back_low(kept, grad):
    return (low(grad),)
low.defvjp(low_keep, low_pass)
low_back.defvjp(back_keep, back_low)

def layer_norm(row_values, gain_row, shift_row):
    centre = lax.optimization_barrier(jnp.mean(row_values, axis=-1, keepdims=True))
    centred = row_values - centre
    spread = lax.optimization_barrier(jnp.mean(centred * centred, axis=-1, keepdims=True))
    return centred * lax.rsqrt(spread + epsilon) * gain_row + shift_row

def matmul(left_side, right_side):
    return jnp.dot(left_side, right_side, precision=lax.Precision.HIGHEST)

def rounded_both(values):
    return low_back(low(values))

def attend_block(query_block, block_ids, key_rows, value_rows, group_ids):
    rows_here = query_block.shape[0]
    queries = query_block.reshape(rows_here, H, HD)
    keys_split = key_rows.reshape(key_rows.shape[0], H, HD)
    values_split = value_rows.reshape(value_rows.shape[0], H, HD)
    raw_scores = low_back(jnp.einsum('qhd,khd->hqk', queries, keys_split, precision=lax.Precision.HIGHEST))
    same_clip = block_ids[:, None] == group_ids[None, :]
    scores = jnp.where(same_clip[None, :, :], raw_scores * HD ** (-0.5), masked_score)
    row_top = lax.optimization_barrier(jnp.max(scores, axis=-1, keepdims=True))
    exponent = jnp.exp(scores - row_top)
    probs = low(exponent / lax.optimization_barrier(jnp.sum(exponent, axis=-1, keepdims=True)))
    mixed_part = jnp.einsum('hqk,khd->qhd', probs, values_split, precision=lax.Precision.HIGHEST)
    return mixed_part.reshape(rows_here, H * HD)

def one_row(params, frame_values, group_ids):
    query_full, key_full, value_full, output_full, inner_full, outer_full, query_shift, value_shift, output_shift, inner_shift, outer_shift, gain_one, shift_one, gain_two, shift_two = params
    normed = low(layer_norm(frame_values, gain_one, shift_one))
    query_rows = rounded_both(matmul(normed, query_full) + query_shift)
    key_rows = rounded_both(matmul(normed, key_full))
    value_rows = rounded_both(matmul(normed, value_full) + value_shift)
    block_rows = min(512, GROUP)
    block_count = GROUP // block_rows
    query_blocks = query_rows.reshape(block_count, block_rows, D)
    id_blocks = group_ids.reshape(block_count, block_rows)

    def one_block(block_pair):
        return attend_block(block_pair[0], block_pair[1], key_rows, value_rows, group_ids)
    attended = lax.map(jax.checkpoint(one_block), (query_blocks, id_blocks))
    attended = rounded_both(attended.reshape(GROUP, D))
    branch = low_back(matmul(attended, output_full) + output_shift)
    middle = frame_values + branch
    normed_two = low(layer_norm(middle, gain_two, shift_two))
    inner_rows = low_back(matmul(normed_two, inner_full) + inner_shift)
    active = low(jax.nn.gelu(inner_rows, approximate=False))
    return middle + (matmul(active, outer_full) + outer_shift)

def reference(frames, clip_ids, query_weight, key_weight, value_weight, output_weight, inner_weight, outer_weight, query_bias, value_bias, output_bias, inner_bias, outer_bias, first_gain, first_shift, second_gain, second_shift, out_cotangent):
    params = tuple((piece.astype(jnp.float32) for piece in (query_weight, key_weight, value_weight, output_weight, inner_weight, outer_weight, query_bias, value_bias, output_bias, inner_bias, outer_bias, first_gain, first_shift, second_gain, second_shift)))
    row_count = MICRO * GROUPS
    frame_rows = frames.astype(jnp.float32).reshape(row_count, GROUP, D)
    id_rows = clip_ids.reshape(row_count, GROUP)

    def forward(param_set, row_values):

        def one_group(group_pair):
            return jax.checkpoint(one_row)(param_set, group_pair[0], group_pair[1])
        return lax.map(one_group, (row_values, id_rows))
    outputs, pullback = jax.vjp(forward, params, frame_rows)
    grad_tuple, frame_grads = pullback(out_cotangent.astype(jnp.float32).reshape(row_count, GROUP, D))
    layer_out = outputs.astype(jnp.bfloat16).reshape(MICRO, GROUPS, GROUP, D)
    frames_grad = frame_grads.reshape(MICRO, GROUPS, GROUP, D)
    return (layer_out, frames_grad, grad_tuple[0], grad_tuple[1], grad_tuple[2], grad_tuple[3], grad_tuple[4], grad_tuple[5], grad_tuple[6], grad_tuple[7], grad_tuple[8], grad_tuple[9], grad_tuple[10], grad_tuple[11], grad_tuple[12], grad_tuple[13], grad_tuple[14])
```

```python
import functools
import math

import jax
import jax.numpy as jnp
from jax import lax
from jax.experimental import pallas as pl
from jax.experimental.pallas import tpu as pltpu
from jax.sharding import Mesh
from jax.sharding import PartitionSpec as P

H = 16
HD = 80
TAGS = 16
epsilon = 1e-05
masked_score = -1e30
low = jnp.bfloat16
wide = jnp.float32


def dims(left_side, right_side, left_dim, right_dim):
    return lax.dot_general(
        left_side,
        right_side,
        (((left_dim,), (right_dim,)), ((), ())),
        preferred_element_type=wide,
    )


def attend_forward_kernel(blocks, q_ref, qa_ref, k_ref, v_ref, ka_ref, out_ref, log_ref):
    factor = HD ** (-0.5) * math.log2(math.e)
    query = jnp.concatenate([q_ref[...], qa_ref[...]], axis=0)
    scores = []
    for b in range(blocks):
        key = jnp.concatenate([k_ref[b], ka_ref[b]], axis=0)
        scores.append(dims(key, query, 0, 0))
    top = functools.reduce(jnp.maximum, [jnp.max(s, axis=0, keepdims=True) for s in scores])
    top = top * factor
    total = jnp.zeros_like(top)
    mixed = jnp.zeros((HD, query.shape[1]), wide)
    for b in range(blocks):
        part = jnp.exp2(scores[b] * factor - top)
        total = total + jnp.sum(part, axis=0, keepdims=True)
        mixed = mixed + dims(v_ref[b], part.astype(low), 1, 0)
    out_ref[...] = (mixed / total).astype(low)
    log_ref[0] = top + jnp.log2(total)


def attend_forward(q_t, tags_q, kv, tags_k, heads, tile):
    blocks, _, width = kv.shape
    rows = q_t.shape[1]
    grid = (heads, rows // tile)
    return pl.pallas_call(
        functools.partial(attend_forward_kernel, blocks),
        grid=grid,
        out_shape=(
            jax.ShapeDtypeStruct((heads * HD, rows), low),
            jax.ShapeDtypeStruct((heads, 1, rows), wide),
        ),
        in_specs=[
            pl.BlockSpec((HD, tile), lambda h, t: (h, t)),
            pl.BlockSpec((TAGS, tile), lambda h, t: (0, t)),
            pl.BlockSpec((blocks, HD, width), lambda h, t: (0, h, 0)),
            pl.BlockSpec((blocks, HD, width), lambda h, t: (0, heads + h, 0)),
            pl.BlockSpec((blocks, TAGS, width), lambda h, t: (0, 0, 0)),
        ],
        out_specs=(
            pl.BlockSpec((HD, tile), lambda h, t: (h, t)),
            pl.BlockSpec((1, 1, tile), lambda h, t: (h, 0, t)),
        ),
        cost_estimate=pl.CostEstimate(
            flops=4 * heads * rows * blocks * width * HD,
            bytes_accessed=2 * kv.size,
            transcendentals=heads * rows * blocks * width,
        ),
        name="attend_forward",
    )(q_t, tags_q, kv, kv, tags_k)


def attend_backward_kernel(
    blocks, q_ref, qa_ref, k_ref, v_ref, ka_ref, o_ref, log_ref, g_ref, dq_ref, own_ref, far_ref, acc_k, acc_v
):
    factor = HD ** (-0.5) * math.log2(math.e)
    step, steps = pl.program_id(1), pl.num_programs(1)
    head_query = q_ref[...]
    grad = g_ref[...]
    query = jnp.concatenate([head_query, qa_ref[...]], axis=0)
    delta = jnp.sum(grad.astype(wide) * o_ref[...].astype(wide), axis=0, keepdims=True)
    logs = log_ref[0]
    query_rows = head_query.T
    grad_rows = grad.T
    dq = jnp.zeros(head_query.shape, wide)

    @pl.when(step == 0)
    def _():
        acc_k[...] = jnp.zeros_like(acc_k)
        acc_v[...] = jnp.zeros_like(acc_v)

    for b in range(blocks):
        key = jnp.concatenate([k_ref[b], ka_ref[b]], axis=0)
        probs = jnp.exp2(dims(key, query, 0, 0) * factor - logs)
        grad_probs = dims(v_ref[b], grad, 0, 0)
        score_grad = (probs * (grad_probs - delta)).astype(low)
        acc_v[b] += dims(probs.astype(low), grad_rows, 1, 0)
        acc_k[b] += dims(score_grad, query_rows, 1, 0)
        dq = dq + dims(k_ref[b], score_grad, 1, 0)
    dq_ref[...] = (dq * HD ** (-0.5)).astype(low)

    @pl.when(step == steps - 1)
    def _():
        for b in range(blocks):
            key_part = acc_k[b].T * HD ** (-0.5)
            value_part = acc_v[b].T
            if b == 0:
                own_ref[0] = key_part
                own_ref[1] = value_part
            else:
                far_ref[b - 1, 0] = key_part.astype(low)
                far_ref[b - 1, 1] = value_part.astype(low)


def attend_backward(q_t, tags_q, kv, tags_k, mixed_t, logs, grad_t, heads, tile):
    blocks, _, width = kv.shape
    rows = q_t.shape[1]
    grid = (heads, rows // tile)
    per_query = pl.BlockSpec((HD, tile), lambda h, t: (h, t))
    return pl.pallas_call(
        functools.partial(attend_backward_kernel, blocks),
        grid=grid,
        out_shape=(
            jax.ShapeDtypeStruct((heads * HD, rows), low),
            jax.ShapeDtypeStruct((2, heads * HD, width), wide),
            jax.ShapeDtypeStruct((blocks - 1, 2, heads * HD, width), low),
        ),
        in_specs=[
            per_query,
            pl.BlockSpec((TAGS, tile), lambda h, t: (0, t)),
            pl.BlockSpec((blocks, HD, width), lambda h, t: (0, h, 0)),
            pl.BlockSpec((blocks, HD, width), lambda h, t: (0, heads + h, 0)),
            pl.BlockSpec((blocks, TAGS, width), lambda h, t: (0, 0, 0)),
            per_query,
            pl.BlockSpec((1, 1, tile), lambda h, t: (h, 0, t)),
            per_query,
        ],
        out_specs=(
            per_query,
            pl.BlockSpec((2, HD, width), lambda h, t: (0, h, 0)),
            pl.BlockSpec((blocks - 1, 2, HD, width), lambda h, t: (0, 0, h, 0)),
        ),
        scratch_shapes=[
            pltpu.VMEM((blocks, width, HD), wide),
            pltpu.VMEM((blocks, width, HD), wide),
        ],
        cost_estimate=pl.CostEstimate(
            flops=10 * heads * rows * blocks * width * HD,
            bytes_accessed=4 * kv.size,
            transcendentals=heads * rows * blocks * width,
        ),
        name="attend_backward",
    )(q_t, tags_q, kv, kv, tags_k, mixed_t, logs, grad_t)


CHIPS = ("cy", "cx", "zz")


def gather_blocks(shards):
    return tuple(lax.all_gather(s, CHIPS, axis=0, tiled=False) for s in shards)


def scatter_blocks(blocks):
    return tuple(
        lax.psum_scatter(b, CHIPS, scatter_dimension=0, tiled=False).astype(wide) for b in blocks
    )


def row_stats(values):
    centre = jnp.mean(values, axis=-1, keepdims=True)
    centred = values - centre
    inverse = lax.rsqrt(jnp.mean(centred * centred, axis=-1, keepdims=True) + epsilon)
    return centred * inverse, inverse


def norm_pull(grad, gain, xhat, inverse):
    e = grad * gain
    return inverse * (
        e
        - jnp.mean(e, axis=-1, keepdims=True)
        - xhat * jnp.mean(e * xhat, axis=-1, keepdims=True)
    )


def gelu_parts(u):
    phi_sum = 0.5 * (1.0 + lax.erf(u * math.sqrt(0.5)))
    density = jnp.exp(-0.5 * u * u) * (1.0 / math.sqrt(2.0 * math.pi))
    return u * phi_sum, phi_sum + u * density


def body(
    n_chip_rows,
    Z,
    frames,
    clip_ids,
    query_weight,
    key_weight,
    value_weight,
    output_weight,
    inner_weight,
    outer_weight,
    query_bias,
    value_bias,
    output_bias,
    inner_bias,
    outer_bias,
    first_gain,
    first_shift,
    second_gain,
    second_shift,
    out_cotangent,
):
    K = n_chip_rows * Z
    R, D = frames.shape[2], frames.shape[3]
    FF = inner_weight.shape[1]
    r = query_weight.shape[0]
    f = outer_weight.shape[0]
    hw = D // 2
    heads = H // 2
    half = Z // 2
    core = lax.axis_index("core")
    first_core = core == 0
    zz = lax.axis_index("zz")
    micro = zz // half
    first_half = micro == 0
    place = zz % half

    def swap_core(v):
        return lax.ppermute(v, "core", [(0, 1), (1, 0)])

    def swap_half(v):
        return lax.ppermute(v, "zz", [(z, (z + half) % Z) for z in range(Z)])

    def by_core(own, other, axis):
        return jnp.where(
            first_core,
            jnp.concatenate([own, other], axis),
            jnp.concatenate([other, own], axis),
        )

    def pick(v, index, axis):
        return lax.dynamic_index_in_dim(v, index, axis, keepdims=False)

    def take_rows(v):
        v = v[:, 0]
        own, away = pick(v, micro, 0), pick(v, 1 - micro, 0)
        got = swap_half(away)
        pair = jnp.where(first_half, jnp.stack([own, got]), jnp.stack([got, own]))
        both = by_core(pair[:, None], swap_core(pair)[:, None], 1)
        return both.reshape(4 * R, D)

    qkv = jnp.stack([query_weight, key_weight, value_weight], 1).reshape(r, 3, 2, hw)
    inner_split = inner_weight.reshape(r, K, 2, f)
    vectors = (
        query_bias, value_bias, output_bias, outer_bias,
        first_gain, first_shift, second_gain, second_shift, inner_bias,
    )
    small = jnp.concatenate(vectors)
    n_small = small.shape[0]

    def column_half(which):
        return jnp.concatenate(
            [
                pick(qkv, which, 2).reshape(r, 3 * hw),
                pick(inner_split, which, 2).reshape(r, FF // 2),
            ],
            1,
        )

    mine = column_half(core)
    theirs = swap_core(column_half(1 - core))
    both = by_core(mine[None], theirs[None], 0)
    small_both = by_core(small[None], swap_core(small)[None], 0)
    small_pad = -(-n_small // 1024) * 1024
    small_both = jnp.pad(small_both, ((0, 0), (0, small_pad - n_small)))
    shards = (
        small_both.reshape(2, small_pad // 128, 128),
        both[:, :, : 3 * hw],
        output_weight.reshape(r, 2, hw).transpose(1, 0, 2),
        both[:, :, 3 * hw :],
        outer_weight.reshape(2, f // 2, D),
    )
    small_all, qkv_all, out_all, inner_all, outer_all = gather_blocks(shards)
    x_rows = take_rows(frames)
    cot = take_rows(out_cotangent)

    w_qkv = qkv_all.reshape(D, 3 * hw)
    w_inner = inner_all.reshape(D, FF // 2)
    w_outer = outer_all.reshape(FF // 2, D)
    out_own = out_all.transpose(0, 2, 1, 3).reshape(K, 1, r, D)
    w_out = by_core(out_own, swap_core(out_own), 1).reshape(D, D)
    small_all = small_all.reshape(K, 2, small_pad)[:, :, :n_small].astype(wide)
    names = ("qb", "vb", "ob", "ub", "g1", "s1", "g2", "s2")
    vec = {n: small_all[:, :, i * r : (i + 1) * r].reshape(D) for i, n in enumerate(names)}
    ib_half = pick(small_all[:, :, 8 * r :], core, 1).reshape(FF // 2)

    def own_columns(v):
        return lax.dynamic_slice_in_dim(v, core * hw, hw, v.ndim - 1)

    ids = pick(clip_ids[:, 0], micro, 0).reshape(2, half, 2 * R)
    ids_q = pick(ids, place, 1).reshape(4 * R)
    order = (place - jnp.arange(half)) % half
    ids_k = jnp.take(ids, order, axis=1).transpose(1, 0, 2).reshape(half, 4 * R)
    tag = jnp.arange(TAGS, dtype=jnp.int32)[:, None]
    tags_q = jnp.where(ids_q[None, :] == tag, 0.0, masked_score).astype(low)
    tags_k = (ids_k[:, None, :] == tag[None]).astype(low)

    xf = x_rows.astype(wide)
    xhat, inverse = row_stats(xf)
    normed = (xhat * vec["g1"] + vec["s1"]).astype(low)
    bias_qkv = jnp.concatenate(
        [own_columns(vec["qb"]), jnp.zeros((hw,), wide), own_columns(vec["vb"])]
    )
    qkv_t = (dims(w_qkv, normed, 0, 1) + bias_qkv[:, None]).astype(low)
    q_t, kv_own = qkv_t[:hw], qkv_t[hw:]
    kv_parts = [kv_own]
    for o in range(1, half):
        kv_parts.append(
            lax.ppermute(
                kv_own, "zz", [(z, (z // half) * half + (z + o) % half) for z in range(Z)]
            )
        )
    kv = jnp.stack(kv_parts)
    tile = 256
    mixed_t, logs = attend_forward(q_t, tags_q, kv, tags_k, heads, tile)
    mixed_full = by_core(mixed_t, swap_core(mixed_t), 0)
    middle = xf + (dims(mixed_full, w_out, 0, 0) + vec["ob"])
    xhat_two, inverse_two = row_stats(middle)
    normed_two = (xhat_two * vec["g2"] + vec["s2"]).astype(low)
    inner = dims(normed_two, w_inner, 1, 0) + ib_half
    active, slope = gelu_parts(inner)
    active = active.astype(low)
    out_part = dims(active, w_outer, 1, 0)

    def split_rows(v):
        return v.reshape(2, 2, R, D)

    def reduce_rows(v):
        v = split_rows(v)
        return pick(v, core, 1) + swap_core(pick(v, 1 - core, 1).astype(low)).astype(wide)

    def home_rows(v):
        stay = pick(v, micro, 0)
        got = swap_half(pick(v, 1 - micro, 0))
        return jnp.where(first_half, jnp.stack([stay, got]), jnp.stack([got, stay]))[:, None]

    own_middle = pick(split_rows(middle), core, 1)
    layer_rows = (own_middle + (reduce_rows(out_part) + vec["ub"])).astype(low)
    layer_out = home_rows(layer_rows)

    grad_active = dims(cot, w_outer, 1, 1)
    inner_grad = (grad_active * slope).astype(low)
    part_two = dims(inner_grad, w_inner, 1, 1)
    grad_two = part_two + swap_core(part_two.astype(low)).astype(wide)
    middle_grad = cot.astype(wide) + norm_pull(grad_two, vec["g2"], xhat_two, inverse_two)
    branch_grad = middle_grad.astype(low)
    w_out_heads = lax.dynamic_slice_in_dim(w_out, core * hw, hw, 0)
    mixed_grad = dims(w_out_heads, branch_grad, 1, 1).astype(low)
    dq_t, own_kv, far_kv = attend_backward(
        q_t, tags_q, kv, tags_k, mixed_t, logs, mixed_grad, heads, tile
    )
    dkv = own_kv.reshape(2 * hw, 4 * R)
    for o in range(1, half):
        back = lax.ppermute(
            far_kv[o - 1], "zz", [(z, (z // half) * half + (z - o) % half) for z in range(Z)]
        )
        dkv = dkv + back.reshape(2 * hw, 4 * R).astype(wide)
    dqkv_t = jnp.concatenate([dq_t, dkv.astype(low)], 0)
    grad_one = reduce_rows(dims(dqkv_t, w_qkv, 0, 1))
    own_xhat = pick(split_rows(xhat), core, 1)
    own_inverse = pick(inverse.reshape(2, 2, R, 1), core, 1)
    frame_rows = pick(split_rows(middle_grad), core, 1) + norm_pull(
        grad_one, vec["g1"], own_xhat, own_inverse
    )
    sent = swap_half(pick(frame_rows, 1 - micro, 0).astype(low)).astype(wide)
    stay = pick(frame_rows, micro, 0)
    frames_grad = jnp.where(first_half, jnp.stack([stay, sent]), jnp.stack([sent, stay]))[:, None]

    g_qkv = dims(normed, dqkv_t, 0, 1).astype(low)
    g_out = dims(mixed_full, own_columns(branch_grad), 1, 0).astype(low)
    g_inner = dims(normed_two, inner_grad, 0, 0).astype(low)
    g_outer = dims(active, cot, 0, 0).astype(low)

    def zero_rest(v):
        return by_core(v, jnp.zeros_like(v), 0)

    bias_sums = jnp.sum(dqkv_t.astype(wide), axis=1)
    halves = 0.5
    col = {
        "qb": zero_rest(bias_sums[:hw]),
        "vb": zero_rest(bias_sums[2 * hw :]),
        "ob": halves * jnp.sum(branch_grad.astype(wide), 0),
        "ub": halves * jnp.sum(cot.astype(wide), 0),
        "g1": jnp.sum(grad_one * own_xhat, (0, 1)),
        "s1": jnp.sum(grad_one, (0, 1)),
        "g2": halves * jnp.sum(grad_two * xhat_two, 0),
        "s2": halves * jnp.sum(grad_two, 0),
    }
    ib_sum = jnp.sum(inner_grad.astype(wide), 0).reshape(K, 1, f)
    small_grad = jnp.concatenate(
        [col[n].reshape(K, 2, r) for n in names]
        + [by_core(ib_sum, jnp.zeros_like(ib_sum), 1)],
        2,
    )
    small_grad = jnp.pad(small_grad, ((0, 0), (0, 0), (0, small_pad - n_small)))
    small_grad = small_grad.reshape(K, 2, small_pad // 128, 128).astype(low)
    g_outer, g_inner, g_out, g_qkv, g_small = scatter_blocks(
        (
            g_outer.reshape(K, 2, f // 2, D),
            g_inner.reshape(K, 2, r, FF // 2),
            g_out.reshape(K, 2, r, hw),
            g_qkv.reshape(K, 2, r, 3 * hw),
            small_grad,
        )
    )
    wide_rows = jnp.concatenate([g_qkv, g_out, g_inner], 2)
    mine = pick(wide_rows, core, 0)
    theirs = swap_core(pick(wide_rows, 1 - core, 0))

    def whole(a, b, parts):
        a, b = a.reshape(r, parts, 1, -1), b.reshape(r, parts, 1, -1)
        return by_core(a, b, 2).reshape(r, -1)

    outs = []
    for i in range(4):
        outs.append(whole(mine[:, i * hw : (i + 1) * hw], theirs[:, i * hw : (i + 1) * hw], 1))
    outs.append(whole(mine[:, 4 * hw :], theirs[:, 4 * hw :], K))
    outs.append(g_outer.reshape(f, D))
    g_small = g_small.reshape(2, small_pad)[:, :n_small]
    g_small = pick(g_small, core, 0) + swap_core(pick(g_small, 1 - core, 0))
    sv = {n: g_small[i * r : (i + 1) * r] for i, n in enumerate(names)}
    return (layer_out, frames_grad) + tuple(outs) + (
        sv["qb"], sv["vb"], sv["ob"], g_small[8 * r :], sv["ub"],
        sv["g1"], sv["s1"], sv["g2"], sv["s2"],
    )


def solution(mesh):
    C, S = mesh.shape["clip"], mesh.shape["seq"]
    fine = Mesh(mesh.devices.reshape(2, C // 2, S // 2, 2), ("cy", "cx", "zz", "core"))
    clip, seq = ("cy", "cx"), ("zz", "core")
    every = clip + seq
    rows, mat, vec = P(None, clip, seq, None), P(every, None), P(every)
    in_specs = (rows, P(None, clip, None)) + (mat,) * 6 + (vec,) * 9 + (rows,)
    out_specs = (rows, rows) + (mat,) * 6 + (vec,) * 9
    return jax.shard_map(
        functools.partial(body, C, S // 2),
        mesh=fine,
        in_specs=in_specs,
        out_specs=out_specs,
        check_vma=False,
    )
```

```python
import functools
import math

import jax
import jax.numpy as jnp
from jax import lax
from jax.experimental import pallas as pl
from jax.experimental.pallas import tpu as pltpu
from jax.sharding import Mesh
from jax.sharding import PartitionSpec as P

H = 16
HD = 80
TAGS = 16
epsilon = 1e-05
masked_score = -1e30
low = jnp.bfloat16
wide = jnp.float32


def dims(left_side, right_side, left_dim, right_dim):
    return lax.dot_general(
        left_side,
        right_side,
        (((left_dim,), (right_dim,)), ((), ())),
        preferred_element_type=wide,
    )


def attend_forward_kernel(blocks, q_ref, qa_ref, k_ref, v_ref, ka_ref, out_ref, log_ref):
    factor = HD ** (-0.5) * math.log2(math.e)
    query = jnp.concatenate([q_ref[...], qa_ref[...]], axis=0)
    scores = []
    for b in range(blocks):
        key = jnp.concatenate([k_ref[b], ka_ref[b]], axis=0)
        scores.append(dims(key, query, 0, 0))
    top = functools.reduce(jnp.maximum, [jnp.max(s, axis=0, keepdims=True) for s in scores])
    top = top * factor
    total = jnp.zeros_like(top)
    mixed = jnp.zeros((HD, query.shape[1]), wide)
    for b in range(blocks):
        part = jnp.exp2(scores[b] * factor - top)
        total = total + jnp.sum(part, axis=0, keepdims=True)
        mixed = mixed + dims(v_ref[b], part.astype(low), 1, 0)
    out_ref[...] = (mixed / total).astype(low)
    log_ref[0] = top + jnp.log2(total)


def attend_forward(q_t, tags_q, kv, tags_k, heads, tile):
    blocks, _, width = kv.shape
    rows = q_t.shape[1]
    grid = (heads, rows // tile)
    return pl.pallas_call(
        functools.partial(attend_forward_kernel, blocks),
        grid=grid,
        out_shape=(
            jax.ShapeDtypeStruct((heads * HD, rows), low),
            jax.ShapeDtypeStruct((heads, 1, rows), wide),
        ),
        in_specs=[
            pl.BlockSpec((HD, tile), lambda h, t: (h, t)),
            pl.BlockSpec((TAGS, tile), lambda h, t: (0, t)),
            pl.BlockSpec((blocks, HD, width), lambda h, t: (0, h, 0)),
            pl.BlockSpec((blocks, HD, width), lambda h, t: (0, heads + h, 0)),
            pl.BlockSpec((blocks, TAGS, width), lambda h, t: (0, 0, 0)),
        ],
        out_specs=(
            pl.BlockSpec((HD, tile), lambda h, t: (h, t)),
            pl.BlockSpec((1, 1, tile), lambda h, t: (h, 0, t)),
        ),
        cost_estimate=pl.CostEstimate(
            flops=4 * heads * rows * blocks * width * HD,
            bytes_accessed=2 * kv.size,
            transcendentals=heads * rows * blocks * width,
        ),
        name="attend_forward",
    )(q_t, tags_q, kv, kv, tags_k)


def attend_backward_kernel(
    blocks, q_ref, qa_ref, k_ref, v_ref, ka_ref, o_ref, log_ref, g_ref, dq_ref, own_ref, far_ref, acc_k, acc_v
):
    factor = HD ** (-0.5) * math.log2(math.e)
    step, steps = pl.program_id(1), pl.num_programs(1)
    head_query = q_ref[...]
    grad = g_ref[...]
    query = jnp.concatenate([head_query, qa_ref[...]], axis=0)
    delta = jnp.sum(grad.astype(wide) * o_ref[...].astype(wide), axis=0, keepdims=True)
    logs = log_ref[0]
    query_rows = head_query.T
    grad_rows = grad.T
    dq = jnp.zeros(head_query.shape, wide)

    @pl.when(step == 0)
    def _():
        acc_k[...] = jnp.zeros_like(acc_k)
        acc_v[...] = jnp.zeros_like(acc_v)

    for b in range(blocks):
        key = jnp.concatenate([k_ref[b], ka_ref[b]], axis=0)
        probs = jnp.exp2(dims(key, query, 0, 0) * factor - logs)
        grad_probs = dims(v_ref[b], grad, 0, 0)
        score_grad = (probs * (grad_probs - delta)).astype(low)
        acc_v[b] += dims(probs.astype(low), grad_rows, 1, 0)
        acc_k[b] += dims(score_grad, query_rows, 1, 0)
        dq = dq + dims(k_ref[b], score_grad, 1, 0)
    dq_ref[...] = (dq * HD ** (-0.5)).astype(low)

    @pl.when(step == steps - 1)
    def _():
        for b in range(blocks):
            key_part = acc_k[b].T * HD ** (-0.5)
            value_part = acc_v[b].T
            if b == 0:
                own_ref[0] = key_part
                own_ref[1] = value_part
            else:
                far_ref[b - 1, 0] = key_part.astype(low)
                far_ref[b - 1, 1] = value_part.astype(low)


def attend_backward(q_t, tags_q, kv, tags_k, mixed_t, logs, grad_t, heads, tile):
    blocks, _, width = kv.shape
    rows = q_t.shape[1]
    grid = (heads, rows // tile)
    per_query = pl.BlockSpec((HD, tile), lambda h, t: (h, t))
    return pl.pallas_call(
        functools.partial(attend_backward_kernel, blocks),
        grid=grid,
        out_shape=(
            jax.ShapeDtypeStruct((heads * HD, rows), low),
            jax.ShapeDtypeStruct((2, heads * HD, width), wide),
            jax.ShapeDtypeStruct((blocks - 1, 2, heads * HD, width), low),
        ),
        in_specs=[
            per_query,
            pl.BlockSpec((TAGS, tile), lambda h, t: (0, t)),
            pl.BlockSpec((blocks, HD, width), lambda h, t: (0, h, 0)),
            pl.BlockSpec((blocks, HD, width), lambda h, t: (0, heads + h, 0)),
            pl.BlockSpec((blocks, TAGS, width), lambda h, t: (0, 0, 0)),
            per_query,
            pl.BlockSpec((1, 1, tile), lambda h, t: (h, 0, t)),
            per_query,
        ],
        out_specs=(
            per_query,
            pl.BlockSpec((2, HD, width), lambda h, t: (0, h, 0)),
            pl.BlockSpec((blocks - 1, 2, HD, width), lambda h, t: (0, 0, h, 0)),
        ),
        scratch_shapes=[
            pltpu.VMEM((blocks, width, HD), wide),
            pltpu.VMEM((blocks, width, HD), wide),
        ],
        cost_estimate=pl.CostEstimate(
            flops=10 * heads * rows * blocks * width * HD,
            bytes_accessed=4 * kv.size,
            transcendentals=heads * rows * blocks * width,
        ),
        name="attend_backward",
    )(q_t, tags_q, kv, kv, tags_k, mixed_t, logs, grad_t)


CHIPS = ("cy", "cx", "zz")
MESH = pl.DeviceIdType.MESH


def offsets(Z):
    steps = []
    for d in range(1, Z):
        steps += [-d, d]
    return steps


class Links:
    def __init__(self, Z):
        self.Z = Z
        self.y, self.x, self.z = (lax.axis_index(a) for a in CHIPS)

    def chip(self, y, x, z):
        return (y * 2 + x) * self.Z + z

    def sides(self, colour):
        return (("cx", "cy"), ("cy", "cx"))[colour]

    def at(self, flipped, z):
        y = 1 - self.y if "cy" in flipped else self.y
        x = 1 - self.x if "cx" in flipped else self.x
        return self.chip(y, x, z)

    def peer(self, axis):
        return {axis: 1 - (self.y if axis == "cy" else self.x)}

    def has(self, step):
        there = self.z + step
        return jnp.logical_and(there >= 0, there < self.Z)

    def barrier(self):
        sem = pltpu.get_barrier_semaphore()
        for axis in ("cy", "cx"):
            pl.semaphore_signal(sem, inc=1, device_id=self.peer(axis), device_id_type=MESH)
        for step in (-1, 1):

            @pl.when(self.has(step))
            def _():
                pl.semaphore_signal(
                    sem, inc=1, device_id={"zz": self.z + step}, device_id_type=MESH
                )

        ends = jnp.minimum(self.z, 1) + jnp.minimum(self.Z - 1 - self.z, 1)
        pl.semaphore_wait(sem, 2 + ends)


class Gather:
    def __init__(self, links, shards, outs, send_sem, recv_sem):
        self.l, self.shards, self.outs = links, shards, outs
        self.send_sem, self.recv_sem = send_sem, recv_sem
        self.sent = []

    def copy(self, i, colour, k, slot, target, own=False):
        block = self.outs[i].at[k, colour]
        return pltpu.make_async_remote_copy(
            src_ref=self.shards[i].at[colour] if own else block,
            dst_ref=block,
            send_sem=self.send_sem.at[i, colour, slot],
            recv_sem=self.recv_sem.at[i, colour, k],
            device_id=target,
            device_id_type=MESH,
        )

    def send(self, conds, *what):
        cond = functools.reduce(jnp.logical_and, conds) if conds else None

        def start():
            self.copy(*what).start()

        if cond is None:
            start()
        else:
            pl.when(cond)(start)
        self.sent.append((cond, what))

    def arrive(self, i, colour, k):
        self.copy(i, colour, k, 0, {"zz": self.l.z}).wait_recv()

    def own(self, i):
        l, Z = self.l, self.l.Z
        for colour in (0, 1):
            near, far = l.sides(colour)
            k = l.at((), l.z)
            for step, base in ((1, 0), (-1, Z)):
                self.send([l.has(step)], i, colour, k, base + l.z, {"zz": l.z + step}, True)
            self.send([], i, colour, k, 3 * Z + l.z, l.peer(far), True)
            self.send([], i, colour, k, 2 * Z + l.z, l.peer(near), True)

    def along(self, i, step):
        l, Z = self.l, self.l.Z
        for colour in (0, 1):
            near, far = l.sides(colour)
            z = l.z + step
            k = l.at((), z)
            valid = l.has(step)

            @pl.when(valid)
            def _():
                self.arrive(i, colour, k)

            onward = 1 if step < 0 else -1
            self.send(
                [valid, l.has(onward)],
                i, colour, k, (0 if step < 0 else Z) + z, {"zz": l.z + onward},
            )
            self.send([valid], i, colour, k, 3 * Z + z, l.peer(far))
            self.send([valid], i, colour, k, 2 * Z + z, l.peer(near))

    def across(self, i, step):
        l, Z = self.l, self.l.Z
        for colour in (0, 1):
            near, far = l.sides(colour)
            z = l.z + step
            k = l.at((near,), z)
            valid = l.has(step) if step else None

            def arrive():
                self.arrive(i, colour, k)

            if step:
                pl.when(valid)(arrive)
            else:
                arrive()
            self.send([valid] if step else [], i, colour, k, 4 * Z + z, l.peer(far))

    def last(self, i):
        l = self.l
        for colour in (0, 1):
            near, far = l.sides(colour)
            for step in [0] + offsets(l.Z):
                for flips in ((far,), (far, near)):
                    k = l.at(flips, l.z + step)

                    def arrive():
                        self.arrive(i, colour, k)

                    if step:
                        pl.when(l.has(step))(arrive)
                    else:
                        arrive()

    def drain(self):
        for cond, what in self.sent:

            def wait():
                self.copy(*what).wait_send()

            if cond is None:
                wait()
            else:
                pl.when(cond)(wait)

    def ticks(self):
        n = len(self.shards)
        steps = offsets(self.l.Z)
        out = [lambda: self.own(0)]
        for i in range(n):

            def first(i=i):
                self.across(i, 0)
                if i + 1 < n:
                    self.own(i + 1)

            out.append(first)
            for s in range(0, len(steps), 2):

                def later(i=i, s=s):
                    self.along(i, steps[s])
                    self.along(i, steps[s + 1])
                    self.across(i, steps[s])
                    self.across(i, steps[s + 1])

                out.append(later)
        for i in range(n):
            out.append(lambda i=i: self.last(i))
        out.append(self.drain)
        return out


def gather_kernel(Z, n, *refs):
    shards, outs = refs[:n], refs[n : 2 * n]
    send_sem, recv_sem, own_sem = refs[2 * n :]
    links = Links(Z)
    links.barrier()
    gather = Gather(links, shards, outs, send_sem, recv_sem)
    mine = [
        pltpu.make_async_copy(shards[i], outs[i].at[links.at((), links.z)], own_sem.at[i])
        for i in range(n)
    ]
    for copy in mine:
        copy.start()
    for tick in gather.ticks():
        tick()
    for copy in mine:
        copy.wait()


def gather_blocks(shards, Z, K):
    if K != 4 * Z or Z > 4:
        return tuple(lax.all_gather(s, CHIPS, axis=0, tiled=False) for s in shards)
    n = len(shards)
    return pl.pallas_call(
        functools.partial(gather_kernel, Z, n),
        out_shape=tuple(jax.ShapeDtypeStruct((K,) + s.shape, s.dtype) for s in shards),
        in_specs=[pl.BlockSpec(memory_space=pltpu.VMEM)] * n,
        out_specs=tuple([pl.BlockSpec(memory_space=pl.ANY)] * n),
        scratch_shapes=[
            pltpu.SemaphoreType.DMA((n, 2, 5 * Z)),
            pltpu.SemaphoreType.DMA((n, 2, K)),
            pltpu.SemaphoreType.DMA((n,)),
        ],
        compiler_params=pltpu.CompilerParams(collective_id=0, has_side_effects=True),
        name="gather_parameters",
    )(*shards)


class Scatter:
    def __init__(self, links, i, grads, out, held, from_far, from_near, from_line, sems):
        self.l, self.i, self.grads, self.out = links, i, grads, out
        self.held, self.from_far, self.from_near, self.from_line = held, from_far, from_near, from_line
        self.load_sem, self.send_sem, self.recv_sem = sems
        self.sent = []

    def load(self, colour, side, z):
        l = self.l
        near, far = l.sides(colour)
        return pltpu.make_async_copy(
            self.grads.at[l.at((near,) if side else (), z), colour],
            self.held.at[colour, side, z],
            self.load_sem.at[self.i, colour, side * l.Z + z],
        )

    def remote(self, colour, kind, z, target):
        l, Z = self.l, self.l.Z
        near, far = l.sides(colour)
        if kind in ("far0", "far1"):
            side = int(kind[3])
            src = self.grads.at[l.at((near, far) if side else (far,), z), colour]
            dst = self.from_far.at[colour, side, z]
            send, recv = side * Z, side * Z
        elif kind == "near":
            src, dst = self.held.at[colour, 1, z], self.from_near.at[colour, z]
            send, recv = 2 * Z, 2 * Z
        else:
            way = int(kind[4])
            src, dst = self.held.at[colour, 0, z], self.from_line.at[colour, way, z]
            send, recv = 3 * Z, (3 + way) * Z
        return pltpu.make_async_remote_copy(
            src_ref=src,
            dst_ref=dst,
            send_sem=self.send_sem.at[self.i, colour, send + z],
            recv_sem=self.recv_sem.at[self.i, colour, recv + z],
            device_id=target,
            device_id_type=MESH,
        )

    def arrive(self, colour, kind, z):
        self.remote(colour, kind, z, {"zz": self.l.z}).wait_recv()

    def order(self):
        return offsets(self.l.Z)[::-1] + [0]

    def guard(self, step, run):
        if step:
            pl.when(self.l.has(step))(run)
        else:
            run()

    def start(self):
        l = self.l
        for side in (1, 0):
            for step in self.order():
                for colour in (0, 1):
                    near, far = l.sides(colour)
                    z = l.z + step
                    what = (colour, f"far{side}", z, l.peer(far))

                    def run():
                        self.remote(*what).start()
                        self.load(colour, side, z).start()

                    self.guard(step, run)
                    self.sent.append((l.has(step) if step else None, what))

    def total(self, target, parts):
        rows, cols = target.shape
        pieces = 5 if cols % 640 == 0 else 1
        wide_cols = cols // pieces

        def one(p, carry):
            window = pl.ds(pl.multiple_of(p * wide_cols, 128), wide_cols)
            value = parts[0][:, window].astype(wide)
            for part in parts[1:]:
                value = value + part[:, window].astype(wide)
            target[:, window] = value.astype(target.dtype)
            return carry

        lax.fori_loop(0, pieces, one, 0)

    def near(self, step):
        l = self.l
        for colour in (0, 1):
            near, far = l.sides(colour)
            z = l.z + step
            what = (colour, "near", z, l.peer(near))

            def run():
                self.load(colour, 1, z).wait()
                self.arrive(colour, "far1", z)
                mine = self.held.at[colour, 1, z]
                self.total(mine, [mine, self.from_far.at[colour, 1, z]])
                self.remote(*what).start()

            self.guard(step, run)
            self.sent.append((l.has(step) if step else None, what))

    def parts(self, colour, z):
        self.load(colour, 0, z).wait()
        self.arrive(colour, "far0", z)
        self.arrive(colour, "near", z)
        return [
            self.held.at[colour, 0, z],
            self.from_far.at[colour, 0, z],
            self.from_near.at[colour, z],
        ]

    def line(self, step):
        l = self.l
        toward, way = (1, 0) if step > 0 else (-1, 1)
        behind = l.has(-toward)
        for colour in (0, 1):
            z = l.z + step
            what = (colour, f"line{way}", z, {"zz": l.z + toward})

            def run():
                parts = self.parts(colour, z)
                mine = self.held.at[colour, 0, z]

                @pl.when(behind)
                def _():
                    self.arrive(colour, f"line{way}", z)
                    self.total(mine, parts + [self.from_line.at[colour, way, z]])

                @pl.when(jnp.logical_not(behind))
                def _():
                    self.total(mine, parts)

                self.remote(*what).start()

            self.guard(step, run)
            self.sent.append((l.has(step), what))

    def finish(self):
        l, Z = self.l, self.l.Z
        for colour in (0, 1):
            z = l.z
            parts = self.parts(colour, z)
            left, right = self.from_line.at[colour, 0, z], self.from_line.at[colour, 1, z]
            target = self.out.at[colour]

            @pl.when(l.has(-1))
            def _():
                self.arrive(colour, "line0", z)

            @pl.when(l.has(1))
            def _():
                self.arrive(colour, "line1", z)

            @pl.when(jnp.logical_and(l.has(-1), l.has(1)))
            def _():
                self.total(target, parts + [left, right])

            @pl.when(jnp.logical_not(l.has(-1)))
            def _():
                self.total(target, parts + [right])

            @pl.when(jnp.logical_not(l.has(1)))
            def _():
                self.total(target, parts + [left])

    def drain(self):
        for cond, what in self.sent:

            def wait():
                self.remote(*what).wait_send()

            if cond is None:
                wait()
            else:
                pl.when(cond)(wait)


def scatter_kernel(Z, n, *refs):
    grads, outs = refs[:n], refs[n : 2 * n]
    held, from_far, from_near, from_line = (refs[(2 + j) * n : (3 + j) * n] for j in range(4))
    sems = refs[6 * n :]
    links = Links(Z)
    links.barrier()
    works = [
        Scatter(links, i, grads[i], outs[i], held[i], from_far[i], from_near[i], from_line[i], sems)
        for i in range(n)
    ]
    order = works[0].order()
    works[0].start()
    for i, work in enumerate(works):
        for step in order:
            work.near(step)
        if i + 1 < n:
            works[i + 1].start()
        for step in order[:-1]:
            work.line(step)
        if i:
            works[i - 1].finish()
    works[-1].finish()
    for work in works:
        work.drain()


def scatter_blocks(blocks, Z, K):
    if K != 4 * Z or Z > 4:
        return tuple(
            lax.psum_scatter(b, CHIPS, scatter_dimension=0, tiled=False).astype(wide)
            for b in blocks
        )
    n = len(blocks)

    def buffers(*lead):
        return [pltpu.VMEM((2,) + lead + b.shape[2:], low) for b in blocks]

    return pl.pallas_call(
        functools.partial(scatter_kernel, Z, n),
        out_shape=tuple(jax.ShapeDtypeStruct(b.shape[1:], wide) for b in blocks),
        in_specs=[pl.BlockSpec(memory_space=pl.ANY)] * n,
        out_specs=tuple([pl.BlockSpec(memory_space=pltpu.VMEM)] * n),
        scratch_shapes=buffers(2, Z)
        + buffers(2, Z)
        + buffers(Z)
        + buffers(2, Z)
        + [
            pltpu.SemaphoreType.DMA((n, 2, 2 * Z)),
            pltpu.SemaphoreType.DMA((n, 2, 4 * Z)),
            pltpu.SemaphoreType.DMA((n, 2, 5 * Z)),
        ],
        compiler_params=pltpu.CompilerParams(
            collective_id=1, has_side_effects=True, vmem_limit_bytes=60 * 1024 * 1024
        ),
        name="scatter_gradients",
    )(*blocks)


def row_stats(values):
    centre = jnp.mean(values, axis=-1, keepdims=True)
    centred = values - centre
    inverse = lax.rsqrt(jnp.mean(centred * centred, axis=-1, keepdims=True) + epsilon)
    return centred * inverse, inverse


def norm_pull(grad, gain, xhat, inverse):
    e = grad * gain
    return inverse * (
        e
        - jnp.mean(e, axis=-1, keepdims=True)
        - xhat * jnp.mean(e * xhat, axis=-1, keepdims=True)
    )


def gelu_parts(u):
    phi_sum = 0.5 * (1.0 + lax.erf(u * math.sqrt(0.5)))
    density = jnp.exp(-0.5 * u * u) * (1.0 / math.sqrt(2.0 * math.pi))
    return u * phi_sum, phi_sum + u * density


def body(
    n_chip_rows,
    Z,
    frames,
    clip_ids,
    query_weight,
    key_weight,
    value_weight,
    output_weight,
    inner_weight,
    outer_weight,
    query_bias,
    value_bias,
    output_bias,
    inner_bias,
    outer_bias,
    first_gain,
    first_shift,
    second_gain,
    second_shift,
    out_cotangent,
):
    K = n_chip_rows * Z
    R, D = frames.shape[2], frames.shape[3]
    FF = inner_weight.shape[1]
    r = query_weight.shape[0]
    f = outer_weight.shape[0]
    hw = D // 2
    heads = H // 2
    half = Z // 2
    core = lax.axis_index("core")
    first_core = core == 0
    zz = lax.axis_index("zz")
    micro = zz // half
    first_half = micro == 0
    place = zz % half

    def swap_core(v):
        return lax.ppermute(v, "core", [(0, 1), (1, 0)])

    def swap_half(v):
        return lax.ppermute(v, "zz", [(z, (z + half) % Z) for z in range(Z)])

    def by_core(own, other, axis):
        return jnp.where(
            first_core,
            jnp.concatenate([own, other], axis),
            jnp.concatenate([other, own], axis),
        )

    def pick(v, index, axis):
        return lax.dynamic_index_in_dim(v, index, axis, keepdims=False)

    def take_rows(v):
        v = v[:, 0]
        own, away = pick(v, micro, 0), pick(v, 1 - micro, 0)
        got = swap_half(away)
        pair = jnp.where(first_half, jnp.stack([own, got]), jnp.stack([got, own]))
        both = by_core(pair[:, None], swap_core(pair)[:, None], 1)
        return both.reshape(4 * R, D)

    qkv = jnp.stack([query_weight, key_weight, value_weight], 1).reshape(r, 3, 2, hw)
    inner_split = inner_weight.reshape(r, K, 2, f)
    vectors = (
        query_bias, value_bias, output_bias, outer_bias,
        first_gain, first_shift, second_gain, second_shift, inner_bias,
    )
    small = jnp.concatenate(vectors)
    n_small = small.shape[0]

    def column_half(which):
        return jnp.concatenate(
            [
                pick(qkv, which, 2).reshape(r, 3 * hw),
                pick(inner_split, which, 2).reshape(r, FF // 2),
            ],
            1,
        )

    mine = column_half(core)
    theirs = swap_core(column_half(1 - core))
    both = by_core(mine[None], theirs[None], 0)
    small_both = by_core(small[None], swap_core(small)[None], 0)
    small_pad = -(-n_small // 1024) * 1024
    small_both = jnp.pad(small_both, ((0, 0), (0, small_pad - n_small)))
    shards = (
        small_both.reshape(2, small_pad // 128, 128),
        both[:, :, : 3 * hw],
        output_weight.reshape(r, 2, hw).transpose(1, 0, 2),
        both[:, :, 3 * hw :],
        outer_weight.reshape(2, f // 2, D),
    )
    small_all, qkv_all, out_all, inner_all, outer_all = gather_blocks(shards, Z, K)
    x_rows = take_rows(frames)
    cot = take_rows(out_cotangent)

    w_qkv = qkv_all.reshape(D, 3 * hw)
    w_inner = inner_all.reshape(D, FF // 2)
    w_outer = outer_all.reshape(FF // 2, D)
    out_own = out_all.transpose(0, 2, 1, 3).reshape(K, 1, r, D)
    w_out = by_core(out_own, swap_core(out_own), 1).reshape(D, D)
    small_all = small_all.reshape(K, 2, small_pad)[:, :, :n_small].astype(wide)
    names = ("qb", "vb", "ob", "ub", "g1", "s1", "g2", "s2")
    vec = {n: small_all[:, :, i * r : (i + 1) * r].reshape(D) for i, n in enumerate(names)}
    ib_half = pick(small_all[:, :, 8 * r :], core, 1).reshape(FF // 2)

    def own_columns(v):
        return lax.dynamic_slice_in_dim(v, core * hw, hw, v.ndim - 1)

    ids = pick(clip_ids[:, 0], micro, 0).reshape(2, half, 2 * R)
    ids_q = pick(ids, place, 1).reshape(4 * R)
    order = (place - jnp.arange(half)) % half
    ids_k = jnp.take(ids, order, axis=1).transpose(1, 0, 2).reshape(half, 4 * R)
    tag = jnp.arange(TAGS, dtype=jnp.int32)[:, None]
    tags_q = jnp.where(ids_q[None, :] == tag, 0.0, masked_score).astype(low)
    tags_k = (ids_k[:, None, :] == tag[None]).astype(low)

    xf = x_rows.astype(wide)
    xhat, inverse = row_stats(xf)
    normed = (xhat * vec["g1"] + vec["s1"]).astype(low)
    bias_qkv = jnp.concatenate(
        [own_columns(vec["qb"]), jnp.zeros((hw,), wide), own_columns(vec["vb"])]
    )
    qkv_t = (dims(w_qkv, normed, 0, 1) + bias_qkv[:, None]).astype(low)
    q_t, kv_own = qkv_t[:hw], qkv_t[hw:]
    kv_parts = [kv_own]
    for o in range(1, half):
        kv_parts.append(
            lax.ppermute(
                kv_own, "zz", [(z, (z // half) * half + (z + o) % half) for z in range(Z)]
            )
        )
    kv = jnp.stack(kv_parts)
    tile = 256
    mixed_t, logs = attend_forward(q_t, tags_q, kv, tags_k, heads, tile)
    mixed_full = by_core(mixed_t, swap_core(mixed_t), 0)
    middle = xf + (dims(mixed_full, w_out, 0, 0) + vec["ob"])
    xhat_two, inverse_two = row_stats(middle)
    normed_two = (xhat_two * vec["g2"] + vec["s2"]).astype(low)
    inner = dims(normed_two, w_inner, 1, 0) + ib_half
    active, slope = gelu_parts(inner)
    active = active.astype(low)
    out_part = dims(active, w_outer, 1, 0)

    def split_rows(v):
        return v.reshape(2, 2, R, D)

    def reduce_rows(v):
        v = split_rows(v)
        return pick(v, core, 1) + swap_core(pick(v, 1 - core, 1).astype(low)).astype(wide)

    def home_rows(v):
        stay = pick(v, micro, 0)
        got = swap_half(pick(v, 1 - micro, 0))
        return jnp.where(first_half, jnp.stack([stay, got]), jnp.stack([got, stay]))[:, None]

    own_middle = pick(split_rows(middle), core, 1)
    layer_rows = (own_middle + (reduce_rows(out_part) + vec["ub"])).astype(low)
    layer_out = home_rows(layer_rows)

    grad_active = dims(cot, w_outer, 1, 1)
    inner_grad = (grad_active * slope).astype(low)
    part_two = dims(inner_grad, w_inner, 1, 1)
    grad_two = part_two + swap_core(part_two.astype(low)).astype(wide)
    middle_grad = cot.astype(wide) + norm_pull(grad_two, vec["g2"], xhat_two, inverse_two)
    branch_grad = middle_grad.astype(low)
    w_out_heads = lax.dynamic_slice_in_dim(w_out, core * hw, hw, 0)
    mixed_grad = dims(w_out_heads, branch_grad, 1, 1).astype(low)
    dq_t, own_kv, far_kv = attend_backward(
        q_t, tags_q, kv, tags_k, mixed_t, logs, mixed_grad, heads, tile
    )
    dkv = own_kv.reshape(2 * hw, 4 * R)
    for o in range(1, half):
        back = lax.ppermute(
            far_kv[o - 1], "zz", [(z, (z // half) * half + (z - o) % half) for z in range(Z)]
        )
        dkv = dkv + back.reshape(2 * hw, 4 * R).astype(wide)
    dqkv_t = jnp.concatenate([dq_t, dkv.astype(low)], 0)
    grad_one = reduce_rows(dims(dqkv_t, w_qkv, 0, 1))
    own_xhat = pick(split_rows(xhat), core, 1)
    own_inverse = pick(inverse.reshape(2, 2, R, 1), core, 1)
    frame_rows = pick(split_rows(middle_grad), core, 1) + norm_pull(
        grad_one, vec["g1"], own_xhat, own_inverse
    )
    sent = swap_half(pick(frame_rows, 1 - micro, 0).astype(low)).astype(wide)
    stay = pick(frame_rows, micro, 0)
    frames_grad = jnp.where(first_half, jnp.stack([stay, sent]), jnp.stack([sent, stay]))[:, None]

    g_qkv = dims(normed, dqkv_t, 0, 1).astype(low)
    g_out = dims(mixed_full, own_columns(branch_grad), 1, 0).astype(low)
    g_inner = dims(normed_two, inner_grad, 0, 0).astype(low)
    g_outer = dims(active, cot, 0, 0).astype(low)

    def zero_rest(v):
        return by_core(v, jnp.zeros_like(v), 0)

    bias_sums = jnp.sum(dqkv_t.astype(wide), axis=1)
    halves = 0.5
    col = {
        "qb": zero_rest(bias_sums[:hw]),
        "vb": zero_rest(bias_sums[2 * hw :]),
        "ob": halves * jnp.sum(branch_grad.astype(wide), 0),
        "ub": halves * jnp.sum(cot.astype(wide), 0),
        "g1": jnp.sum(grad_one * own_xhat, (0, 1)),
        "s1": jnp.sum(grad_one, (0, 1)),
        "g2": halves * jnp.sum(grad_two * xhat_two, 0),
        "s2": halves * jnp.sum(grad_two, 0),
    }
    ib_sum = jnp.sum(inner_grad.astype(wide), 0).reshape(K, 1, f)
    small_grad = jnp.concatenate(
        [col[n].reshape(K, 2, r) for n in names]
        + [by_core(ib_sum, jnp.zeros_like(ib_sum), 1)],
        2,
    )
    small_grad = jnp.pad(small_grad, ((0, 0), (0, 0), (0, small_pad - n_small)))
    small_grad = small_grad.reshape(K, 2, small_pad // 128, 128).astype(low)
    g_outer, g_inner, g_out, g_qkv, g_small = scatter_blocks(
        (
            g_outer.reshape(K, 2, f // 2, D),
            g_inner.reshape(K, 2, r, FF // 2),
            g_out.reshape(K, 2, r, hw),
            g_qkv.reshape(K, 2, r, 3 * hw),
            small_grad,
        ),
        Z,
        K,
    )
    wide_rows = jnp.concatenate([g_qkv, g_out, g_inner], 2)
    mine = pick(wide_rows, core, 0)
    theirs = swap_core(pick(wide_rows, 1 - core, 0))

    def whole(a, b, parts):
        a, b = a.reshape(r, parts, 1, -1), b.reshape(r, parts, 1, -1)
        return by_core(a, b, 2).reshape(r, -1)

    outs = []
    for i in range(4):
        outs.append(whole(mine[:, i * hw : (i + 1) * hw], theirs[:, i * hw : (i + 1) * hw], 1))
    outs.append(whole(mine[:, 4 * hw :], theirs[:, 4 * hw :], K))
    outs.append(g_outer.reshape(f, D))
    g_small = g_small.reshape(2, small_pad)[:, :n_small]
    g_small = pick(g_small, core, 0) + swap_core(pick(g_small, 1 - core, 0))
    sv = {n: g_small[i * r : (i + 1) * r] for i, n in enumerate(names)}
    return (layer_out, frames_grad) + tuple(outs) + (
        sv["qb"], sv["vb"], sv["ob"], g_small[8 * r :], sv["ub"],
        sv["g1"], sv["s1"], sv["g2"], sv["s2"],
    )


def solution(mesh):
    C, S = mesh.shape["clip"], mesh.shape["seq"]
    fine = Mesh(mesh.devices.reshape(2, C // 2, S // 2, 2), ("cy", "cx", "zz", "core"))
    clip, seq = ("cy", "cx"), ("zz", "core")
    every = clip + seq
    rows, mat, vec = P(None, clip, seq, None), P(every, None), P(every)
    in_specs = (rows, P(None, clip, None)) + (mat,) * 6 + (vec,) * 9 + (rows,)
    out_specs = (rows, rows) + (mat,) * 6 + (vec,) * 9
    return jax.shard_map(
        functools.partial(body, C, S // 2),
        mesh=fine,
        in_specs=in_specs,
        out_specs=out_specs,
        check_vma=False,
    )
```

```python
import functools
import math
from typing import Any, NamedTuple

import jax
import jax.numpy as jnp
from jax import lax
from jax.experimental import pallas as pl
from jax.experimental.pallas import tpu as pltpu
from jax.sharding import Mesh
from jax.sharding import PartitionSpec as P

H = 16
HD = 80
TAGS = 16
epsilon = 1e-05
masked_score = -1e30
low = jnp.bfloat16
wide = jnp.float32


def dims(left_side, right_side, left_dim, right_dim):
    return lax.dot_general(
        left_side,
        right_side,
        (((left_dim,), (right_dim,)), ((), ())),
        preferred_element_type=wide,
    )


def attend_forward_kernel(blocks, q_ref, qa_ref, k_ref, v_ref, ka_ref, out_ref, log_ref):
    factor = HD ** (-0.5) * math.log2(math.e)
    query = jnp.concatenate([q_ref[...], qa_ref[...]], axis=0)
    scores = []
    for b in range(blocks):
        key = jnp.concatenate([k_ref[b], ka_ref[b]], axis=0)
        scores.append(dims(key, query, 0, 0))
    top = functools.reduce(jnp.maximum, [jnp.max(s, axis=0, keepdims=True) for s in scores])
    top = top * factor
    total = jnp.zeros_like(top)
    mixed = jnp.zeros((HD, query.shape[1]), wide)
    for b in range(blocks):
        part = jnp.exp2(scores[b] * factor - top)
        total = total + jnp.sum(part, axis=0, keepdims=True)
        mixed = mixed + dims(v_ref[b], part.astype(low), 1, 0)
    out_ref[...] = (mixed / total).astype(low)
    log_ref[0] = top + jnp.log2(total)


def attend_forward(q_t, tags_q, kv, tags_k, heads, tile):
    blocks, _, width = kv.shape
    rows = q_t.shape[1]
    grid = (heads, rows // tile)
    return pl.pallas_call(
        functools.partial(attend_forward_kernel, blocks),
        grid=grid,
        out_shape=(
            jax.ShapeDtypeStruct((heads * HD, rows), low),
            jax.ShapeDtypeStruct((heads, 1, rows), wide),
        ),
        in_specs=[
            pl.BlockSpec((HD, tile), lambda h, t: (h, t)),
            pl.BlockSpec((TAGS, tile), lambda h, t: (0, t)),
            pl.BlockSpec((blocks, HD, width), lambda h, t: (0, h, 0)),
            pl.BlockSpec((blocks, HD, width), lambda h, t: (0, heads + h, 0)),
            pl.BlockSpec((blocks, TAGS, width), lambda h, t: (0, 0, 0)),
        ],
        out_specs=(
            pl.BlockSpec((HD, tile), lambda h, t: (h, t)),
            pl.BlockSpec((1, 1, tile), lambda h, t: (h, 0, t)),
        ),
        cost_estimate=pl.CostEstimate(
            flops=4 * heads * rows * blocks * width * HD,
            bytes_accessed=2 * kv.size,
            transcendentals=heads * rows * blocks * width,
        ),
    )(q_t, tags_q, kv, kv, tags_k)


def attend_backward_kernel(
    blocks, q_ref, qa_ref, k_ref, v_ref, ka_ref, o_ref, log_ref, g_ref, dq_ref, own_ref, far_ref, acc_k, acc_v
):
    factor = HD ** (-0.5) * math.log2(math.e)
    step, steps = pl.program_id(1), pl.num_programs(1)
    head_query = q_ref[...]
    grad = g_ref[...]
    query = jnp.concatenate([head_query, qa_ref[...]], axis=0)
    delta = jnp.sum(grad.astype(wide) * o_ref[...].astype(wide), axis=0, keepdims=True)
    logs = log_ref[0]
    query_rows = head_query.T
    grad_rows = grad.T
    dq = jnp.zeros(head_query.shape, wide)

    @pl.when(step == 0)
    def _():
        acc_k[...] = jnp.zeros_like(acc_k)
        acc_v[...] = jnp.zeros_like(acc_v)

    for b in range(blocks):
        key = jnp.concatenate([k_ref[b], ka_ref[b]], axis=0)
        probs = jnp.exp2(dims(key, query, 0, 0) * factor - logs)
        grad_probs = dims(v_ref[b], grad, 0, 0)
        score_grad = (probs * (grad_probs - delta)).astype(low)
        acc_v[b] += dims(probs.astype(low), grad_rows, 1, 0)
        acc_k[b] += dims(score_grad, query_rows, 1, 0)
        dq = dq + dims(k_ref[b], score_grad, 1, 0)
    dq_ref[...] = (dq * HD ** (-0.5)).astype(low)

    @pl.when(step == steps - 1)
    def _():
        for b in range(blocks):
            key_part = acc_k[b].T * HD ** (-0.5)
            value_part = acc_v[b].T
            if b == 0:
                own_ref[0] = key_part
                own_ref[1] = value_part
            else:
                far_ref[b - 1, 0] = key_part.astype(low)
                far_ref[b - 1, 1] = value_part.astype(low)


def attend_backward(q_t, tags_q, kv, tags_k, mixed_t, logs, grad_t, heads, tile):
    blocks, _, width = kv.shape
    rows = q_t.shape[1]
    grid = (heads, rows // tile)
    per_query = pl.BlockSpec((HD, tile), lambda h, t: (h, t))
    return pl.pallas_call(
        functools.partial(attend_backward_kernel, blocks),
        grid=grid,
        out_shape=(
            jax.ShapeDtypeStruct((heads * HD, rows), low),
            jax.ShapeDtypeStruct((2, heads * HD, width), wide),
            jax.ShapeDtypeStruct((blocks - 1, 2, heads * HD, width), low),
        ),
        in_specs=[
            per_query,
            pl.BlockSpec((TAGS, tile), lambda h, t: (0, t)),
            pl.BlockSpec((blocks, HD, width), lambda h, t: (0, h, 0)),
            pl.BlockSpec((blocks, HD, width), lambda h, t: (0, heads + h, 0)),
            pl.BlockSpec((blocks, TAGS, width), lambda h, t: (0, 0, 0)),
            per_query,
            pl.BlockSpec((1, 1, tile), lambda h, t: (h, 0, t)),
            per_query,
        ],
        out_specs=(
            per_query,
            pl.BlockSpec((2, HD, width), lambda h, t: (0, h, 0)),
            pl.BlockSpec((blocks - 1, 2, HD, width), lambda h, t: (0, 0, h, 0)),
        ),
        scratch_shapes=[
            pltpu.VMEM((blocks, width, HD), wide),
            pltpu.VMEM((blocks, width, HD), wide),
        ],
        cost_estimate=pl.CostEstimate(
            flops=10 * heads * rows * blocks * width * HD,
            bytes_accessed=4 * kv.size,
            transcendentals=heads * rows * blocks * width,
        ),
    )(q_t, tags_q, kv, kv, tags_k, mixed_t, logs, grad_t)


def row_stats(values):
    centre = jnp.mean(values, axis=-1, keepdims=True)
    centred = values - centre
    inverse = lax.rsqrt(jnp.mean(centred * centred, axis=-1, keepdims=True) + epsilon)
    return centred * inverse, inverse


def norm_pull(grad, gain, xhat, inverse):
    e = grad * gain
    return inverse * (
        e
        - jnp.mean(e, axis=-1, keepdims=True)
        - xhat * jnp.mean(e * xhat, axis=-1, keepdims=True)
    )


def gelu_parts(u):
    phi_sum = 0.5 * (1.0 + lax.erf(u * math.sqrt(0.5)))
    density = jnp.exp(-0.5 * u * u) * (1.0 / math.sqrt(2.0 * math.pi))
    return u * phi_sum, phi_sum + u * density


CHIPS = ("cy", "cx", "zz")
MESH = pl.DeviceIdType.MESH
BIG = 62 * 1024 * 1024


def offsets(Z):
    steps = []
    for d in range(1, Z):
        steps += [-d, d]
    return steps


def full(n, space=pltpu.VMEM):
    return [pl.BlockSpec(memory_space=space)] * n


class Links:
    def __init__(self, Z):
        self.Z = Z
        self.y, self.x, self.z = (lax.axis_index(a) for a in CHIPS)
        self.core = lax.axis_index("core")
        self.half = lax.div(self.z, Z // 2)
        self.crossed = lax.rem(self.y + self.core, 2)

    def sides(self, colour):
        return (("cx", "cy"), ("cy", "cx"))[colour]

    def coords(self, flips, z):
        y = 1 - self.y if "cy" in flips else self.y
        x = 1 - self.x if "cx" in flips else self.x
        return y, x, z

    def index(self, place):
        y, x, z = place
        return (y * 2 + x) * self.Z + z

    def at(self, flips, z):
        return self.index(self.coords(flips, z))

    def target(self, to):
        if to == "cy":
            return {"cy": 1 - self.y}
        if to == "cx":
            return {"cx": 1 - self.x}
        if to == "core":
            return {"core": 1 - self.core}
        if to == "pair":
            return {"zz": self.z + 1 - 2 * lax.rem(self.z, 2)}
        if to == "swap":
            return {"zz": self.z + (self.Z // 2) * (1 - 2 * self.half)}
        if to == "diagonal":
            return {"cy": self.core, "core": self.y}
        return {"zz": self.z + to}

    def has(self, step):
        there = self.z + step
        return jnp.logical_and(there >= 0, there < self.Z)

    def when(self, steps, run):
        steps = [s for s in steps if s]
        if steps:
            pl.when(functools.reduce(jnp.logical_and, [self.has(s) for s in steps]))(run)
        else:
            run()

    def barrier(self, *more):
        sem = pltpu.get_barrier_semaphore()
        for to in ("cy", "cx") + tuple(m for m in more if m != "diagonal"):
            pl.semaphore_signal(sem, inc=1, device_id=self.target(to), device_id_type=MESH)
        for step in (-1, 1):

            @pl.when(self.has(step))
            def _():
                pl.semaphore_signal(
                    sem, inc=1, device_id=self.target(step), device_id_type=MESH
                )

        count = 2 + len([m for m in more if m != "diagonal"])
        count = count + jnp.minimum(self.z, 1) + jnp.minimum(self.Z - 1 - self.z, 1)
        if "diagonal" in more:

            @pl.when(self.crossed == 1)
            def _():
                pl.semaphore_signal(
                    sem, inc=1, device_id=self.target("diagonal"), device_id_type=MESH
                )

            count = count + self.crossed
        pl.semaphore_wait(sem, count)


def remote(src, dst, send, recv, to):
    return pltpu.make_async_remote_copy(
        src_ref=src, dst_ref=dst, send_sem=send, recv_sem=recv, device_id=to, device_id_type=MESH
    )


class Gather:
    def __init__(self, links, block, sems):
        self.l, self.block = links, block
        self.send_sem, self.recv_sem = sems
        self.sent = []

    def copy(self, i, colour, flips, step, base, to):
        place = self.l.coords(flips, self.l.z + step)
        block = self.block(i, colour, place)
        return remote(
            block,
            block,
            self.send_sem.at[i, colour, base + self.l.z + step],
            self.recv_sem.at[i, colour, self.l.index(place)],
            self.l.target(to),
        )

    def send(self, steps, *what):
        self.l.when(steps, lambda: self.copy(*what).start())
        self.sent.append((steps, what))

    def arrive(self, i, colour, flips, step):
        self.l.when([step], lambda: self.copy(i, colour, flips, step, 0, "cx").wait_recv())

    def own(self, i):
        for colour in (0, 1):
            for step, base in ((1, 0), (-1, self.l.Z)):
                self.send([step], i, colour, (), 0, base, step)

    def along(self, i, distance):
        for step in (-distance, distance):
            onward = 1 if step < 0 else -1
            for colour in (0, 1):
                self.arrive(i, colour, (), step)
                self.send([step, onward], i, colour, (), step, 0 if step < 0 else self.l.Z, onward)

    def aside(self, i, distance):
        for step in (-distance, distance) if distance else (0,):
            for colour in (0, 1):
                near, far = self.l.sides(colour)
                self.send([step], i, colour, (), step, 2 * self.l.Z, near)
                self.send([step], i, colour, (), step, 3 * self.l.Z, far)

    def across(self, i, distance):
        for step in (-distance, distance) if distance else (0,):
            for colour in (0, 1):
                near, far = self.l.sides(colour)
                self.arrive(i, colour, (near,), step)
                self.send([step], i, colour, (near,), step, 4 * self.l.Z, far)

    def last(self, i):
        for colour in (0, 1):
            near, far = self.l.sides(colour)
            for step in [0] + offsets(self.l.Z):
                self.arrive(i, colour, (far,), step)
                self.arrive(i, colour, (far, near), step)

    def drain(self):
        for steps, what in self.sent:
            self.l.when(steps, lambda: self.copy(*what).wait_send())

    @staticmethod
    def semaphores(n, Z):
        return [
            pltpu.SemaphoreType.DMA((n, 2, 5 * Z)),
            pltpu.SemaphoreType.DMA((n, 2, 4 * Z)),
        ]


GROUP_HEADS = 2
class ForwardOuts(NamedTuple):
    vectors: Any
    w_qkv: Any
    w_out: Any
    w_inner: Any
    w_outer: Any
    cot_rows: Any
    x_rows: Any
    normed: Any
    qkv: Any
    far: Any
    mixed: Any
    logs: Any
    middle: Any
    normed_two: Any
    active: Any
    slope: Any


class ForwardScratch(NamedTuple):
    small_all: Any
    hidden_bias: Any
    x: Any
    norm_v: Any
    qkv_v: Any
    far_v: Any
    mix_v: Any
    wq_v: Any
    wo_v: Any
    wi_v: Any
    n2_v: Any
    mid_v: Any
    act_v: Any
    slo_v: Any
    cot_own: Any
    local: Any
    core_send: Any
    core_recv: Any
    row_sem: Any
    kv_send: Any
    kv_recv: Any
    mix_send: Any
    mix_recv: Any
    wo_sem: Any
    out_sem: Any
    load_sem: Any
    gather_send: Any
    gather_recv: Any


def norm_rows(values, gain, shift):
    xhat, _ = row_stats(values)
    return (xhat * gain + shift).astype(low)


def forward_kernel(Z, heads, tile, *refs):
    (frames, cot, wq, wk, wv, wo, wi, w2, small, tags_q, tags_k) = refs[:11]
    n_outs = len(ForwardOuts._fields)
    o = ForwardOuts(*refs[11 : 11 + n_outs])
    s = ForwardScratch(*refs[11 + n_outs :])
    l = Links(Z)
    core, K = l.core, 4 * Z
    here = l.at((), l.z)
    r, D = wq.shape
    hw = D // 2
    f = w2.shape[0]
    R = frames.shape[2]
    rows = 4 * R
    width = heads * HD
    tiles = rows // tile
    groups = heads // GROUP_HEADS
    span = GROUP_HEADS * HD
    factor = HD ** (-0.5) * math.log2(math.e)
    vectors = o.vectors

    def natural(place):
        y, x, z = place
        return (x * Z + z) * 2 + y

    def block(i, colour, place):
        k = l.index(place)
        rows80 = pl.ds(pl.multiple_of(k * 2 * r, 16), 2 * r)
        if i == 0:
            return s.small_all.at[k, colour]
        if i == 1:
            return o.w_qkv.at[rows80, pl.ds(colour * hw, hw)]
        if i == 2:
            if colour == 0:
                return o.w_qkv.at[rows80, pl.ds(2 * hw, hw)]
            return o.w_out.at[core, rows80, :]
        if i < 5:
            return o.w_inner.at[rows80, pl.ds(((i - 3) * 2 + colour) * hw, hw)]
        at = natural(place) * f + ((i - 5) * 2 + colour) * (f // 4)
        return o.w_outer.at[pl.ds(pl.multiple_of(at, 8), f // 4), :]

    gather = Gather(l, block, (s.gather_send, s.gather_recv))

    def my_rows():
        return pl.ds(pl.multiple_of(here * 2 * r + core * r, 8), r)

    sources = ((wq, hw), (wk, hw), (wv, hw), (wo, hw), (wi, 2 * D))

    def place_of(m, of_core):
        if m == 3:
            return o.w_out.at[of_core, my_rows(), :]
        if m == 4:
            return o.w_inner.at[my_rows(), :]
        return o.w_qkv.at[my_rows(), pl.ds(m * hw, hw)]

    def keep(m):
        if m == 5:
            return pltpu.make_async_copy(small, s.small_all.at[here, core], s.local.at[m])
        src, cols = sources[m]
        window = pl.ds(pl.multiple_of(core * cols, 128), cols)
        return pltpu.make_async_copy(src.at[:, window], place_of(m, core), s.local.at[m])

    def give(m):
        sems = s.core_send.at[m], s.core_recv.at[m]
        if m == 5:
            return remote(small, s.small_all.at[here, core], *sems, l.target("core"))
        src, cols = sources[m]
        window = pl.ds(pl.multiple_of((1 - core) * cols, 128), cols)
        return remote(src.at[:, window], place_of(m, 1 - core), *sems, l.target("core"))

    outer_rows = pl.ds(pl.multiple_of(((l.x * Z + l.z) * 2 + core) * f, 16), f)

    def outer_keep():
        return pltpu.make_async_copy(w2, o.w_outer.at[outer_rows, :], s.local.at[6])

    def outer_give():
        return remote(
            w2,
            o.w_outer.at[outer_rows, :],
            s.core_send.at[6],
            s.core_recv.at[6],
            l.target("diagonal"),
        )

    def begin(m):
        keep(m).start()
        give(m).start()

    def ready(m):
        keep(m).wait()
        give(m).wait_recv()

    def row_copies(source, target, base, own_slot, near_slot):
        m = l.half
        mine, theirs = m * 2 + core, (1 - m) * 2 + core
        return (
            remote(
                source.at[1 - m, 0], target.at[mine],
                s.row_sem.at[base], s.row_sem.at[base + 1], l.target("swap"),
            ),
            remote(
                source.at[m, 0], target.at[mine],
                s.row_sem.at[base + 2], s.row_sem.at[base + 3], l.target("core"),
            ),
            remote(
                target.at[theirs], target.at[theirs],
                s.row_sem.at[base + 4], s.row_sem.at[base + 5], l.target("core"),
            ),
        )

    frame_copies = lambda: row_copies(frames, s.x, 0, 0, 0)
    cot_copies = lambda: row_copies(cot, o.cot_rows, 6, 0, 0)
    frame_own = lambda: pltpu.make_async_copy(
        frames.at[l.half, 0], s.x.at[l.half * 2 + core], s.local.at[7]
    )
    cot_load = lambda: pltpu.make_async_copy(cot.at[l.half, 0], s.cot_own, s.local.at[8])
    cot_store = lambda: pltpu.make_async_copy(
        s.cot_own, o.cot_rows.at[l.half * 2 + core], s.local.at[8]
    )

    def kv_copy(g, which):
        at = which * width + g * span
        return remote(
            s.qkv_v.at[pl.ds(width + at, span)],
            s.far_v.at[pl.ds(at, span)],
            s.kv_send.at[g, which],
            s.kv_recv.at[g, which],
            l.target("pair"),
        )

    def mix_copy(g, of_core):
        at = pl.ds(pl.multiple_of(of_core * width + g * span, 16), span)
        return remote(
            s.mix_v.at[at],
            s.mix_v.at[at],
            s.mix_send.at[g],
            s.mix_recv.at[g],
            l.target("core"),
        )

    def wo_copy(of_core):
        return remote(
            o.w_out.at[of_core], o.w_out.at[of_core],
            s.wo_sem.at[0], s.wo_sem.at[1], l.target("core"),
        )

    def wide_load(which):
        return pltpu.make_async_copy(
            o.w_qkv.at[:, pl.ds(which * hw, hw)], s.wq_v.at[which], s.load_sem.at[which]
        )

    def wo_load():
        return pltpu.make_async_copy(o.w_out, s.wo_v, s.load_sem.at[3])

    inner_tile = 256

    def wi_load(c):
        cols = pl.ds(pl.multiple_of(c * inner_tile, inner_tile), inner_tile)
        slot = lax.rem(c, 2)
        return pltpu.make_async_copy(
            o.w_inner.at[:, cols], s.wi_v.at[slot], s.load_sem.at[4 + slot]
        )

    stores = (
        (s.x, o.x_rows), (s.norm_v, o.normed), (s.qkv_v, o.qkv), (s.far_v, o.far), (s.mix_v, o.mixed),
        (s.mid_v, o.middle), (s.n2_v, o.normed_two), (s.act_v, o.active), (s.slo_v, o.slope),
    )

    def store(i):
        return pltpu.make_async_copy(*stores[i], s.out_sem.at[i])

    big = rows // 2

    def big_rows(t):
        return pl.ds(pl.multiple_of(t * big, 128), big)

    def x_tile(t):
        return s.x[pl.ds(2 * t, 2)].reshape(big, D).astype(wide)

    def project(t, whiches):
        if 0 in whiches:
            s.norm_v[big_rows(t), :] = norm_rows(x_tile(t), vectors[4:5, :], vectors[5:6, :])
        source = s.norm_v[big_rows(t), :]
        mine = pl.ds(pl.multiple_of(core * hw, 128), hw)
        for which in whiches:
            part = dims(source, s.wq_v[which], 1, 0)
            if which == 0:
                part = part + vectors[0:1, mine]
            if which == 2:
                part = part + vectors[1:2, mine]
            s.qkv_v[pl.ds(which * hw, hw), big_rows(t)] = part.T.astype(low)

    def attend(index):
        head, part = index // tiles, lax.rem(index, tiles)
        row = head * HD
        columns = pl.ds(pl.multiple_of(part * tile, tile), tile)
        qkv, far = s.qkv_v, s.far_v

        def feature(base):
            return pl.ds(pl.multiple_of(base + row, 16), HD)

        query = jnp.concatenate([qkv[feature(0), columns], tags_q[:, columns]], axis=0)
        keys = (qkv[feature(width), :], far[feature(0), :])
        values = (qkv[feature(2 * width), :], far[feature(width), :])
        scores = [
            dims(jnp.concatenate([keys[b], tags_k[b]], axis=0), query, 0, 0) for b in (0, 1)
        ]
        top = jnp.maximum(*[jnp.max(v, axis=0, keepdims=True) for v in scores]) * factor
        total = jnp.zeros_like(top)
        sums = jnp.zeros((HD, tile), wide)
        for b in (0, 1):
            part_values = jnp.exp2(scores[b] * factor - top)
            total = total + jnp.sum(part_values, axis=0, keepdims=True)
            sums = sums + dims(values[b], part_values.astype(low), 1, 0)
        s.mix_v[feature(core * width), columns] = (sums / total).astype(low)
        o.logs[head, :, columns] = top + jnp.log2(total)

    def branch(t):
        parts = [dims(s.mix_v[:, big_rows(t)], s.wo_v[b], 0, 0) for b in (0, 1)]
        middle = x_tile(t) + (jnp.concatenate(parts, axis=1) + vectors[2:3, :])
        s.mid_v[big_rows(t), :] = middle
        s.n2_v[big_rows(t), :] = norm_rows(middle, vectors[6:7, :], vectors[7:8, :])

    column_tiles = 2 * D // inner_tile

    def inner(index):
        c, t = index // 2, lax.rem(index, 2)

        @pl.when(t == 0)
        def _():
            @pl.when(c + 1 < column_tiles)
            def _():
                wi_load(c + 1).start()

            wi_load(c).wait()

        cols = pl.ds(pl.multiple_of(c * inner_tile, inner_tile), inner_tile)
        bias_at = pl.ds(pl.multiple_of(core * 2 * D + c * inner_tile, inner_tile), inner_tile)
        value = dims(s.n2_v[big_rows(t), :], s.wi_v[lax.rem(c, 2)], 1, 0)
        active, slope = gelu_parts(value + s.hidden_bias[:, bias_at])
        s.act_v[big_rows(t), cols] = active.astype(low)
        s.slo_v[big_rows(t), cols] = slope

    def unpack():
        for k in range(K):
            for q in (0, 1):
                d = 2 * k + q
                vectors[:, d * r : (d + 1) * r] = s.small_all[k, q, 0:8, 0:r].astype(wide)
                per = f // r
                for j in range(per):
                    at = d * f + j * r
                    s.hidden_bias[:, at : at + r] = s.small_all[
                        k, q, 8 + j : 9 + j, 0:r
                    ].astype(wide)

    l.barrier("core", "swap", "diagonal")
    begin(5)
    begin(0)
    begin(1)
    swap_f, own_f, relay_f = frame_copies()
    own_f.start()
    frame_own().start()
    for m in (2, 3, 4):
        begin(m)
    pl.when(l.crossed == 1)(lambda: outer_give().start())
    pl.when(l.crossed == 0)(lambda: outer_keep().start())
    cot_load().start()

    plan = {}

    def at(step, *runs):
        plan.setdefault(step, []).extend(runs)

    def own_outer():
        pl.when(l.crossed == 1)(lambda: outer_give().wait_recv())
        pl.when(l.crossed == 0)(lambda: outer_keep().wait())

    along = lambda i, d: functools.partial(gather.along, i, d)
    across = lambda i, d: functools.partial(gather.across, i, d)
    last = lambda i: functools.partial(gather.last, i)

    def rows_arrive():
        swap, mine, pass_on = frame_copies()
        swap.wait_recv()
        pass_on.start()
        mine.wait_recv()
        pass_on.wait_recv()
        frame_own().wait()

    def kv_ready(g):
        for which in (0, 1):
            kv_copy(g, which).wait_recv()

    def cot_start():
        cot_load().wait()
        swap, mine, _ = cot_copies()
        swap.start()
        mine.start()
        cot_store().start()

    def cot_pass():
        swap, _, pass_on = cot_copies()
        swap.wait_recv()
        pass_on.start()

    def after_v():
        wo_copy(1 - core).wait_recv()
        wo_load().start()

    def mix_ready():
        for g in range(groups):
            mix_copy(g, 1 - core).wait_recv()

    def kv_send(which, *gs):
        for g in gs:
            kv_copy(g, which).start()

    def swap_start():
        swap_f.start()

    attends = heads * tiles
    v0, a0 = 2, 4
    b0 = a0 + attends
    i0 = b0 + 2
    end = i0 + 2 * column_tiles
    own = lambda i: functools.partial(gather.own, i)
    aside = lambda i, d: functools.partial(gather.aside, i, d)
    here_now = lambda *ms: (lambda: [ready(m) for m in ms])
    send_kv = lambda which, *gs: functools.partial(kv_send, which, *gs)

    at(0, here_now(5), own(0), aside(0, 0), here_now(0, 1), own(1), aside(1, 0))
    at(0, along(0, 1), aside(0, 1), here_now(2, 3), own(2), along(0, 2), aside(0, 2), along(0, 3), aside(0, 3))
    at(0, aside(2, 0), across(0, 0), across(0, 1), across(0, 2), across(0, 3))
    at(0, along(1, 1), aside(1, 1), swap_start, along(1, 2), aside(1, 2), here_now(4), own(3), across(1, 0))
    at(0, along(2, 1), aside(2, 1), along(1, 3), aside(1, 3), across(1, 1), along(2, 2), aside(2, 2))
    at(0, own(4), across(1, 2), along(2, 3), aside(2, 3), across(1, 3), along(3, 1), last(0), unpack)
    at(0, aside(3, 0), across(2, 0), aside(3, 1), along(3, 2), rows_arrive, lambda: store(0).start())
    at(0, last(1), lambda: wide_load(0).start(), lambda: wide_load(1).start())
    at(0, lambda: wide_load(0).wait(), lambda: wide_load(1).wait())
    at(1, across(2, 1), along(4, 1), aside(3, 2), own_outer, own(5), along(3, 3))
    at(2, send_kv(0, 0, 1), lambda: store(1).start(), across(2, 2), aside(3, 3), across(2, 3), aside(4, 0))
    at(2, along(4, 2), across(3, 0), own(6), send_kv(0, 2, 3), aside(4, 1), across(3, 1), along(4, 3), last(2))
    at(2, lambda: wide_load(2).start(), lambda: wo_copy(core).start(), lambda: wide_load(2).wait())
    at(a0, send_kv(1, 0, 1, 2, 3), lambda: store(2).start(), aside(4, 2))
    at(a0 + 1, across(3, 2), aside(4, 3))
    at(a0 + 3, along(5, 1), across(3, 3))
    at(a0 + 4, cot_start)
    at(a0 + 5, aside(5, 0), across(4, 0), along(5, 2))
    at(a0 + 7, aside(5, 1), across(4, 1))
    at(a0 + 9, along(6, 1), after_v)
    at(a0 + 11, aside(5, 2), across(4, 2))
    at(a0 + 13, along(5, 3), aside(5, 3))
    at(a0 + 15, across(4, 3))
    at(a0 + 17, along(6, 2), aside(6, 0))
    at(a0 + 19, across(5, 0), aside(6, 1))
    at(a0 + 20, across(5, 1))
    at(a0 + 21, along(6, 3), aside(6, 2))
    at(a0 + 22, cot_pass)
    at(a0 + 23, across(5, 2))
    for g in range(groups):
        at(a0 + g * GROUP_HEADS * tiles, functools.partial(kv_ready, g))
        at(a0 + (g + 1) * GROUP_HEADS * tiles, lambda g=g: mix_copy(g, core).start())
    at(b0, aside(6, 3), across(5, 3), lambda: store(3).start())
    at(b0, lambda: wo_load().wait(), mix_ready, lambda: store(4).start())
    at(b0 + 1, across(6, 0))
    at(i0, across(6, 1), lambda: store(5).start(), lambda: store(6).start(), last(3))
    at(i0, lambda: wi_load(0).start())
    at(i0 + 3, across(6, 2))
    at(i0 + 7, across(6, 3))
    at(i0 + 8, last(4))

    def one(step, carry):
        for when in sorted(plan):

            def run():
                for tick in plan[when]:
                    tick()

            pl.when(step == when)(run)
        inside = lambda lo, n: jnp.logical_and(step >= lo, step < lo + n)
        pl.when(step < v0)(lambda: project(step, (0, 1)))
        pl.when(inside(v0, 2))(lambda: project(step - v0, (2,)))
        pl.when(inside(a0, attends))(lambda: attend(step - a0))
        pl.when(inside(b0, 2))(lambda: branch(step - b0))
        pl.when(inside(i0, 2 * column_tiles))(lambda: inner(step - i0))
        return carry

    lax.fori_loop(0, end, one, 0)
    store(7).start()
    store(8).start()
    gather.last(5)
    gather.last(6)
    gather.drain()
    for m in range(6):
        give(m).wait_send()
    pl.when(l.crossed == 1)(lambda: outer_give().wait_send())
    for copies in (frame_copies(), cot_copies()):
        for copy in copies:
            copy.wait_send()
    _, mine, pass_on = cot_copies()
    mine.wait_recv()
    pass_on.wait_recv()
    cot_store().wait()
    wo_copy(core).wait_send()
    for g in range(groups):
        mix_copy(g, core).wait_send()
        for which in (0, 1):
            kv_copy(g, which).wait_send()
    for i in range(len(stores)):
        store(i).wait()


def forward_linked(frames, cot, weights, small, tags_q, tags_k, Z, heads, tile):
    K = 4 * Z
    r, D = weights[0].shape
    FF2 = weights[4].shape[1] // 2
    R = frames.shape[2]
    rows = 4 * R
    hw = D // 2
    groups = heads // GROUP_HEADS
    shape = jax.ShapeDtypeStruct
    outs = ForwardOuts(
        vectors=shape((8, D), wide),
        w_qkv=shape((D, 3 * hw), low),
        w_out=shape((2, D, hw), low),
        w_inner=shape((D, FF2), low),
        w_outer=shape((FF2, D), low),
        cot_rows=shape((4, R, D), low),
        x_rows=shape((4, R, D), low),
        normed=shape((rows, D), low),
        qkv=shape((3 * hw, rows), low),
        far=shape((2 * hw, rows), low),
        mixed=shape((D, rows), low),
        logs=shape((heads, 1, rows), wide),
        middle=shape((rows, D), wide),
        normed_two=shape((rows, D), low),
        active=shape((rows, FF2), low),
        slope=shape((rows, FF2), wide),
    )
    dma = pltpu.SemaphoreType.DMA
    scratch = [
        pltpu.VMEM((K, 2) + small.shape, low),
        pltpu.VMEM((1, 2 * FF2), wide),
        pltpu.VMEM((4, R, D), low),
        pltpu.VMEM((rows, D), low),
        pltpu.VMEM((3 * hw, rows), low),
        pltpu.VMEM((2 * hw, rows), low),
        pltpu.VMEM((D, rows), low),
        pltpu.VMEM((3, D, hw), low),
        pltpu.VMEM((2, D, hw), low),
        pltpu.VMEM((2, D, 256), low),
        pltpu.VMEM((rows, D), low),
        pltpu.VMEM((rows, D), wide),
        pltpu.VMEM((rows, FF2), low),
        pltpu.VMEM((rows, FF2), wide),
        pltpu.VMEM((R, D), low),
        dma((9,)),
        dma((7,)),
        dma((7,)),
        dma((12,)),
        dma((groups, 2)),
        dma((groups, 2)),
        dma((groups,)),
        dma((groups,)),
        dma((2,)),
        dma((9,)),
        dma((6,)),
    ]
    spaces = [pltpu.VMEM if v in (outs.vectors, outs.logs) else pl.ANY for v in outs]
    results = pl.pallas_call(
        functools.partial(forward_kernel, Z, heads, tile),
        out_shape=tuple(outs),
        in_specs=full(2, pl.ANY) + full(9),
        out_specs=tuple(pl.BlockSpec(memory_space=space) for space in spaces),
        scratch_shapes=scratch + Gather.semaphores(7, Z),
        compiler_params=pltpu.CompilerParams(
            collective_id=0, has_side_effects=True, vmem_limit_bytes=BIG
        ),
    )(frames, cot, *weights, small, tags_q, tags_k)
    return ForwardOuts(*results)


class Scatter:
    def __init__(self, links, i, grads, out, buffers, sems, natural=False):
        self.natural = natural
        self.l, self.i, self.grads, self.out = links, i, grads, out
        self.held, self.from_far, self.from_near, self.from_line = buffers
        self.load_sem, self.send_sem, self.recv_sem = sems
        self.sent = []

    def owner(self, flips, z):
        y, x, z = self.l.coords(flips, z)
        return (x * self.l.Z + z) * 2 + y if self.natural else self.l.index((y, x, z))

    def load(self, colour, side, step):
        l = self.l
        near, far = l.sides(colour)
        z = l.z + step
        return pltpu.make_async_copy(
            self.grads.at[self.owner((near,) if side else (), z), colour],
            self.held.at[colour, side, z],
            self.load_sem.at[self.i, colour, side * l.Z + z],
        )

    def remote(self, colour, kind, step, to):
        l, Z = self.l, self.l.Z
        near, far = l.sides(colour)
        z = l.z + step
        if kind in ("far0", "far1"):
            side = int(kind[3])
            src = self.grads.at[self.owner((near, far) if side else (far,), z), colour]
            dst = self.from_far.at[colour, side, z]
            send, recv = side * Z, side * Z
        elif kind == "near":
            src, dst = self.held.at[colour, 1, z], self.from_near.at[colour, z]
            send, recv = 2 * Z, 2 * Z
        else:
            way = int(kind[4])
            src, dst = self.held.at[colour, 0, z], self.from_line.at[colour, way, z]
            send, recv = 3 * Z, (3 + way) * Z
        return pltpu.make_async_remote_copy(
            src_ref=src,
            dst_ref=dst,
            send_sem=self.send_sem.at[self.i, colour, send + z],
            recv_sem=self.recv_sem.at[self.i, colour, recv + z],
            device_id=l.target(to),
            device_id_type=MESH,
        )

    def arrive(self, colour, kind, step):
        self.remote(colour, kind, step, "cx").wait_recv()

    def send(self, step, *what):
        self.remote(*what).start()
        self.sent.append((step, what))

    def order(self):
        return offsets(self.l.Z)[::-1] + [0]

    def start(self):
        for step in self.order():
            for colour in (0, 1):
                near, far = self.l.sides(colour)

                def run():
                    self.send(step, colour, "far1", step, far)
                    self.load(colour, 1, step).start()

                self.l.when([step], run)

    def rest(self, step):
        for colour in (0, 1):
            near, far = self.l.sides(colour)

            def run():
                self.send(step, colour, "far0", step, far)
                self.load(colour, 0, step).start()

            self.l.when([step], run)

    def total(self, target, parts):
        rows, cols = target.shape
        pieces = 5 if cols % 640 == 0 else 1
        wide_cols = cols // pieces

        def one(p, carry):
            window = pl.ds(pl.multiple_of(p * wide_cols, 128), wide_cols)
            value = parts[0][:, window].astype(wide)
            for part in parts[1:]:
                value = value + part[:, window].astype(wide)
            target[:, window] = value.astype(target.dtype)
            return carry

        lax.fori_loop(0, pieces, one, 0)

    def near(self, step):
        for colour in (0, 1):
            near, far = self.l.sides(colour)

            def run():
                z = self.l.z + step
                self.load(colour, 1, step).wait()
                self.arrive(colour, "far1", step)
                mine = self.held.at[colour, 1, z]
                self.total(mine, [mine, self.from_far.at[colour, 1, z]])
                self.send(step, colour, "near", step, near)

            self.l.when([step], run)

    def parts(self, colour, step):
        z = self.l.z + step
        self.load(colour, 0, step).wait()
        self.arrive(colour, "far0", step)
        self.arrive(colour, "near", step)
        return [
            self.held.at[colour, 0, z],
            self.from_far.at[colour, 0, z],
            self.from_near.at[colour, z],
        ]

    def line(self, step):
        l = self.l
        toward, way = (1, 0) if step > 0 else (-1, 1)
        for colour in (0, 1):

            def run():
                z = l.z + step
                behind = l.has(-toward)
                parts = self.parts(colour, step)
                mine = self.held.at[colour, 0, z]

                @pl.when(behind)
                def _():
                    self.arrive(colour, f"line{way}", step)
                    self.total(mine, parts + [self.from_line.at[colour, way, z]])

                @pl.when(jnp.logical_not(behind))
                def _():
                    self.total(mine, parts)

                self.send(step, colour, f"line{way}", step, toward)

            l.when([step], run)

    def finish(self):
        l = self.l
        for colour in (0, 1):
            z = l.z
            parts = self.parts(colour, 0)
            left, right = self.from_line.at[colour, 0, z], self.from_line.at[colour, 1, z]
            target = self.out.at[colour]
            l.when([-1], lambda: self.arrive(colour, "line0", 0))
            l.when([1], lambda: self.arrive(colour, "line1", 0))
            l.when([-1, 1], lambda: self.total(target, parts + [left, right]))
            pl.when(jnp.logical_not(l.has(-1)))(lambda: self.total(target, parts + [right]))
            pl.when(jnp.logical_not(l.has(1)))(lambda: self.total(target, parts + [left]))

    def drain(self):
        for step, what in self.sent:
            self.l.when([step], lambda: self.remote(*what).wait_send())

    @staticmethod
    def buffers(blocks, Z):
        sizes = ((2, Z), (2, Z), (Z,), (2, Z))
        return [pltpu.VMEM((2,) + lead + b.shape[2:], low) for lead in sizes for b in blocks]

    @staticmethod
    def semaphores(n, Z):
        return [
            pltpu.SemaphoreType.DMA((n, 2, 2 * Z)),
            pltpu.SemaphoreType.DMA((n, 2, 4 * Z)),
            pltpu.SemaphoreType.DMA((n, 2, 5 * Z)),
        ]

    @staticmethod
    def works(links, grads, outs, buffers, sems, natural=()):
        n = len(grads)
        return [
            Scatter(
                links, i, grads[i], outs[i], [buffers[j * n + i] for j in range(4)], sems, i in natural
            )
            for i in range(n)
        ]

    @staticmethod
    def ticks(works):
        order = works[0].order()
        pairs = [order[p : p + 2] for p in range(0, len(order), 2)]

        def near(work, pair):
            for step in pair:
                work.near(step)
                work.rest(step)

        def line(work, pair):
            for step in pair:
                work.line(step)

        out = [works[0].start]
        for i, work in enumerate(works):
            out += [functools.partial(near, work, pair) for pair in pairs]
            if i + 1 < len(works):
                out.append(works[i + 1].start)
            out += [functools.partial(line, work, pair) for pair in pairs[:-1]]
            if i:
                out.append(works[i - 1].finish)
        out.append(works[-1].finish)
        return out


def scatter_kernel(Z, n, *refs):
    links = Links(Z)
    links.barrier()
    works = Scatter.works(links, refs[:n], refs[n : 2 * n], refs[2 * n : 6 * n], refs[6 * n :])
    for tick in Scatter.ticks(works):
        tick()
    for work in works:
        work.drain()


def scatter_blocks(blocks, Z):
    n = len(blocks)
    return pl.pallas_call(
        functools.partial(scatter_kernel, Z, n),
        out_shape=tuple(jax.ShapeDtypeStruct(b.shape[1:], wide) for b in blocks),
        in_specs=full(n, pl.ANY),
        out_specs=tuple(full(n)),
        scratch_shapes=Scatter.buffers(blocks, Z) + Scatter.semaphores(n, Z),
        compiler_params=pltpu.CompilerParams(
            collective_id=1, has_side_effects=True, vmem_limit_bytes=BIG
        ),
    )(*blocks)


def spread(ticks, first, steps):
    plan = {}
    for j, tick in enumerate(ticks):
        plan.setdefault(first + (j * steps) // len(ticks), []).append(tick)
    return plan


def run_plan(plan, step):
    for at in sorted(plan):

        def run():
            for tick in plan[at]:
                tick()

        pl.when(step == at)(run)


def backward_beside_scatter_kernel(Z, n, heads, tile, *refs):
    qkv, far, tags_q, tags_k, mixed, logs, grad_in = refs[:7]
    grads = refs[7 : 7 + n]
    outs = refs[7 + n : 7 + 2 * n]
    dqkv = refs[7 + 2 * n]
    rest = refs[8 + 2 * n :]
    acc_k, acc_v, own, away, got, send_sem, recv_sem = rest[:7]
    links = Links(Z)
    core = lax.axis_index("core")
    works = Scatter.works(
        links, grads, outs, rest[7 : 7 + 4 * n], rest[7 + 4 * n :], natural=(0,)
    )
    width = heads * HD
    rows = qkv.shape[1]
    tiles = rows // tile
    groups = heads // GROUP_HEADS
    span = GROUP_HEADS * HD
    scale = HD ** (-0.5)
    factor = scale * math.log2(math.e)

    def back_copy(g, which):
        at = pl.ds(which * width + g * span, span)
        return pltpu.make_async_remote_copy(
            src_ref=away.at[at],
            dst_ref=got.at[at],
            send_sem=send_sem.at[g, which],
            recv_sem=recv_sem.at[g, which],
            device_id=links.target("pair"),
            device_id_type=MESH,
        )

    def send_back(g):
        for which in (0, 1):
            back_copy(g, which).start()

    def add_back(g):
        for which in (0, 1):
            back_copy(g, which).wait_recv()
            for h in range(GROUP_HEADS):
                at = which * width + g * span + h * HD
                dqkv[pl.ds(width + at, HD)] = (
                    own[pl.ds(at, HD)] + got[pl.ds(at, HD)].astype(wide)
                ).astype(low)

    links.barrier()
    steps = heads * tiles
    plan = spread(Scatter.ticks(works), 0, steps)
    per = GROUP_HEADS * tiles
    for g in range(groups - 1):
        plan.setdefault((g + 1) * per + 1, []).append(functools.partial(send_back, g))

    def attend(index):
        head, part = index // tiles, lax.rem(index, tiles)
        row = head * HD
        columns = pl.ds(pl.multiple_of(part * tile, tile), tile)

        def feature(base):
            return pl.ds(pl.multiple_of(base + row, 16), HD)

        head_query = qkv[feature(0), columns]
        grad = grad_in[feature(0), columns]
        query = jnp.concatenate([head_query, tags_q[:, columns]], axis=0)
        attended = mixed[feature(core * width), columns]
        delta = jnp.sum(grad.astype(wide) * attended.astype(wide), axis=0, keepdims=True)
        log_row = logs[head, :, columns]
        query_rows = head_query.T
        grad_rows = grad.T
        dq = jnp.zeros((HD, tile), wide)

        @pl.when(part == 0)
        def _():
            acc_k[...] = jnp.zeros_like(acc_k)
            acc_v[...] = jnp.zeros_like(acc_v)

        keys = (qkv[feature(width), :], far[feature(0), :])
        values = (qkv[feature(2 * width), :], far[feature(width), :])
        for b in (0, 1):
            key = jnp.concatenate([keys[b], tags_k[b]], axis=0)
            probs = jnp.exp2(dims(key, query, 0, 0) * factor - log_row)
            grad_probs = dims(values[b], grad, 0, 0)
            score_grad = (probs * (grad_probs - delta)).astype(low)
            acc_v[b] += dims(probs.astype(low), grad_rows, 1, 0)
            acc_k[b] += dims(score_grad, query_rows, 1, 0)
            dq = dq + dims(keys[b], score_grad, 1, 0)
        dqkv[feature(0), columns] = (dq * scale).astype(low)

        @pl.when(part == tiles - 1)
        def _():
            own[feature(0), :] = acc_k[0].T * scale
            own[feature(width), :] = acc_v[0].T
            away[feature(0), :] = (acc_k[1].T * scale).astype(low)
            away[feature(width), :] = acc_v[1].T.astype(low)

    def step(s, carry):
        run_plan(plan, s)
        attend(s)
        return carry

    lax.fori_loop(0, steps, step, 0)
    send_back(groups - 1)
    for g in range(groups):
        add_back(g)
    for g in range(groups):
        for which in (0, 1):
            back_copy(g, which).wait_send()
    for work in works:
        work.drain()


def backward_beside_scatter(qkv_t, far, tags_q, tags_k, mixed, logs, grad, blocks, Z, heads, tile):
    n = len(blocks)
    rows = qkv_t.shape[1]
    groups = heads // GROUP_HEADS
    outs = pl.pallas_call(
        functools.partial(backward_beside_scatter_kernel, Z, n, heads, tile),
        out_shape=tuple(jax.ShapeDtypeStruct(b.shape[1:], wide) for b in blocks)
        + (jax.ShapeDtypeStruct(qkv_t.shape, low),),
        in_specs=full(7) + full(n, pl.ANY),
        out_specs=tuple(full(n + 1)),
        scratch_shapes=[
            pltpu.VMEM((2, rows, HD), wide),
            pltpu.VMEM((2, rows, HD), wide),
            pltpu.VMEM((2 * heads * HD, rows), wide),
            pltpu.VMEM((2 * heads * HD, rows), low),
            pltpu.VMEM((2 * heads * HD, rows), low),
            pltpu.SemaphoreType.DMA((groups, 2)),
            pltpu.SemaphoreType.DMA((groups, 2)),
        ]
        + Scatter.buffers(blocks, Z)
        + Scatter.semaphores(n, Z),
        compiler_params=pltpu.CompilerParams(
            collective_id=3, has_side_effects=True, vmem_limit_bytes=BIG
        ),
    )(qkv_t, far, tags_q, tags_k, mixed, logs, grad, *blocks)
    return outs[:n], outs[n]


def general_body(
    n_chip_rows,
    Z,
    frames,
    clip_ids,
    query_weight,
    key_weight,
    value_weight,
    output_weight,
    inner_weight,
    outer_weight,
    query_bias,
    value_bias,
    output_bias,
    inner_bias,
    outer_bias,
    first_gain,
    first_shift,
    second_gain,
    second_shift,
    out_cotangent,
):
    K = n_chip_rows * Z
    R, D = frames.shape[2], frames.shape[3]
    FF = inner_weight.shape[1]
    r = query_weight.shape[0]
    f = outer_weight.shape[0]
    hw = D // 2
    heads = H // 2
    half = Z // 2
    core = lax.axis_index("core")
    first_core = core == 0
    zz = lax.axis_index("zz")
    micro = zz // half
    first_half = micro == 0
    place = zz % half

    def swap_core(v):
        return lax.ppermute(v, "core", [(0, 1), (1, 0)])

    def swap_half(v):
        return lax.ppermute(v, "zz", [(z, (z + half) % Z) for z in range(Z)])

    def by_core(own, other, axis):
        return jnp.where(
            first_core,
            jnp.concatenate([own, other], axis),
            jnp.concatenate([other, own], axis),
        )

    def pick(v, index, axis):
        return lax.dynamic_index_in_dim(v, index, axis, keepdims=False)

    def take_rows(v):
        v = v[:, 0]
        own, away = pick(v, micro, 0), pick(v, 1 - micro, 0)
        got = swap_half(away)
        pair = jnp.where(first_half, jnp.stack([own, got]), jnp.stack([got, own]))
        both = by_core(pair[:, None], swap_core(pair)[:, None], 1)
        return both.reshape(4 * R, D)

    qkv = jnp.stack([query_weight, key_weight, value_weight], 1).reshape(r, 3, 2, hw)
    inner_split = inner_weight.reshape(r, K, 2, f)
    vectors = (
        query_bias, value_bias, output_bias, outer_bias,
        first_gain, first_shift, second_gain, second_shift, inner_bias,
    )
    small = jnp.concatenate(vectors)
    n_small = small.shape[0]

    def column_half(which):
        return jnp.concatenate(
            [
                pick(qkv, which, 2).reshape(r, 3 * hw),
                pick(inner_split, which, 2).reshape(r, FF // 2),
            ],
            1,
        )

    mine = column_half(core)
    theirs = swap_core(column_half(1 - core))
    both = by_core(mine[None], theirs[None], 0)
    small_both = by_core(small[None], swap_core(small)[None], 0)
    small_pad = -(-n_small // 1024) * 1024
    small_both = jnp.pad(small_both, ((0, 0), (0, small_pad - n_small)))
    shards = (
        small_both.reshape(2, small_pad // 128, 128),
        both[:, :, : 3 * hw],
        output_weight.reshape(r, 2, hw).transpose(1, 0, 2),
        both[:, :, 3 * hw :],
        outer_weight.reshape(2, f // 2, D),
    )
    small_all, qkv_all, out_all, inner_all, outer_all = (
        lax.all_gather(v, CHIPS, axis=0, tiled=False) for v in shards
    )
    x_rows = take_rows(frames)
    cot = take_rows(out_cotangent)

    w_qkv = qkv_all.reshape(D, 3 * hw)
    w_inner = inner_all.reshape(D, FF // 2)
    w_outer = outer_all.reshape(FF // 2, D)
    out_own = out_all.transpose(0, 2, 1, 3).reshape(K, 1, r, D)
    w_out = by_core(out_own, swap_core(out_own), 1).reshape(D, D)
    small_all = small_all.reshape(K, 2, small_pad)[:, :, :n_small].astype(wide)
    names = ("qb", "vb", "ob", "ub", "g1", "s1", "g2", "s2")
    vec = {n: small_all[:, :, i * r : (i + 1) * r].reshape(D) for i, n in enumerate(names)}
    ib_half = pick(small_all[:, :, 8 * r :], core, 1).reshape(FF // 2)

    def own_columns(v):
        return lax.dynamic_slice_in_dim(v, core * hw, hw, v.ndim - 1)

    ids = pick(clip_ids[:, 0], micro, 0).reshape(2, half, 2 * R)
    ids_q = pick(ids, place, 1).reshape(4 * R)
    order = (place - jnp.arange(half)) % half
    ids_k = jnp.take(ids, order, axis=1).transpose(1, 0, 2).reshape(half, 4 * R)
    tag = jnp.arange(TAGS, dtype=jnp.int32)[:, None]
    tags_q = jnp.where(ids_q[None, :] == tag, 0.0, masked_score).astype(low)
    tags_k = (ids_k[:, None, :] == tag[None]).astype(low)

    xf = x_rows.astype(wide)
    xhat, inverse = row_stats(xf)
    normed = (xhat * vec["g1"] + vec["s1"]).astype(low)
    bias_qkv = jnp.concatenate(
        [own_columns(vec["qb"]), jnp.zeros((hw,), wide), own_columns(vec["vb"])]
    )
    qkv_t = (dims(w_qkv, normed, 0, 1) + bias_qkv[:, None]).astype(low)
    q_t, kv_own = qkv_t[:hw], qkv_t[hw:]
    kv_parts = [kv_own]
    for o in range(1, half):
        kv_parts.append(
            lax.ppermute(
                kv_own, "zz", [(z, (z // half) * half + (z + o) % half) for z in range(Z)]
            )
        )
    kv = jnp.stack(kv_parts)
    tile = 256
    mixed_t, logs = attend_forward(q_t, tags_q, kv, tags_k, heads, tile)
    mixed_full = by_core(mixed_t, swap_core(mixed_t), 0)
    middle = xf + (dims(mixed_full, w_out, 0, 0) + vec["ob"])
    xhat_two, inverse_two = row_stats(middle)
    normed_two = (xhat_two * vec["g2"] + vec["s2"]).astype(low)
    inner = dims(normed_two, w_inner, 1, 0) + ib_half
    active, slope = gelu_parts(inner)
    active = active.astype(low)
    out_part = dims(active, w_outer, 1, 0)

    def split_rows(v):
        return v.reshape(2, 2, R, D)

    def reduce_rows(v):
        v = split_rows(v)
        return pick(v, core, 1) + swap_core(pick(v, 1 - core, 1).astype(low)).astype(wide)

    def home_rows(v):
        stay = pick(v, micro, 0)
        got = swap_half(pick(v, 1 - micro, 0))
        return jnp.where(first_half, jnp.stack([stay, got]), jnp.stack([got, stay]))[:, None]

    own_middle = pick(split_rows(middle), core, 1)
    layer_rows = (own_middle + (reduce_rows(out_part) + vec["ub"])).astype(low)
    layer_out = home_rows(layer_rows)

    grad_active = dims(cot, w_outer, 1, 1)
    inner_grad = (grad_active * slope).astype(low)
    part_two = dims(inner_grad, w_inner, 1, 1)
    grad_two = part_two + swap_core(part_two.astype(low)).astype(wide)
    middle_grad = cot.astype(wide) + norm_pull(grad_two, vec["g2"], xhat_two, inverse_two)
    branch_grad = middle_grad.astype(low)
    w_out_heads = lax.dynamic_slice_in_dim(w_out, core * hw, hw, 0)
    mixed_grad = dims(w_out_heads, branch_grad, 1, 1).astype(low)
    dq_t, own_kv, far_kv = attend_backward(
        q_t, tags_q, kv, tags_k, mixed_t, logs, mixed_grad, heads, tile
    )
    dkv = own_kv.reshape(2 * hw, 4 * R)
    for o in range(1, half):
        back = lax.ppermute(
            far_kv[o - 1], "zz", [(z, (z // half) * half + (z - o) % half) for z in range(Z)]
        )
        dkv = dkv + back.reshape(2 * hw, 4 * R).astype(wide)
    dqkv_t = jnp.concatenate([dq_t, dkv.astype(low)], 0)
    grad_one = reduce_rows(dims(dqkv_t, w_qkv, 0, 1))
    own_xhat = pick(split_rows(xhat), core, 1)
    own_inverse = pick(inverse.reshape(2, 2, R, 1), core, 1)
    frame_rows = pick(split_rows(middle_grad), core, 1) + norm_pull(
        grad_one, vec["g1"], own_xhat, own_inverse
    )
    sent = swap_half(pick(frame_rows, 1 - micro, 0).astype(low)).astype(wide)
    stay = pick(frame_rows, micro, 0)
    frames_grad = jnp.where(first_half, jnp.stack([stay, sent]), jnp.stack([sent, stay]))[:, None]

    g_qkv = dims(normed, dqkv_t, 0, 1).astype(low)
    g_out = dims(mixed_full, own_columns(branch_grad), 1, 0).astype(low)
    g_inner = dims(normed_two, inner_grad, 0, 0).astype(low)
    g_outer = dims(active, cot, 0, 0).astype(low)

    def zero_rest(v):
        return by_core(v, jnp.zeros_like(v), 0)

    bias_sums = jnp.sum(dqkv_t.astype(wide), axis=1)
    halves = 0.5
    col = {
        "qb": zero_rest(bias_sums[:hw]),
        "vb": zero_rest(bias_sums[2 * hw :]),
        "ob": halves * jnp.sum(branch_grad.astype(wide), 0),
        "ub": halves * jnp.sum(cot.astype(wide), 0),
        "g1": jnp.sum(grad_one * own_xhat, (0, 1)),
        "s1": jnp.sum(grad_one, (0, 1)),
        "g2": halves * jnp.sum(grad_two * xhat_two, 0),
        "s2": halves * jnp.sum(grad_two, 0),
    }
    ib_sum = jnp.sum(inner_grad.astype(wide), 0).reshape(K, 1, f)
    small_grad = jnp.concatenate(
        [col[n].reshape(K, 2, r) for n in names]
        + [by_core(ib_sum, jnp.zeros_like(ib_sum), 1)],
        2,
    )
    small_grad = jnp.pad(small_grad, ((0, 0), (0, 0), (0, small_pad - n_small)))
    small_grad = small_grad.reshape(K, 2, small_pad // 128, 128).astype(low)
    g_outer, g_inner, g_out, g_qkv, g_small = (
        lax.psum_scatter(v, CHIPS, scatter_dimension=0, tiled=False).astype(wide)
        for v in (
            g_outer.reshape(K, 2, f // 2, D),
            g_inner.reshape(K, 2, r, FF // 2),
            g_out.reshape(K, 2, r, hw),
            g_qkv.reshape(K, 2, r, 3 * hw),
            small_grad,
        )
    )
    wide_rows = jnp.concatenate([g_qkv, g_out, g_inner], 2)
    mine = pick(wide_rows, core, 0)
    theirs = swap_core(pick(wide_rows, 1 - core, 0))

    def whole(a, b, parts):
        a, b = a.reshape(r, parts, 1, -1), b.reshape(r, parts, 1, -1)
        return by_core(a, b, 2).reshape(r, -1)

    outs = []
    for i in range(4):
        outs.append(whole(mine[:, i * hw : (i + 1) * hw], theirs[:, i * hw : (i + 1) * hw], 1))
    outs.append(whole(mine[:, 4 * hw :], theirs[:, 4 * hw :], K))
    outs.append(g_outer.reshape(f, D))
    g_small = g_small.reshape(2, small_pad)[:, :n_small]
    g_small = pick(g_small, core, 0) + swap_core(pick(g_small, 1 - core, 0))
    sv = {n: g_small[i * r : (i + 1) * r] for i, n in enumerate(names)}
    return (layer_out, frames_grad) + tuple(outs) + (
        sv["qb"], sv["vb"], sv["ob"], g_small[8 * r :], sv["ub"],
        sv["g1"], sv["s1"], sv["g2"], sv["s2"],
    )


VECTORS = ("qb", "vb", "ob", "ub", "g1", "s1", "g2", "s2")


def linked_body(
    Z,
    frames,
    clip_ids,
    query_weight,
    key_weight,
    value_weight,
    output_weight,
    inner_weight,
    outer_weight,
    query_bias,
    value_bias,
    output_bias,
    inner_bias,
    outer_bias,
    first_gain,
    first_shift,
    second_gain,
    second_shift,
    out_cotangent,
):
    K = 4 * Z
    R, D = frames.shape[2], frames.shape[3]
    FF = inner_weight.shape[1]
    r = query_weight.shape[0]
    f = outer_weight.shape[0]
    hw = D // 2
    heads = H // 2
    half = Z // 2
    core = lax.axis_index("core")
    first_core = core == 0
    zz = lax.axis_index("zz")
    micro = zz // half
    first_half = micro == 0
    place = zz % half
    tile = 256

    def swap_core(v):
        return lax.ppermute(v, "core", [(0, 1), (1, 0)])

    def swap_half(v):
        return lax.ppermute(v, "zz", [(z, (z + half) % Z) for z in range(Z)])

    def by_core(own, other, axis):
        return jnp.where(
            first_core,
            jnp.concatenate([own, other], axis),
            jnp.concatenate([other, own], axis),
        )

    def pick(v, index, axis):
        return lax.dynamic_index_in_dim(v, index, axis, keepdims=False)

    def own_columns(v):
        return lax.dynamic_slice_in_dim(v, core * hw, hw, v.ndim - 1)

    small = jnp.concatenate(
        [
            jnp.stack(
                [
                    query_bias, value_bias, output_bias, outer_bias,
                    first_gain, first_shift, second_gain, second_shift,
                ]
            ),
            inner_bias.reshape(f // r, r),
        ]
    )
    small = jnp.pad(small, ((0, 16 - small.shape[0]), (0, 128 - r)))

    ids = pick(clip_ids[:, 0], micro, 0).reshape(2, half, 2 * R)
    ids_q = pick(ids, place, 1).reshape(4 * R)
    ids_far = pick(ids, 1 - place, 1).reshape(4 * R)
    tag = jnp.arange(TAGS, dtype=jnp.int32)[:, None]
    tags_q = jnp.where(ids_q[None, :] == tag, 0.0, masked_score).astype(low)
    tags_k = (jnp.stack([ids_q, ids_far])[:, None, :] == tag[None]).astype(low)

    weights = (query_weight, key_weight, value_weight, output_weight, inner_weight, outer_weight)
    fw = forward_linked(frames, out_cotangent, weights, small, tags_q, tags_k, Z, heads, tile)
    vec = {n: fw.vectors[i] for i, n in enumerate(VECTORS)}
    cot = fw.cot_rows.reshape(4 * R, D)
    active, slope, middle = fw.active, fw.slope, fw.middle
    normed, normed_two = fw.normed, fw.normed_two
    g_outer = dims(active, cot, 0, 0).astype(low).reshape(K, 2, f // 2, D)
    out_part = dims(active, fw.w_outer, 1, 0)

    def split_rows(v):
        return v.reshape(2, 2, R, D)

    def reduce_rows(v):
        v = split_rows(v)
        return pick(v, core, 1) + swap_core(pick(v, 1 - core, 1).astype(low)).astype(wide)

    def home_rows(v):
        stay = pick(v, micro, 0)
        got = swap_half(pick(v, 1 - micro, 0))
        return jnp.where(first_half, jnp.stack([stay, got]), jnp.stack([got, stay]))[:, None]

    own_middle = pick(split_rows(middle), core, 1)
    layer_rows = (own_middle + (reduce_rows(out_part) + vec["ub"])).astype(low)
    grad_active = dims(cot, fw.w_outer, 1, 1)
    inner_grad = (grad_active * slope).astype(low)
    part_two = dims(inner_grad, fw.w_inner, 1, 1)
    grad_two = part_two + swap_core(part_two.astype(low)).astype(wide)
    xhat_two, inverse_two = row_stats(middle)
    middle_grad = cot.astype(wide) + norm_pull(grad_two, vec["g2"], xhat_two, inverse_two)
    branch_grad = middle_grad.astype(low)
    w_heads = lax.dynamic_slice_in_dim(fw.w_out, core * hw, hw, 1)
    mixed_grad = sum(
        dims(w_heads[b], branch_grad[:, b * hw : (b + 1) * hw], 1, 1) for b in (0, 1)
    ).astype(low)
    g_inner = dims(normed_two, inner_grad, 0, 0).astype(low).reshape(K, 2, r, FF // 2)
    (g_outer, g_inner), dqkv_t = backward_beside_scatter(
        fw.qkv, fw.far, tags_q, tags_k, fw.mixed, fw.logs, mixed_grad,
        (g_outer, g_inner), Z, heads, tile,
    )
    layer_rows, dqkv_t = lax.optimization_barrier((layer_rows, dqkv_t))
    layer_out = home_rows(layer_rows)
    g_outer = lax.ppermute(
        g_outer.reshape(f, D), ("cy", "core"), [(0, 0), (1, 2), (2, 1), (3, 3)]
    )
    grad_one = reduce_rows(dims(dqkv_t, fw.w_qkv, 0, 1))
    own_xhat, own_inverse = row_stats(pick(split_rows(fw.x_rows), core, 1).astype(wide))
    frame_rows = pick(split_rows(middle_grad), core, 1) + norm_pull(
        grad_one, vec["g1"], own_xhat, own_inverse
    )
    sent = swap_half(pick(frame_rows, 1 - micro, 0).astype(low)).astype(wide)
    stay = pick(frame_rows, micro, 0)
    frames_grad = jnp.where(first_half, jnp.stack([stay, sent]), jnp.stack([sent, stay]))[:, None]

    g_qkv = dims(normed, dqkv_t, 0, 1).astype(low)
    g_out = dims(fw.mixed, own_columns(branch_grad), 1, 0).astype(low)

    def zero_rest(v):
        return by_core(v, jnp.zeros_like(v), 0)

    bias_sums = jnp.sum(dqkv_t.astype(wide), axis=1)
    halves = 0.5
    col = {
        "qb": zero_rest(bias_sums[:hw]),
        "vb": zero_rest(bias_sums[2 * hw :]),
        "ob": halves * jnp.sum(branch_grad.astype(wide), 0),
        "ub": halves * jnp.sum(cot.astype(wide), 0),
        "g1": jnp.sum(grad_one * own_xhat, (0, 1)),
        "s1": jnp.sum(grad_one, (0, 1)),
        "g2": halves * jnp.sum(grad_two * xhat_two, 0),
        "s2": halves * jnp.sum(grad_two, 0),
    }
    ib_sum = zero_rest(jnp.sum(inner_grad.astype(wide), 0))
    small_grad = jnp.concatenate(
        [col[n].reshape(K, 2, r) for n in VECTORS] + [ib_sum.reshape(K, 2, f)], 2
    )
    n_small = 8 * r + f
    small_pad = -(-n_small // 1024) * 1024
    small_grad = jnp.pad(small_grad, ((0, 0), (0, 0), (0, small_pad - n_small)))
    small_grad = small_grad.reshape(K, 2, small_pad // 128, 128).astype(low)
    g_small, g_qkv, g_out = scatter_blocks(
        (small_grad, g_qkv.reshape(K, 2, r, 3 * hw), g_out.reshape(K, 2, r, hw)), Z
    )
    wide_rows = jnp.concatenate([g_qkv, g_out], 2)

    def own_rows(v):
        mine = pick(v, core, 0)
        theirs = swap_core(pick(v, 1 - core, 0))
        return mine, theirs

    mine, theirs = own_rows(wide_rows)
    outs = [
        by_core(mine[:, i * hw : (i + 1) * hw], theirs[:, i * hw : (i + 1) * hw], 1)
        for i in range(4)
    ]
    outs.append(by_core(*own_rows(g_inner), 1))
    outs.append(g_outer)
    g_small = g_small.reshape(2, small_pad)[:, :n_small]
    g_small = pick(g_small, core, 0) + swap_core(pick(g_small, 1 - core, 0))
    sv = {n: g_small[i * r : (i + 1) * r] for i, n in enumerate(VECTORS)}
    return (layer_out, frames_grad) + tuple(outs) + (
        sv["qb"], sv["vb"], sv["ob"], g_small[8 * r :], sv["ub"],
        sv["g1"], sv["s1"], sv["g2"], sv["s2"],
    )


def solution(mesh):
    C, S = mesh.shape["clip"], mesh.shape["seq"]
    fine = Mesh(mesh.devices.reshape(2, C // 2, S // 2, 2), ("cy", "cx", "zz", "core"))
    clip, seq = ("cy", "cx"), ("zz", "core")
    every = clip + seq
    rows, mat, vec = P(None, clip, seq, None), P(every, None), P(every)
    in_specs = (rows, P(None, clip, None)) + (mat,) * 6 + (vec,) * 9 + (rows,)
    out_specs = (rows, rows) + (mat,) * 6 + (vec,) * 9
    linked = C == 4 and S == 8
    run = functools.partial(linked_body, S // 2) if linked else functools.partial(general_body, C, S // 2)
    return jax.shard_map(
        run,
        mesh=fine,
        in_specs=in_specs,
        out_specs=out_specs,
        check_vma=False,
    )
```

```python
import functools
import math
from typing import Any, NamedTuple

import jax
import jax.numpy as jnp
from jax import lax
from jax.experimental import pallas as pl
from jax.experimental.pallas import tpu as pltpu
from jax.sharding import Mesh
from jax.sharding import PartitionSpec as P

H = 16
HD = 80
TAGS = 16
epsilon = 1e-05
masked_score = -1e30
low = jnp.bfloat16
wide = jnp.float32


def dims(left_side, right_side, left_dim, right_dim):
    return lax.dot_general(
        left_side,
        right_side,
        (((left_dim,), (right_dim,)), ((), ())),
        preferred_element_type=wide,
    )


def attend_forward_kernel(blocks, q_ref, qa_ref, k_ref, v_ref, ka_ref, out_ref, log_ref):
    factor = HD ** (-0.5) * math.log2(math.e)
    query = jnp.concatenate([q_ref[...], qa_ref[...]], axis=0)
    scores = []
    for b in range(blocks):
        key = jnp.concatenate([k_ref[b], ka_ref[b]], axis=0)
        scores.append(dims(key, query, 0, 0))
    top = functools.reduce(jnp.maximum, [jnp.max(s, axis=0, keepdims=True) for s in scores])
    top = top * factor
    total = jnp.zeros_like(top)
    mixed = jnp.zeros((HD, query.shape[1]), wide)
    for b in range(blocks):
        part = jnp.exp2(scores[b] * factor - top)
        total = total + jnp.sum(part, axis=0, keepdims=True)
        mixed = mixed + dims(v_ref[b], part.astype(low), 1, 0)
    out_ref[...] = (mixed / total).astype(low)
    log_ref[0] = top + jnp.log2(total)


def attend_forward(q_t, tags_q, kv, tags_k, heads, tile):
    blocks, _, width = kv.shape
    rows = q_t.shape[1]
    grid = (heads, rows // tile)
    return pl.pallas_call(
        functools.partial(attend_forward_kernel, blocks),
        grid=grid,
        out_shape=(
            jax.ShapeDtypeStruct((heads * HD, rows), low),
            jax.ShapeDtypeStruct((heads, 1, rows), wide),
        ),
        in_specs=[
            pl.BlockSpec((HD, tile), lambda h, t: (h, t)),
            pl.BlockSpec((TAGS, tile), lambda h, t: (0, t)),
            pl.BlockSpec((blocks, HD, width), lambda h, t: (0, h, 0)),
            pl.BlockSpec((blocks, HD, width), lambda h, t: (0, heads + h, 0)),
            pl.BlockSpec((blocks, TAGS, width), lambda h, t: (0, 0, 0)),
        ],
        out_specs=(
            pl.BlockSpec((HD, tile), lambda h, t: (h, t)),
            pl.BlockSpec((1, 1, tile), lambda h, t: (h, 0, t)),
        ),
        cost_estimate=pl.CostEstimate(
            flops=4 * heads * rows * blocks * width * HD,
            bytes_accessed=2 * kv.size,
            transcendentals=heads * rows * blocks * width,
        ),
    )(q_t, tags_q, kv, kv, tags_k)


def attend_backward_kernel(
    blocks, q_ref, qa_ref, k_ref, v_ref, ka_ref, o_ref, log_ref, g_ref, dq_ref, own_ref, far_ref, acc_k, acc_v
):
    factor = HD ** (-0.5) * math.log2(math.e)
    step, steps = pl.program_id(1), pl.num_programs(1)
    head_query = q_ref[...]
    grad = g_ref[...]
    query = jnp.concatenate([head_query, qa_ref[...]], axis=0)
    delta = jnp.sum(grad.astype(wide) * o_ref[...].astype(wide), axis=0, keepdims=True)
    logs = log_ref[0]
    query_rows = head_query.T
    grad_rows = grad.T
    dq = jnp.zeros(head_query.shape, wide)

    @pl.when(step == 0)
    def _():
        acc_k[...] = jnp.zeros_like(acc_k)
        acc_v[...] = jnp.zeros_like(acc_v)

    for b in range(blocks):
        key = jnp.concatenate([k_ref[b], ka_ref[b]], axis=0)
        probs = jnp.exp2(dims(key, query, 0, 0) * factor - logs)
        grad_probs = dims(v_ref[b], grad, 0, 0)
        score_grad = (probs * (grad_probs - delta)).astype(low)
        acc_v[b] += dims(probs.astype(low), grad_rows, 1, 0)
        acc_k[b] += dims(score_grad, query_rows, 1, 0)
        dq = dq + dims(k_ref[b], score_grad, 1, 0)
    dq_ref[...] = (dq * HD ** (-0.5)).astype(low)

    @pl.when(step == steps - 1)
    def _():
        for b in range(blocks):
            key_part = acc_k[b].T * HD ** (-0.5)
            value_part = acc_v[b].T
            if b == 0:
                own_ref[0] = key_part
                own_ref[1] = value_part
            else:
                far_ref[b - 1, 0] = key_part.astype(low)
                far_ref[b - 1, 1] = value_part.astype(low)


def attend_backward(q_t, tags_q, kv, tags_k, mixed_t, logs, grad_t, heads, tile):
    blocks, _, width = kv.shape
    rows = q_t.shape[1]
    grid = (heads, rows // tile)
    per_query = pl.BlockSpec((HD, tile), lambda h, t: (h, t))
    return pl.pallas_call(
        functools.partial(attend_backward_kernel, blocks),
        grid=grid,
        out_shape=(
            jax.ShapeDtypeStruct((heads * HD, rows), low),
            jax.ShapeDtypeStruct((2, heads * HD, width), wide),
            jax.ShapeDtypeStruct((blocks - 1, 2, heads * HD, width), low),
        ),
        in_specs=[
            per_query,
            pl.BlockSpec((TAGS, tile), lambda h, t: (0, t)),
            pl.BlockSpec((blocks, HD, width), lambda h, t: (0, h, 0)),
            pl.BlockSpec((blocks, HD, width), lambda h, t: (0, heads + h, 0)),
            pl.BlockSpec((blocks, TAGS, width), lambda h, t: (0, 0, 0)),
            per_query,
            pl.BlockSpec((1, 1, tile), lambda h, t: (h, 0, t)),
            per_query,
        ],
        out_specs=(
            per_query,
            pl.BlockSpec((2, HD, width), lambda h, t: (0, h, 0)),
            pl.BlockSpec((blocks - 1, 2, HD, width), lambda h, t: (0, 0, h, 0)),
        ),
        scratch_shapes=[
            pltpu.VMEM((blocks, width, HD), wide),
            pltpu.VMEM((blocks, width, HD), wide),
        ],
        cost_estimate=pl.CostEstimate(
            flops=10 * heads * rows * blocks * width * HD,
            bytes_accessed=4 * kv.size,
            transcendentals=heads * rows * blocks * width,
        ),
    )(q_t, tags_q, kv, kv, tags_k, mixed_t, logs, grad_t)


def row_stats(values):
    centre = jnp.mean(values, axis=-1, keepdims=True)
    centred = values - centre
    inverse = lax.rsqrt(jnp.mean(centred * centred, axis=-1, keepdims=True) + epsilon)
    return centred * inverse, inverse


def norm_pull(grad, gain, xhat, inverse):
    e = grad * gain
    return inverse * (
        e
        - jnp.mean(e, axis=-1, keepdims=True)
        - xhat * jnp.mean(e * xhat, axis=-1, keepdims=True)
    )


def gelu_parts(u):
    phi_sum = 0.5 * (1.0 + lax.erf(u * math.sqrt(0.5)))
    density = jnp.exp(-0.5 * u * u) * (1.0 / math.sqrt(2.0 * math.pi))
    return u * phi_sum, phi_sum + u * density


CHIPS = ("cy", "cx", "zz")
MESH = pl.DeviceIdType.MESH
BIG = 62 * 1024 * 1024


def offsets(Z):
    steps = []
    for d in range(1, Z):
        steps += [-d, d]
    return steps


def full(n, space=pltpu.VMEM):
    return [pl.BlockSpec(memory_space=space)] * n


class Links:
    def __init__(self, Z):
        self.Z = Z
        self.y, self.x, self.z = (lax.axis_index(a) for a in CHIPS)
        self.core = lax.axis_index("core")
        self.half = lax.div(self.z, Z // 2)
        self.crossed = lax.rem(self.y + self.core, 2)

    def sides(self, colour):
        return (("cx", "cy"), ("cy", "cx"))[colour]

    def coords(self, flips, z):
        y = 1 - self.y if "cy" in flips else self.y
        x = 1 - self.x if "cx" in flips else self.x
        return y, x, z

    def index(self, place):
        y, x, z = place
        return (y * 2 + x) * self.Z + z

    def at(self, flips, z):
        return self.index(self.coords(flips, z))

    def target(self, to):
        if to == "cy":
            return {"cy": 1 - self.y}
        if to == "cx":
            return {"cx": 1 - self.x}
        if to == "core":
            return {"core": 1 - self.core}
        if to == "pair":
            return {"zz": self.z + 1 - 2 * lax.rem(self.z, 2)}
        if to == "swap":
            return {"zz": self.z + (self.Z // 2) * (1 - 2 * self.half)}
        if to == "diagonal":
            return {"cy": self.core, "core": self.y}
        return {"zz": self.z + to}

    def has(self, step):
        there = self.z + step
        return jnp.logical_and(there >= 0, there < self.Z)

    def when(self, steps, run):
        steps = [s for s in steps if s]
        if steps:
            pl.when(functools.reduce(jnp.logical_and, [self.has(s) for s in steps]))(run)
        else:
            run()

    def barrier(self, *more):
        sem = pltpu.get_barrier_semaphore()
        for to in ("cy", "cx") + tuple(m for m in more if m != "diagonal"):
            pl.semaphore_signal(sem, inc=1, device_id=self.target(to), device_id_type=MESH)
        for step in (-1, 1):

            @pl.when(self.has(step))
            def _():
                pl.semaphore_signal(
                    sem, inc=1, device_id=self.target(step), device_id_type=MESH
                )

        count = 2 + len([m for m in more if m != "diagonal"])
        count = count + jnp.minimum(self.z, 1) + jnp.minimum(self.Z - 1 - self.z, 1)
        if "diagonal" in more:

            @pl.when(self.crossed == 1)
            def _():
                pl.semaphore_signal(
                    sem, inc=1, device_id=self.target("diagonal"), device_id_type=MESH
                )

            count = count + self.crossed
        pl.semaphore_wait(sem, count)


def remote(src, dst, send, recv, to):
    return pltpu.make_async_remote_copy(
        src_ref=src, dst_ref=dst, send_sem=send, recv_sem=recv, device_id=to, device_id_type=MESH
    )


class Gather:
    def __init__(self, links, block, sems):
        self.l, self.block = links, block
        self.send_sem, self.recv_sem = sems
        self.sent = []

    def copy(self, i, colour, flips, step, base, to):
        place = self.l.coords(flips, self.l.z + step)
        block = self.block(i, colour, place)
        return remote(
            block,
            block,
            self.send_sem.at[i, colour, base + self.l.z + step],
            self.recv_sem.at[i, colour, self.l.index(place)],
            self.l.target(to),
        )

    def send(self, steps, *what):
        self.l.when(steps, lambda: self.copy(*what).start())
        self.sent.append((steps, what))

    def arrive(self, i, colour, flips, step):
        self.l.when([step], lambda: self.copy(i, colour, flips, step, 0, "cx").wait_recv())

    def own(self, i):
        for colour in (0, 1):
            for step, base in ((1, 0), (-1, self.l.Z)):
                self.send([step], i, colour, (), 0, base, step)

    def along(self, i, distance):
        for step in (-distance, distance):
            onward = 1 if step < 0 else -1
            for colour in (0, 1):
                self.arrive(i, colour, (), step)
                self.send([step, onward], i, colour, (), step, 0 if step < 0 else self.l.Z, onward)

    def aside(self, i, distance):
        for step in (-distance, distance) if distance else (0,):
            for colour in (0, 1):
                near, far = self.l.sides(colour)
                self.send([step], i, colour, (), step, 2 * self.l.Z, near)
                self.send([step], i, colour, (), step, 3 * self.l.Z, far)

    def across(self, i, distance):
        for step in (-distance, distance) if distance else (0,):
            for colour in (0, 1):
                near, far = self.l.sides(colour)
                self.arrive(i, colour, (near,), step)
                self.send([step], i, colour, (near,), step, 4 * self.l.Z, far)

    def last(self, i):
        for colour in (0, 1):
            near, far = self.l.sides(colour)
            for step in [0] + offsets(self.l.Z):
                self.arrive(i, colour, (far,), step)
                self.arrive(i, colour, (far, near), step)

    def drain(self):
        for steps, what in self.sent:
            self.l.when(steps, lambda: self.copy(*what).wait_send())

    @staticmethod
    def semaphores(n, Z):
        return [
            pltpu.SemaphoreType.DMA((n, 2, 5 * Z)),
            pltpu.SemaphoreType.DMA((n, 2, 4 * Z)),
        ]


GROUP_HEADS = 2
PARTS = 4
class ForwardOuts(NamedTuple):
    vectors: Any
    w_qkv: Any
    w_out: Any
    w_inner: Any
    w_outer: Any
    cot_rows: Any
    x_rows: Any
    normed: Any
    qkv: Any
    far: Any
    mixed: Any
    logs: Any
    middle: Any
    normed_two: Any
    active: Any
    slope: Any


class ForwardScratch(NamedTuple):
    small_all: Any
    hidden_bias: Any
    x: Any
    norm_v: Any
    qkv_v: Any
    far_v: Any
    mix_v: Any
    wq_v: Any
    wo_v: Any
    wi_v: Any
    n2_v: Any
    mid_v: Any
    act_v: Any
    slo_v: Any
    cot_own: Any
    local: Any
    core_send: Any
    core_recv: Any
    row_sem: Any
    kv_send: Any
    kv_recv: Any
    mix_send: Any
    mix_recv: Any
    wo_sem: Any
    out_sem: Any
    load_sem: Any
    gather_send: Any
    gather_recv: Any


def norm_rows(values, gain, shift):
    xhat, _ = row_stats(values)
    return (xhat * gain + shift).astype(low)


def forward_kernel(Z, heads, tile, *refs):
    (frames, cot, wq, wk, wv, wo, wi, w2, small, tags_q, tags_k) = refs[:11]
    n_outs = len(ForwardOuts._fields)
    o = ForwardOuts(*refs[11 : 11 + n_outs])
    s = ForwardScratch(*refs[11 + n_outs :])
    l = Links(Z)
    core, K = l.core, 4 * Z
    here = l.at((), l.z)
    r, D = wq.shape
    hw = D // 2
    f = w2.shape[0]
    R = frames.shape[2]
    rows = 4 * R
    width = heads * HD
    tiles = rows // tile
    groups = heads // GROUP_HEADS
    span = GROUP_HEADS * HD
    factor = HD ** (-0.5) * math.log2(math.e)
    vectors = o.vectors

    def natural(place):
        y, x, z = place
        return (x * Z + z) * 2 + y

    def block(i, colour, place):
        k = l.index(place)
        rows80 = pl.ds(pl.multiple_of(k * 2 * r, 16), 2 * r)
        if i == 0:
            return s.small_all.at[k, colour]
        if i == 1:
            return o.w_qkv.at[rows80, pl.ds(colour * hw, hw)]
        if i == 2:
            if colour == 0:
                return o.w_qkv.at[rows80, pl.ds(2 * hw, hw)]
            return o.w_out.at[core, rows80, :]
        if i < 5:
            return o.w_inner.at[rows80, pl.ds(((i - 3) * 2 + colour) * hw, hw)]
        at = natural(place) * f + ((i - 5) * 2 + colour) * (f // 4)
        return o.w_outer.at[pl.ds(pl.multiple_of(at, 8), f // 4), :]

    gather = Gather(l, block, (s.gather_send, s.gather_recv))

    def my_rows():
        return pl.ds(pl.multiple_of(here * 2 * r + core * r, 8), r)

    sources = ((wq, hw), (wk, hw), (wv, hw), (wo, hw), (wi, 2 * D))

    def place_of(m, of_core):
        if m == 3:
            return o.w_out.at[of_core, my_rows(), :]
        if m == 4:
            return o.w_inner.at[my_rows(), :]
        return o.w_qkv.at[my_rows(), pl.ds(m * hw, hw)]

    def keep(m):
        if m == 5:
            return pltpu.make_async_copy(small, s.small_all.at[here, core], s.local.at[m])
        src, cols = sources[m]
        window = pl.ds(pl.multiple_of(core * cols, 128), cols)
        return pltpu.make_async_copy(src.at[:, window], place_of(m, core), s.local.at[m])

    def give(m):
        sems = s.core_send.at[m], s.core_recv.at[m]
        if m == 5:
            return remote(small, s.small_all.at[here, core], *sems, l.target("core"))
        src, cols = sources[m]
        window = pl.ds(pl.multiple_of((1 - core) * cols, 128), cols)
        return remote(src.at[:, window], place_of(m, 1 - core), *sems, l.target("core"))

    outer_rows = pl.ds(pl.multiple_of(((l.x * Z + l.z) * 2 + core) * f, 16), f)

    def outer_keep():
        return pltpu.make_async_copy(w2, o.w_outer.at[outer_rows, :], s.local.at[6])

    def outer_give():
        return remote(
            w2,
            o.w_outer.at[outer_rows, :],
            s.core_send.at[6],
            s.core_recv.at[6],
            l.target("diagonal"),
        )

    def begin(m):
        keep(m).start()
        give(m).start()

    def ready(m):
        keep(m).wait()
        give(m).wait_recv()

    def row_copies(source, target, base):
        m = l.half
        mine, theirs = m * 2 + core, (1 - m) * 2 + core
        swaps = []
        for p in range(PARTS):
            part = pl.ds(p * (R // PARTS), R // PARTS)
            swaps.append(
                remote(
                    source.at[1 - m, 0, part, :], target.at[mine, part, :],
                    s.row_sem.at[base, p], s.row_sem.at[base + 1, p], l.target("swap"),
                )
            )
        return (
            swaps,
            remote(
                source.at[m, 0], target.at[mine],
                s.row_sem.at[base, PARTS], s.row_sem.at[base + 1, PARTS], l.target("core"),
            ),
            remote(
                target.at[theirs], target.at[theirs],
                s.row_sem.at[base, PARTS + 1], s.row_sem.at[base + 1, PARTS + 1], l.target("core"),
            ),
        )

    frame_copies = lambda: row_copies(frames, s.x, 0)
    cot_copies = lambda: row_copies(cot, o.cot_rows, 2)
    frame_own = lambda: pltpu.make_async_copy(
        frames.at[l.half, 0], s.x.at[l.half * 2 + core], s.local.at[7]
    )
    cot_load = lambda: pltpu.make_async_copy(cot.at[l.half, 0], s.cot_own, s.local.at[8])
    cot_store = lambda: pltpu.make_async_copy(
        s.cot_own, o.cot_rows.at[l.half * 2 + core], s.local.at[8]
    )

    def kv_copy(g, which):
        at = which * width + g * span
        return remote(
            s.qkv_v.at[pl.ds(width + at, span)],
            s.far_v.at[pl.ds(at, span)],
            s.kv_send.at[g, which],
            s.kv_recv.at[g, which],
            l.target("pair"),
        )

    def mix_copy(g, of_core):
        at = pl.ds(pl.multiple_of(of_core * width + g * span, 16), span)
        return remote(
            s.mix_v.at[at],
            s.mix_v.at[at],
            s.mix_send.at[g],
            s.mix_recv.at[g],
            l.target("core"),
        )

    def wo_copy(of_core):
        return remote(
            o.w_out.at[of_core], o.w_out.at[of_core],
            s.wo_sem.at[0], s.wo_sem.at[1], l.target("core"),
        )

    def wide_load(which):
        return pltpu.make_async_copy(
            o.w_qkv.at[:, pl.ds(which * hw, hw)], s.wq_v.at[which], s.load_sem.at[which]
        )

    def wo_load():
        return pltpu.make_async_copy(o.w_out, s.wo_v, s.load_sem.at[3])

    inner_tile = 256

    def wi_load(c):
        cols = pl.ds(pl.multiple_of(c * inner_tile, inner_tile), inner_tile)
        slot = lax.rem(c, 2)
        return pltpu.make_async_copy(
            o.w_inner.at[:, cols], s.wi_v.at[slot], s.load_sem.at[4 + slot]
        )

    stores = (
        (s.x, o.x_rows), (s.norm_v, o.normed), (s.qkv_v, o.qkv), (s.far_v, o.far), (s.mix_v, o.mixed),
        (s.mid_v, o.middle), (s.n2_v, o.normed_two), (s.act_v, o.active), (s.slo_v, o.slope),
    )

    def store(i):
        return pltpu.make_async_copy(*stores[i], s.out_sem.at[i])

    big = rows // 2

    def big_rows(t):
        return pl.ds(pl.multiple_of(t * big, 128), big)

    def x_tile(t):
        return s.x[pl.ds(2 * t, 2)].reshape(big, D).astype(wide)

    def project(t, whiches):
        if 0 in whiches:
            s.norm_v[big_rows(t), :] = norm_rows(x_tile(t), vectors[4:5, :], vectors[5:6, :])
        source = s.norm_v[big_rows(t), :]
        mine = pl.ds(pl.multiple_of(core * hw, 128), hw)
        for which in whiches:
            part = dims(source, s.wq_v[which], 1, 0)
            if which == 0:
                part = part + vectors[0:1, mine]
            if which == 2:
                part = part + vectors[1:2, mine]
            s.qkv_v[pl.ds(which * hw, hw), big_rows(t)] = part.T.astype(low)

    def attend(index):
        head, part = index // tiles, lax.rem(index, tiles)
        row = head * HD
        columns = pl.ds(pl.multiple_of(part * tile, tile), tile)
        qkv, far = s.qkv_v, s.far_v

        def feature(base):
            return pl.ds(pl.multiple_of(base + row, 16), HD)

        query = jnp.concatenate([qkv[feature(0), columns], tags_q[:, columns]], axis=0)
        keys = (qkv[feature(width), :], far[feature(0), :])
        values = (qkv[feature(2 * width), :], far[feature(width), :])
        scores = [
            dims(jnp.concatenate([keys[b], tags_k[b]], axis=0), query, 0, 0) for b in (0, 1)
        ]
        top = jnp.maximum(*[jnp.max(v, axis=0, keepdims=True) for v in scores]) * factor
        total = jnp.zeros_like(top)
        sums = jnp.zeros((HD, tile), wide)
        for b in (0, 1):
            part_values = jnp.exp2(scores[b] * factor - top)
            total = total + jnp.sum(part_values, axis=0, keepdims=True)
            sums = sums + dims(values[b], part_values.astype(low), 1, 0)
        s.mix_v[feature(core * width), columns] = (sums / total).astype(low)
        o.logs[head, :, columns] = top + jnp.log2(total)

    def branch(t):
        parts = [dims(s.mix_v[:, big_rows(t)], s.wo_v[b], 0, 0) for b in (0, 1)]
        middle = x_tile(t) + (jnp.concatenate(parts, axis=1) + vectors[2:3, :])
        s.mid_v[big_rows(t), :] = middle
        s.n2_v[big_rows(t), :] = norm_rows(middle, vectors[6:7, :], vectors[7:8, :])

    column_tiles = 2 * D // inner_tile

    def inner(index):
        c, t = index // 2, lax.rem(index, 2)

        @pl.when(t == 0)
        def _():
            @pl.when(c + 1 < column_tiles)
            def _():
                wi_load(c + 1).start()

            wi_load(c).wait()

        cols = pl.ds(pl.multiple_of(c * inner_tile, inner_tile), inner_tile)
        bias_at = pl.ds(pl.multiple_of(core * 2 * D + c * inner_tile, inner_tile), inner_tile)
        value = dims(s.n2_v[big_rows(t), :], s.wi_v[lax.rem(c, 2)], 1, 0)
        active, slope = gelu_parts(value + s.hidden_bias[:, bias_at])
        s.act_v[big_rows(t), cols] = active.astype(low)
        s.slo_v[big_rows(t), cols] = slope

    def unpack():
        for k in range(K):
            for q in (0, 1):
                d = 2 * k + q
                vectors[:, d * r : (d + 1) * r] = s.small_all[k, q, 0:8, 0:r].astype(wide)
                per = f // r
                for j in range(per):
                    at = d * f + j * r
                    s.hidden_bias[:, at : at + r] = s.small_all[
                        k, q, 8 + j : 9 + j, 0:r
                    ].astype(wide)

    l.barrier("core", "swap", "diagonal")
    begin(5)
    begin(0)
    begin(1)
    _, own_f, _ = frame_copies()
    own_f.start()
    frame_own().start()
    for m in (2, 3, 4):
        begin(m)
    pl.when(l.crossed == 1)(lambda: outer_give().start())
    pl.when(l.crossed == 0)(lambda: outer_keep().start())
    cot_load().start()

    plan = {}

    def at(step, *runs):
        plan.setdefault(step, []).extend(runs)

    def own_outer():
        pl.when(l.crossed == 1)(lambda: outer_give().wait_recv())
        pl.when(l.crossed == 0)(lambda: outer_keep().wait())

    along = lambda i, d: functools.partial(gather.along, i, d)
    across = lambda i, d: functools.partial(gather.across, i, d)
    last = lambda i: functools.partial(gather.last, i)

    def rows_arrive():
        swaps, mine, pass_on = frame_copies()
        for swap in swaps:
            swap.wait_recv()
        pass_on.start()
        mine.wait_recv()
        pass_on.wait_recv()
        frame_own().wait()

    def kv_ready(g):
        for which in (0, 1):
            kv_copy(g, which).wait_recv()

    def cot_start():
        cot_load().wait()
        _, mine, _ = cot_copies()
        mine.start()
        cot_store().start()

    def cot_pass():
        swaps, _, pass_on = cot_copies()
        for swap in swaps:
            swap.wait_recv()
        pass_on.start()

    def after_v():
        wo_copy(1 - core).wait_recv()
        wo_load().start()

    def mix_ready():
        for g in range(groups):
            mix_copy(g, 1 - core).wait_recv()

    def kv_send(which, *gs):
        for g in gs:
            kv_copy(g, which).start()

    def swap_frames(*ps):
        for p in ps:
            frame_copies()[0][p].start()

    def swap_cot(*ps):
        for p in ps:
            cot_copies()[0][p].start()

    frames_go = lambda *ps: functools.partial(swap_frames, *ps)
    cot_go = lambda *ps: functools.partial(swap_cot, *ps)

    attends = heads * tiles
    v0, a0 = 2, 4
    b0 = a0 + attends
    i0 = b0 + 2
    end = i0 + 2 * column_tiles
    own = lambda i: functools.partial(gather.own, i)
    aside = lambda i, d: functools.partial(gather.aside, i, d)
    here_now = lambda *ms: (lambda: [ready(m) for m in ms])
    send_kv = lambda which, *gs: functools.partial(kv_send, which, *gs)

    at(0, here_now(5), own(0), aside(0, 0), here_now(0, 1), own(1), aside(1, 0))
    at(0, along(0, 1), aside(0, 1), here_now(2, 3), own(2), along(0, 2), aside(0, 2), along(0, 3), aside(0, 3))
    at(0, aside(2, 0), frames_go(0), across(0, 0), across(0, 1), across(0, 2), across(0, 3))
    at(0, along(1, 1), aside(1, 1), frames_go(1), along(1, 2), aside(1, 2), here_now(4), own(3), across(1, 0))
    at(0, frames_go(2), along(2, 1), aside(2, 1), along(1, 3), aside(1, 3), across(1, 1), frames_go(3))
    at(0, along(2, 2), aside(2, 2))
    at(0, own(4), across(1, 2), along(2, 3), aside(2, 3), across(1, 3), along(3, 1), last(0), unpack)
    at(0, aside(3, 0), across(2, 0), aside(3, 1), along(3, 2), rows_arrive, lambda: store(0).start())
    at(0, last(1), lambda: wide_load(0).start(), lambda: wide_load(1).start())
    at(0, lambda: wide_load(0).wait(), lambda: wide_load(1).wait())
    at(1, across(2, 1), along(4, 1), aside(3, 2), own_outer, own(5), along(3, 3))
    at(2, send_kv(0, 0), lambda: store(1).start(), across(2, 2), aside(3, 3), across(2, 3), aside(4, 0))
    at(2, along(4, 2), across(3, 0), own(6), send_kv(0, 1), aside(4, 1), across(3, 1), along(4, 3), last(2))
    at(2, lambda: wide_load(2).start(), lambda: wo_copy(core).start(), lambda: wide_load(2).wait())
    at(a0, send_kv(1, 0), lambda: store(2).start(), aside(4, 2))
    at(a0 + 1, across(3, 2), aside(4, 3), send_kv(1, 1))
    at(a0 + 3, along(5, 1), across(3, 3), send_kv(0, 2))
    at(a0 + 4, cot_start)
    at(a0 + 5, aside(5, 0), across(4, 0), along(5, 2), send_kv(1, 2))
    at(a0 + 7, aside(5, 1), across(4, 1))
    at(a0 + 9, along(6, 1), after_v, send_kv(0, 3))
    at(a0 + 11, aside(5, 2), across(4, 2), send_kv(1, 3))
    at(a0 + 13, along(5, 3), aside(5, 3), cot_go(0))
    at(a0 + 15, across(4, 3))
    at(a0 + 17, along(6, 2), aside(6, 0), cot_go(1))
    at(a0 + 19, across(5, 0), aside(6, 1))
    at(a0 + 20, across(5, 1), cot_go(2))
    at(a0 + 21, along(6, 3), aside(6, 2))
    at(a0 + 22, cot_go(3))
    at(a0 + 23, across(5, 2))
    at(i0 + 2, cot_pass)
    for g in range(groups):
        at(a0 + g * GROUP_HEADS * tiles, functools.partial(kv_ready, g))
        at(a0 + (g + 1) * GROUP_HEADS * tiles, lambda g=g: mix_copy(g, core).start())
    at(b0, aside(6, 3), across(5, 3), lambda: store(3).start())
    at(b0, lambda: wo_load().wait(), mix_ready, lambda: store(4).start())
    at(b0 + 1, across(6, 0))
    at(i0, across(6, 1), lambda: store(5).start(), lambda: store(6).start(), last(3))
    at(i0, lambda: wi_load(0).start())
    at(i0 + 3, across(6, 2))
    at(i0 + 7, across(6, 3))
    at(i0 + 8, last(4))

    def one(step, carry):
        for when in sorted(plan):

            def run():
                for tick in plan[when]:
                    tick()

            pl.when(step == when)(run)
        inside = lambda lo, n: jnp.logical_and(step >= lo, step < lo + n)
        pl.when(step < v0)(lambda: project(step, (0, 1)))
        pl.when(inside(v0, 2))(lambda: project(step - v0, (2,)))
        pl.when(inside(a0, attends))(lambda: attend(step - a0))
        pl.when(inside(b0, 2))(lambda: branch(step - b0))
        pl.when(inside(i0, 2 * column_tiles))(lambda: inner(step - i0))
        return carry

    lax.fori_loop(0, end, one, 0)
    store(7).start()
    store(8).start()
    gather.last(5)
    gather.last(6)
    gather.drain()
    for m in range(6):
        give(m).wait_send()
    pl.when(l.crossed == 1)(lambda: outer_give().wait_send())
    for swaps, mine, pass_on in (frame_copies(), cot_copies()):
        for copy in swaps + [mine, pass_on]:
            copy.wait_send()
    _, mine, pass_on = cot_copies()
    mine.wait_recv()
    pass_on.wait_recv()
    cot_store().wait()
    wo_copy(core).wait_send()
    for g in range(groups):
        mix_copy(g, core).wait_send()
        for which in (0, 1):
            kv_copy(g, which).wait_send()
    for i in range(len(stores)):
        store(i).wait()


def forward_linked(frames, cot, weights, small, tags_q, tags_k, Z, heads, tile):
    K = 4 * Z
    r, D = weights[0].shape
    FF2 = weights[4].shape[1] // 2
    R = frames.shape[2]
    rows = 4 * R
    hw = D // 2
    groups = heads // GROUP_HEADS
    shape = jax.ShapeDtypeStruct
    outs = ForwardOuts(
        vectors=shape((8, D), wide),
        w_qkv=shape((D, 3 * hw), low),
        w_out=shape((2, D, hw), low),
        w_inner=shape((D, FF2), low),
        w_outer=shape((FF2, D), low),
        cot_rows=shape((4, R, D), low),
        x_rows=shape((4, R, D), low),
        normed=shape((rows, D), low),
        qkv=shape((3 * hw, rows), low),
        far=shape((2 * hw, rows), low),
        mixed=shape((D, rows), low),
        logs=shape((heads, 1, rows), wide),
        middle=shape((rows, D), wide),
        normed_two=shape((rows, D), low),
        active=shape((rows, FF2), low),
        slope=shape((rows, FF2), wide),
    )
    dma = pltpu.SemaphoreType.DMA
    scratch = [
        pltpu.VMEM((K, 2) + small.shape, low),
        pltpu.VMEM((1, 2 * FF2), wide),
        pltpu.VMEM((4, R, D), low),
        pltpu.VMEM((rows, D), low),
        pltpu.VMEM((3 * hw, rows), low),
        pltpu.VMEM((2 * hw, rows), low),
        pltpu.VMEM((D, rows), low),
        pltpu.VMEM((3, D, hw), low),
        pltpu.VMEM((2, D, hw), low),
        pltpu.VMEM((2, D, 256), low),
        pltpu.VMEM((rows, D), low),
        pltpu.VMEM((rows, D), wide),
        pltpu.VMEM((rows, FF2), low),
        pltpu.VMEM((rows, FF2), wide),
        pltpu.VMEM((R, D), low),
        dma((9,)),
        dma((7,)),
        dma((7,)),
        dma((4, PARTS + 2)),
        dma((groups, 2)),
        dma((groups, 2)),
        dma((groups,)),
        dma((groups,)),
        dma((2,)),
        dma((9,)),
        dma((6,)),
    ]
    spaces = [pltpu.VMEM if v in (outs.vectors, outs.logs) else pl.ANY for v in outs]
    results = pl.pallas_call(
        functools.partial(forward_kernel, Z, heads, tile),
        out_shape=tuple(outs),
        in_specs=full(2, pl.ANY) + full(9),
        out_specs=tuple(pl.BlockSpec(memory_space=space) for space in spaces),
        scratch_shapes=scratch + Gather.semaphores(7, Z),
        compiler_params=pltpu.CompilerParams(
            collective_id=0, has_side_effects=True, vmem_limit_bytes=BIG
        ),
    )(frames, cot, *weights, small, tags_q, tags_k)
    return ForwardOuts(*results)


SETS = 3


class Scatter:
    def __init__(self, links, i, block, out, buffers, sems, credit):
        self.l, self.i, self.block, self.out = links, i, block, out
        self.held, self.from_far, self.from_near, self.from_line = buffers
        self.load_sem, self.send_sem, self.recv_sem = sems
        self.credit = credit
        self.sent = []

    def load(self, colour, side, step):
        l = self.l
        near, far = l.sides(colour)
        z = l.z + step
        return pltpu.make_async_copy(
            self.block(self.i, colour, l.coords((near,) if side else (), z)),
            self.held.at[colour, side, z],
            self.load_sem.at[self.i, colour, side * l.Z + z],
        )

    def remote(self, colour, kind, step, to):
        l, Z = self.l, self.l.Z
        near, far = l.sides(colour)
        z = l.z + step
        if kind < 2:
            src = self.block(self.i, colour, l.coords((near, far) if kind else (far,), z))
            dst = self.from_far.at[colour, kind, z]
        elif kind == 2:
            src, dst = self.held.at[colour, 1, z], self.from_near.at[colour, z]
        else:
            src, dst = self.held.at[colour, 0, z], self.from_line.at[colour, kind - 3, z]
        return remote(
            src,
            dst,
            self.send_sem.at[self.i, colour, min(kind, 3) * Z + z],
            self.recv_sem.at[self.i, colour, kind * Z + z],
            l.target(to),
        )

    def arrive(self, colour, kind, step):
        self.remote(colour, kind, step, "cx").wait_recv()

    def send(self, step, *what):
        self.remote(*what).start()
        self.sent.append((step, what))

    def both(self, distance, run):
        for step in (-distance, distance) if distance else (0,):
            for colour in (0, 1):
                self.l.when([step], functools.partial(run, step, colour))

    def start(self):
        def run(step, colour):
            near, far = self.l.sides(colour)
            self.send(step, colour, 1, step, far)
            self.load(colour, 1, step).start()

        for distance in range(self.l.Z - 1, -1, -1):
            self.both(distance, run)

    def total(self, target, parts):
        rows, cols = target.shape
        pieces = 5 if cols % 640 == 0 else 1
        wide_cols = cols // pieces

        def one(p, carry):
            window = pl.ds(pl.multiple_of(p * wide_cols, 128), wide_cols)
            value = parts[0][:, window].astype(wide)
            for part in parts[1:]:
                value = value + part[:, window].astype(wide)
            target[:, window] = value.astype(target.dtype)
            return carry

        lax.fori_loop(0, pieces, one, 0)

    def near(self, distance):
        def run(step, colour):
            near, far = self.l.sides(colour)
            z = self.l.z + step
            self.load(colour, 1, step).wait()
            self.arrive(colour, 1, step)
            mine = self.held.at[colour, 1, z]
            self.total(mine, [mine, self.from_far.at[colour, 1, z]])
            self.send(step, colour, 2, step, near)

        def rest(step, colour):
            near, far = self.l.sides(colour)
            self.send(step, colour, 0, step, far)
            self.load(colour, 0, step).start()

        self.both(distance, run)
        self.both(distance, rest)

    def parts(self, colour, step):
        z = self.l.z + step
        self.load(colour, 0, step).wait()
        self.arrive(colour, 0, step)
        self.arrive(colour, 2, step)
        return [
            self.held.at[colour, 0, z],
            self.from_far.at[colour, 0, z],
            self.from_near.at[colour, z],
        ]

    def line(self, distance):
        l = self.l

        def run(step, colour):
            toward, kind = (1, 3) if step > 0 else (-1, 4)
            z = l.z + step
            behind = l.has(-toward)
            parts = self.parts(colour, step)
            mine = self.held.at[colour, 0, z]

            @pl.when(behind)
            def _():
                self.arrive(colour, kind, step)
                self.total(mine, parts + [self.from_line.at[colour, kind - 3, z]])

            @pl.when(jnp.logical_not(behind))
            def _():
                self.total(mine, parts)

            self.send(step, colour, kind, step, toward)

        self.both(distance, run)

    def finish(self):
        l = self.l
        for colour in (0, 1):
            z = l.z
            parts = self.parts(colour, 0)
            left, right = self.from_line.at[colour, 0, z], self.from_line.at[colour, 1, z]
            target = self.out.at[colour]
            l.when([-1], lambda: self.arrive(colour, 3, 0))
            l.when([1], lambda: self.arrive(colour, 4, 0))
            l.when([-1, 1], lambda: self.total(target, parts + [left, right]))
            pl.when(jnp.logical_not(l.has(-1)))(lambda: self.total(target, parts + [right]))
            pl.when(jnp.logical_not(l.has(1)))(lambda: self.total(target, parts + [left]))

    def free(self):
        for to in ("cy", "cx", -1, 1):

            def tell():
                pl.semaphore_signal(
                    self.credit.at[self.i], inc=1, device_id=self.l.target(to), device_id_type=MESH
                )

            self.l.when([] if to in ("cy", "cx") else [to], tell)

    def freed(self):
        ends = jnp.minimum(self.l.z, 1) + jnp.minimum(self.l.Z - 1 - self.l.z, 1)
        pl.semaphore_wait(self.credit.at[self.i], 2 + ends)
        self.drain()

    def drain(self):
        for step, what in self.sent:
            self.l.when([step], lambda: self.remote(*what).wait_send())
        self.sent = []

    @staticmethod
    def ticks(works, shared, settle):
        far_first = lambda w, run: [functools.partial(run(w), d) for d in range(w.l.Z - 1, -1, -1)]
        out = [(0, works[0].start)]
        for i, work in enumerate(works):
            out += [(i, t) for t in far_first(work, lambda w: w.near)]
            if i + 1 < len(works):
                if SETS <= i + 1 < shared:
                    out.append((i, works[i + 1 - SETS].freed))
                out.append((i + 1, works[i + 1].start))
            out += [(i, t) for t in far_first(work, lambda w: w.line)[:-1]]
            if i:
                out.append((i - 1, works[i - 1].finish))
                out.append((i - 1, functools.partial(settle, i - 1)))
                if i - 1 + SETS < shared:
                    out.append((i - 1, works[i - 1].free))
        out.append((len(works) - 1, works[-1].finish))
        out.append((len(works) - 1, functools.partial(settle, len(works) - 1)))
        return out


class BackwardOuts(NamedTuple):
    query: Any
    key: Any
    value: Any
    output: Any
    inner: Any
    outer: Any
    small: Any
    frames_grad: Any
    layer_out: Any
    qkv_blocks: Any
    out_blocks: Any


class BackwardScratch(NamedTuple):
    dqkv: Any
    own: Any
    away: Any
    got: Any
    acc_k: Any
    acc_v: Any
    norm_v: Any
    wt: Any
    stage: Any
    stage_o: Any
    part: Any
    part_got: Any
    x_own: Any
    mg_own: Any
    home_out: Any
    home_in: Any
    vec: Any
    small_g: Any
    done: Any
    done_small: Any
    got_small: Any
    done_local: Any
    done_send: Any
    done_recv: Any
    layer_sem: Any
    home_sem: Any
    back_send: Any
    back_recv: Any
    pair_sem: Any
    load: Any
    wt_sem: Any
    stage_sem: Any
    credit: Any
    load_sem: Any
    send_sem: Any
    recv_sem: Any


RATE = 1.2


def backward_kernel(Z, heads, tile, *refs):
    (
        qkv, far, tags_q, tags_k, mixed, logs, grad_in, bg, vectors, small_part, hidden_sums,
        x_rows, middle_grad, normed, w_qkv, g_outer, g_inner, layer_rows,
    ) = refs[:18]
    n_outs, n_scratch = len(BackwardOuts._fields), len(BackwardScratch._fields)
    o = BackwardOuts(*refs[18 : 18 + n_outs])
    s = BackwardScratch(*refs[18 + n_outs : 18 + n_outs + n_scratch])
    buffers = refs[18 + n_outs + n_scratch :]
    l = Links(Z)
    core, K = l.core, 4 * Z
    width = heads * HD
    rows = qkv.shape[1]
    R = rows // 4
    D = bg.shape[1]
    hw = D // 2
    r2 = D // K
    r = r2 // 2
    f = g_outer.shape[0] // K
    tiles = rows // tile
    groups = heads // GROUP_HEADS
    span = GROUP_HEADS * HD
    scale = HD ** (-0.5)
    factor = scale * math.log2(math.e)

    def block(i, colour, place):
        y, x, z = place
        at = pl.ds(pl.multiple_of(l.index(place) * r2, 16), r2)
        if i < 2:
            first = ((x * Z + z) * 2 + y) * f + colour * (f // 2)
            return g_outer.at[pl.ds(pl.multiple_of(first, 16), f // 2), pl.ds(i * hw, hw)]
        if i < 4:
            return g_inner.at[at, pl.ds(((i - 2) * 2 + colour) * hw, hw)]
        if i == 4:
            return o.qkv_blocks.at[at, pl.ds(colour * hw, hw)]
        if i == 5:
            if colour == 0:
                return o.qkv_blocks.at[at, pl.ds(2 * hw, hw)]
            return o.out_blocks.at[at, :]
        return s.small_g.at[l.index(place), colour]

    outs = [s.done.at[i] for i in range(6)] + [s.done_small]
    works = [
        Scatter(
            l, i, block, outs[i],
            buffers[4 * (SETS if i == 6 else i % SETS) :][:4],
            (s.load_sem, s.send_sem, s.recv_sem), s.credit,
        )
        for i in range(7)
    ]

    finals = ((o.query, o.key), (o.value, o.output))

    def final_place(i, colour, of_core):
        if i < 2:
            return o.outer.at[pl.ds(colour * (f // 2), f // 2), pl.ds(i * hw, hw)]
        if i < 4:
            first = of_core * 2 * D + ((i - 2) * 2 + colour) * hw
            return o.inner.at[:, pl.ds(pl.multiple_of(first, 128), hw)]
        return finals[i - 4][colour].at[:, pl.ds(pl.multiple_of(of_core * hw, 128), hw)]

    def final_rows(i, colour, which):
        if i < 2:
            return s.done.at[i, colour]
        return s.done.at[i, colour, pl.ds(pl.multiple_of(which * r, 8), r), :]

    def final_keep(i, colour):
        return pltpu.make_async_copy(
            final_rows(i, colour, core), final_place(i, colour, core), s.done_local.at[i, colour]
        )

    def final_give(i, colour):
        return remote(
            final_rows(i, colour, 1 - core), final_place(i, colour, core),
            s.done_send.at[i, colour], s.done_recv.at[i, colour],
            l.target("diagonal" if i < 2 else "core"),
        )

    small_give = lambda: remote(
        s.done_small.at[1 - core], s.got_small,
        s.done_send.at[6, 0], s.done_recv.at[6, 0], l.target("core"),
    )

    def settle(i):
        if i == 6:
            small_give().start()
            return
        for colour in (0, 1):
            keep = lambda: final_keep(i, colour).start()
            give = lambda: final_give(i, colour).start()
            if i < 2:
                pl.when(l.crossed == 0)(keep)
                pl.when(l.crossed == 1)(give)
            else:
                keep()
                give()

    def settled():
        for i in range(6):
            for colour in (0, 1):
                keep = lambda: final_keep(i, colour).wait()

                def give():
                    final_give(i, colour).wait_send()
                    final_give(i, colour).wait_recv()

                if i < 2:
                    pl.when(l.crossed == 0)(keep)
                    pl.when(l.crossed == 1)(give)
                else:
                    keep()
                    give()
        small_give().wait_recv()
        o.small[...] = s.done_small[core] + s.got_small[...]
        small_give().wait_send()

    def layer_swap(p):
        part = pl.ds(p * (R // PARTS), R // PARTS)
        return remote(
            layer_rows.at[1 - l.half, part, :], o.layer_out.at[l.half, 0, part, :],
            s.home_sem.at[2, p], s.home_sem.at[3, p], l.target("swap"),
        )

    layer_load = lambda: pltpu.make_async_copy(
        layer_rows.at[l.half], s.home_out, s.layer_sem.at[2]
    )
    layer_store = lambda: pltpu.make_async_copy(
        s.home_out, o.layer_out.at[l.half, 0], s.layer_sem.at[2]
    )

    def back_copy(g, which):
        at = pl.ds(which * width + g * span, span)
        return remote(
            s.away.at[at], s.got.at[at],
            s.back_send.at[g, which], s.back_recv.at[g, which], l.target("pair"),
        )

    def send_back(g, which):
        back_copy(g, which).start()

    def add_back(g):
        for which in (0, 1):
            back_copy(g, which).wait_recv()
            for h in range(GROUP_HEADS):
                at = which * width + g * span + h * HD
                s.dqkv[pl.ds(width + at, HD), :] = (
                    s.own[pl.ds(at, HD), :] + s.got[pl.ds(at, HD), :].astype(wide)
                ).astype(low)

    def row_load(h, which):
        source, target = ((x_rows, s.x_own), (middle_grad, s.mg_own))[which]
        return pltpu.make_async_copy(
            source.at[h * 2 + core], target.at[h], s.load.at[h * 2 + which]
        )

    norm_load = lambda: pltpu.make_async_copy(normed, s.norm_v, s.load.at[4])

    def wt_load(c):
        at = pl.ds(pl.multiple_of(c * 256, 256), 256)
        slot = lax.rem(c, 2)
        return pltpu.make_async_copy(w_qkv.at[at, :], s.wt.at[slot], s.wt_sem.at[slot])

    def stage_copy(c, which):
        at = pl.ds(pl.multiple_of(c * 256, 256), 256)
        slot = lax.rem(c, 2)
        source, target = ((s.stage, o.qkv_blocks), (s.stage_o, o.out_blocks))[which]
        return pltpu.make_async_copy(
            source.at[slot], target.at[at, :], s.stage_sem.at[which, slot]
        )

    def part_copy(h):
        return remote(
            s.part.at[h, 1 - core], s.part_got.at[h],
            s.pair_sem.at[h], s.pair_sem.at[2 + h], l.target("core"),
        )

    def home_copy(p):
        part = pl.ds(p * (R // PARTS), R // PARTS)
        return remote(
            s.home_out.at[part, :], s.home_in.at[part, :],
            s.home_sem.at[0, p], s.home_sem.at[1, p], l.target("swap"),
        )

    def home_store(h):
        return pltpu.make_async_copy(s.mg_own.at[h], o.frames_grad.at[h, 0], s.load.at[h])

    def attend(index):
        head, part = index // tiles, lax.rem(index, tiles)
        row = head * HD
        columns = pl.ds(pl.multiple_of(part * tile, tile), tile)

        def feature(base):
            return pl.ds(pl.multiple_of(base + row, 16), HD)

        head_query = qkv[feature(0), columns]
        grad = grad_in[feature(0), columns]
        query = jnp.concatenate([head_query, tags_q[:, columns]], axis=0)
        attended = mixed[feature(core * width), columns]
        delta = jnp.sum(grad.astype(wide) * attended.astype(wide), axis=0, keepdims=True)
        log_row = logs[head, :, columns]
        query_rows = head_query.T
        grad_rows = grad.T
        dq = jnp.zeros((HD, tile), wide)

        @pl.when(part == 0)
        def _():
            s.acc_k[...] = jnp.zeros_like(s.acc_k)
            s.acc_v[...] = jnp.zeros_like(s.acc_v)

        keys = (qkv[feature(width), :], far[feature(0), :])
        values = (qkv[feature(2 * width), :], far[feature(width), :])
        for b in (0, 1):
            key = jnp.concatenate([keys[b], tags_k[b]], axis=0)
            probs = jnp.exp2(dims(key, query, 0, 0) * factor - log_row)
            grad_probs = dims(values[b], grad, 0, 0)
            score_grad = (probs * (grad_probs - delta)).astype(low)
            s.acc_v[b] += dims(probs.astype(low), grad_rows, 1, 0)
            s.acc_k[b] += dims(score_grad, query_rows, 1, 0)
            dq = dq + dims(keys[b], score_grad, 1, 0)
        s.dqkv[feature(0), columns] = (dq * scale).astype(low)

        @pl.when(part == tiles - 1)
        def _():
            s.own[feature(0), :] = s.acc_k[0].T * scale
            s.own[feature(width), :] = s.acc_v[0].T
            s.away[feature(0), :] = (s.acc_k[1].T * scale).astype(low)
            s.away[feature(width), :] = s.acc_v[1].T.astype(low)

    own_cols = pl.ds(pl.multiple_of(core * hw, 128), hw)

    def staged(c, which, value):
        @pl.when(c >= 2)
        def _():
            stage_copy(c - 2, which).wait()

        (s.stage, s.stage_o)[which][lax.rem(c, 2)] = value.astype(low)
        stage_copy(c, which).start()

    def out_grad(c):
        at = pl.ds(pl.multiple_of(c * 256, 256), 256)
        staged(c, 1, dims(mixed[at, :], bg[:, own_cols], 1, 0))

    def qkv_grad(c):
        at = pl.ds(pl.multiple_of(c * 256, 256), 256)
        staged(c, 0, dims(s.norm_v[:, at], s.dqkv[...], 0, 1))

    row_tiles = D // 256

    def norm_grad(index):
        c, h = index // 2, lax.rem(index, 2)

        @pl.when(h == 0)
        def _():
            @pl.when(c + 1 < row_tiles)
            def _():
                wt_load(c + 1).start()

            wt_load(c).wait()

        columns = pl.ds(pl.multiple_of(h * 2 * R, 128), 2 * R)
        value = dims(s.wt[lax.rem(c, 2)], s.dqkv[:, columns], 1, 0).T
        at = pl.ds(pl.multiple_of(c * 256, 256), 256)
        s.part[h, 0, :, at] = value[:R]
        s.part[h, 1, :, at] = value[R:]

    def frame_grad(h):
        grad = s.part[h, core] + s.part_got[h]
        xhat, inverse = row_stats(s.x_own[h].astype(wide))
        s.mg_own[h] = s.mg_own[h] + norm_pull(grad, vectors[4:5, :], xhat, inverse)
        s.vec[4:5, :] += jnp.sum(grad * xhat, axis=0, keepdims=True)
        s.vec[5:6, :] += jnp.sum(grad, axis=0, keepdims=True)

    def bias_sums():
        s.vec[...] = small_part[...]
        ones = jnp.ones((8, rows), low)
        s.vec[0:1, own_cols] = dims(ones, s.dqkv[pl.ds(0, hw), :], 1, 1)[0:1]
        s.vec[1:2, own_cols] = dims(ones, s.dqkv[pl.ds(2 * hw, hw), :], 1, 1)[0:1]

    def rows_home():
        layer_store().wait()
        s.home_out[...] = s.mg_own[1 - l.half].astype(low)
        for p in range(PARTS):
            home_copy(p).start()
        home_store(l.half).start()

    def pack():
        s.small_g[...] = jnp.zeros_like(s.small_g)
        for k in range(K):
            for q in (0, 1):
                d = 2 * k + q
                s.small_g[k, q, 0:8, 0:r] = s.vec[:, d * r : (d + 1) * r].astype(low)
                for j in range(f // r):
                    at = d * f + j * r
                    s.small_g[k, q, 8 + j : 9 + j, 0:r] = hidden_sums[:, at : at + r].astype(low)

    l.barrier("core", "swap", "diagonal")
    layer_load().start()
    for h in (0, 1):
        for which in (0, 1):
            row_load(h, which).start()
    norm_load().start()
    wt_load(0).start()
    attends = heads * tiles
    work = []
    for step in range(attends):
        work.append(None)
        if step % 3 == 2 and step >= GROUP_HEADS * tiles - 1:
            half_group = step // 3 - 1
            work.append(functools.partial(send_back, half_group // 2, half_group % 2))
    work += [functools.partial(send_back, groups - 1, 1)] + [None] * row_tiles
    work += [functools.partial(add_back, g) for g in range(groups)] + [bias_sums]
    work += [lambda: norm_load().wait()] + [None] * row_tiles

    def staged_out():
        for which in (0, 1):
            for c in (row_tiles - 2, row_tiles - 1):
                stage_copy(c, which).wait()

    work.append(staged_out)
    qkv_ready = len(work)
    work += [None] * (2 * row_tiles)

    def exchange_parts():
        for h in (0, 1):
            part_copy(h).start()
        for h in (0, 1):
            for which in (0, 1):
                row_load(h, which).wait()
        for h in (0, 1):
            part_copy(h).wait_recv()

    work.append(exchange_parts)
    work += [None] * 2 + [rows_home, pack]

    def layer_begin():
        layer_load().wait()
        layer_store().start()

    work[8:8] = [layer_begin]
    for p in range(PARTS):
        place = 12 + 6 * p
        work[place:place] = [lambda p=p: layer_swap(p).start()]
    qkv_ready += 1 + PARTS

    ticks = Scatter.ticks(works, 6, settle)
    plan, now, done = {}, 0, 0
    starts = 0
    for j, (i, tick) in enumerate(ticks):
        need = int(j * RATE)
        if tick == works[4].start:
            need = max(need, qkv_ready)
        if tick == works[6].start:
            need = len(work)
        while done < min(need, len(work)):
            if work[done] is None:
                now += 1
            else:
                plan.setdefault(now, []).append(work[done])
            done += 1
        plan.setdefault(now, []).append(tick)
    end = len([w for w in work if w is None])

    o0 = attends
    q0 = o0 + row_tiles
    d0 = q0 + row_tiles
    e0 = d0 + 2 * row_tiles

    def one(step, carry):
        for when in sorted(plan):
            if when < end:

                def run():
                    for tick in plan[when]:
                        tick()

                pl.when(step == when)(run)
        inside = lambda lo, n: jnp.logical_and(step >= lo, step < lo + n)
        pl.when(step < o0)(lambda: attend(step))
        pl.when(inside(o0, row_tiles))(lambda: out_grad(step - o0))
        pl.when(inside(q0, row_tiles))(lambda: qkv_grad(step - q0))
        pl.when(inside(d0, 2 * row_tiles))(lambda: norm_grad(step - d0))
        pl.when(inside(e0, 2))(lambda: frame_grad(step - e0))
        return carry

    lax.fori_loop(0, end, one, 0)
    for tick in plan.get(end, []):
        tick()
    for p in range(PARTS):
        home_copy(p).wait_recv()
    home_store(l.half).wait()
    s.mg_own[1 - l.half] = s.home_in[...].astype(wide)
    home_store(1 - l.half).start()
    for w in works:
        w.drain()
    for g in range(groups):
        for which in (0, 1):
            back_copy(g, which).wait_send()
    for h in (0, 1):
        part_copy(h).wait_send()
    for p in range(PARTS):
        home_copy(p).wait_send()
    home_store(1 - l.half).wait()
    for p in range(PARTS):
        layer_swap(p).wait_recv()
        layer_swap(p).wait_send()
    settled()


def backward_linked(resident, streamed, Z, heads, tile):
    K = 4 * Z
    qkv_t = resident[0]
    rows = qkv_t.shape[1]
    R = rows // 4
    D = resident[7].shape[1]
    hw = D // 2
    r2 = D // K
    groups = heads // GROUP_HEADS
    shape = jax.ShapeDtypeStruct
    dma = pltpu.SemaphoreType.DMA
    outs = BackwardOuts(
        query=shape((r2 // 2, D), wide),
        key=shape((r2 // 2, D), wide),
        value=shape((r2 // 2, D), wide),
        output=shape((r2 // 2, D), wide),
        inner=shape((r2 // 2, 4 * D), wide),
        outer=shape((2 * r2, D), wide),
        small=shape((16, 128), wide),
        frames_grad=shape((2, 1, R, D), wide),
        layer_out=shape((2, 1, R, D), low),
        qkv_blocks=shape((D, 3 * hw), low),
        out_blocks=shape((D, hw), low),
    )
    scratch = [
        pltpu.VMEM((3 * hw, rows), low),
        pltpu.VMEM((2 * hw, rows), wide),
        pltpu.VMEM((2 * hw, rows), low),
        pltpu.VMEM((2 * hw, rows), low),
        pltpu.VMEM((2, rows, HD), wide),
        pltpu.VMEM((2, rows, HD), wide),
        pltpu.VMEM((rows, D), low),
        pltpu.VMEM((2, 256, 3 * hw), low),
        pltpu.VMEM((2, 256, 3 * hw), low),
        pltpu.VMEM((2, 256, hw), low),
        pltpu.VMEM((2, 2, R, D), wide),
        pltpu.VMEM((2, R, D), wide),
        pltpu.VMEM((2, R, D), low),
        pltpu.VMEM((2, R, D), wide),
        pltpu.VMEM((R, D), low),
        pltpu.VMEM((R, D), low),
        pltpu.VMEM((8, D), wide),
        pltpu.VMEM((K, 2, 16, 128), low),
        pltpu.VMEM((6, 2, r2, hw), wide),
        pltpu.VMEM((2, 16, 128), wide),
        pltpu.VMEM((16, 128), wide),
        dma((6, 2)),
        dma((7, 2)),
        dma((7, 2)),
        dma((3,)),
        dma((4, PARTS)),
        dma((groups, 2)),
        dma((groups, 2)),
        dma((6,)),
        dma((5,)),
        dma((2,)),
        dma((2, 2)),
        pltpu.SemaphoreType.REGULAR((SETS,)),
        dma((7, 2, 2 * Z)),
        dma((7, 2, 4 * Z)),
        dma((7, 2, 5 * Z)),
    ]
    for block in ((r2, hw),) * SETS + ((16, 128),):
        scratch += [pltpu.VMEM((2,) + lead + block, low) for lead in ((2, Z), (2, Z), (Z,), (2, Z))]
    results = pl.pallas_call(
        functools.partial(backward_kernel, Z, heads, tile),
        out_shape=tuple(outs),
        in_specs=full(len(resident)) + full(len(streamed), pl.ANY),
        out_specs=tuple(full(6, pl.ANY) + full(1) + full(4, pl.ANY)),
        scratch_shapes=scratch,
        compiler_params=pltpu.CompilerParams(
            collective_id=1, has_side_effects=True, vmem_limit_bytes=67043328
        ),
    )(*resident, *streamed)
    return BackwardOuts(*results)


def general_body(
    n_chip_rows,
    Z,
    frames,
    clip_ids,
    query_weight,
    key_weight,
    value_weight,
    output_weight,
    inner_weight,
    outer_weight,
    query_bias,
    value_bias,
    output_bias,
    inner_bias,
    outer_bias,
    first_gain,
    first_shift,
    second_gain,
    second_shift,
    out_cotangent,
):
    K = n_chip_rows * Z
    R, D = frames.shape[2], frames.shape[3]
    FF = inner_weight.shape[1]
    r = query_weight.shape[0]
    f = outer_weight.shape[0]
    hw = D // 2
    heads = H // 2
    half = Z // 2
    core = lax.axis_index("core")
    first_core = core == 0
    zz = lax.axis_index("zz")
    micro = zz // half
    first_half = micro == 0
    place = zz % half

    def swap_core(v):
        return lax.ppermute(v, "core", [(0, 1), (1, 0)])

    def swap_half(v):
        return lax.ppermute(v, "zz", [(z, (z + half) % Z) for z in range(Z)])

    def by_core(own, other, axis):
        return jnp.where(
            first_core,
            jnp.concatenate([own, other], axis),
            jnp.concatenate([other, own], axis),
        )

    def pick(v, index, axis):
        return lax.dynamic_index_in_dim(v, index, axis, keepdims=False)

    def take_rows(v):
        v = v[:, 0]
        own, away = pick(v, micro, 0), pick(v, 1 - micro, 0)
        got = swap_half(away)
        pair = jnp.where(first_half, jnp.stack([own, got]), jnp.stack([got, own]))
        both = by_core(pair[:, None], swap_core(pair)[:, None], 1)
        return both.reshape(4 * R, D)

    qkv = jnp.stack([query_weight, key_weight, value_weight], 1).reshape(r, 3, 2, hw)
    inner_split = inner_weight.reshape(r, K, 2, f)
    vectors = (
        query_bias, value_bias, output_bias, outer_bias,
        first_gain, first_shift, second_gain, second_shift, inner_bias,
    )
    small = jnp.concatenate(vectors)
    n_small = small.shape[0]

    def column_half(which):
        return jnp.concatenate(
            [
                pick(qkv, which, 2).reshape(r, 3 * hw),
                pick(inner_split, which, 2).reshape(r, FF // 2),
            ],
            1,
        )

    mine = column_half(core)
    theirs = swap_core(column_half(1 - core))
    both = by_core(mine[None], theirs[None], 0)
    small_both = by_core(small[None], swap_core(small)[None], 0)
    small_pad = -(-n_small // 1024) * 1024
    small_both = jnp.pad(small_both, ((0, 0), (0, small_pad - n_small)))
    shards = (
        small_both.reshape(2, small_pad // 128, 128),
        both[:, :, : 3 * hw],
        output_weight.reshape(r, 2, hw).transpose(1, 0, 2),
        both[:, :, 3 * hw :],
        outer_weight.reshape(2, f // 2, D),
    )
    small_all, qkv_all, out_all, inner_all, outer_all = (
        lax.all_gather(v, CHIPS, axis=0, tiled=False) for v in shards
    )
    x_rows = take_rows(frames)
    cot = take_rows(out_cotangent)

    w_qkv = qkv_all.reshape(D, 3 * hw)
    w_inner = inner_all.reshape(D, FF // 2)
    w_outer = outer_all.reshape(FF // 2, D)
    out_own = out_all.transpose(0, 2, 1, 3).reshape(K, 1, r, D)
    w_out = by_core(out_own, swap_core(out_own), 1).reshape(D, D)
    small_all = small_all.reshape(K, 2, small_pad)[:, :, :n_small].astype(wide)
    names = ("qb", "vb", "ob", "ub", "g1", "s1", "g2", "s2")
    vec = {n: small_all[:, :, i * r : (i + 1) * r].reshape(D) for i, n in enumerate(names)}
    ib_half = pick(small_all[:, :, 8 * r :], core, 1).reshape(FF // 2)

    def own_columns(v):
        return lax.dynamic_slice_in_dim(v, core * hw, hw, v.ndim - 1)

    ids = pick(clip_ids[:, 0], micro, 0).reshape(2, half, 2 * R)
    ids_q = pick(ids, place, 1).reshape(4 * R)
    order = (place - jnp.arange(half)) % half
    ids_k = jnp.take(ids, order, axis=1).transpose(1, 0, 2).reshape(half, 4 * R)
    tag = jnp.arange(TAGS, dtype=jnp.int32)[:, None]
    tags_q = jnp.where(ids_q[None, :] == tag, 0.0, masked_score).astype(low)
    tags_k = (ids_k[:, None, :] == tag[None]).astype(low)

    xf = x_rows.astype(wide)
    xhat, inverse = row_stats(xf)
    normed = (xhat * vec["g1"] + vec["s1"]).astype(low)
    bias_qkv = jnp.concatenate(
        [own_columns(vec["qb"]), jnp.zeros((hw,), wide), own_columns(vec["vb"])]
    )
    qkv_t = (dims(w_qkv, normed, 0, 1) + bias_qkv[:, None]).astype(low)
    q_t, kv_own = qkv_t[:hw], qkv_t[hw:]
    kv_parts = [kv_own]
    for o in range(1, half):
        kv_parts.append(
            lax.ppermute(
                kv_own, "zz", [(z, (z // half) * half + (z + o) % half) for z in range(Z)]
            )
        )
    kv = jnp.stack(kv_parts)
    tile = 256
    mixed_t, logs = attend_forward(q_t, tags_q, kv, tags_k, heads, tile)
    mixed_full = by_core(mixed_t, swap_core(mixed_t), 0)
    middle = xf + (dims(mixed_full, w_out, 0, 0) + vec["ob"])
    xhat_two, inverse_two = row_stats(middle)
    normed_two = (xhat_two * vec["g2"] + vec["s2"]).astype(low)
    inner = dims(normed_two, w_inner, 1, 0) + ib_half
    active, slope = gelu_parts(inner)
    active = active.astype(low)
    out_part = dims(active, w_outer, 1, 0)

    def split_rows(v):
        return v.reshape(2, 2, R, D)

    def reduce_rows(v):
        v = split_rows(v)
        return pick(v, core, 1) + swap_core(pick(v, 1 - core, 1).astype(low)).astype(wide)

    def home_rows(v):
        stay = pick(v, micro, 0)
        got = swap_half(pick(v, 1 - micro, 0))
        return jnp.where(first_half, jnp.stack([stay, got]), jnp.stack([got, stay]))[:, None]

    own_middle = pick(split_rows(middle), core, 1)
    layer_rows = (own_middle + (reduce_rows(out_part) + vec["ub"])).astype(low)
    layer_out = home_rows(layer_rows)

    grad_active = dims(cot, w_outer, 1, 1)
    inner_grad = (grad_active * slope).astype(low)
    part_two = dims(inner_grad, w_inner, 1, 1)
    grad_two = part_two + swap_core(part_two.astype(low)).astype(wide)
    middle_grad = cot.astype(wide) + norm_pull(grad_two, vec["g2"], xhat_two, inverse_two)
    branch_grad = middle_grad.astype(low)
    w_out_heads = lax.dynamic_slice_in_dim(w_out, core * hw, hw, 0)
    mixed_grad = dims(w_out_heads, branch_grad, 1, 1).astype(low)
    dq_t, own_kv, far_kv = attend_backward(
        q_t, tags_q, kv, tags_k, mixed_t, logs, mixed_grad, heads, tile
    )
    dkv = own_kv.reshape(2 * hw, 4 * R)
    for o in range(1, half):
        back = lax.ppermute(
            far_kv[o - 1], "zz", [(z, (z // half) * half + (z - o) % half) for z in range(Z)]
        )
        dkv = dkv + back.reshape(2 * hw, 4 * R).astype(wide)
    dqkv_t = jnp.concatenate([dq_t, dkv.astype(low)], 0)
    grad_one = reduce_rows(dims(dqkv_t, w_qkv, 0, 1))
    own_xhat = pick(split_rows(xhat), core, 1)
    own_inverse = pick(inverse.reshape(2, 2, R, 1), core, 1)
    frame_rows = pick(split_rows(middle_grad), core, 1) + norm_pull(
        grad_one, vec["g1"], own_xhat, own_inverse
    )
    sent = swap_half(pick(frame_rows, 1 - micro, 0).astype(low)).astype(wide)
    stay = pick(frame_rows, micro, 0)
    frames_grad = jnp.where(first_half, jnp.stack([stay, sent]), jnp.stack([sent, stay]))[:, None]

    g_qkv = dims(normed, dqkv_t, 0, 1).astype(low)
    g_out = dims(mixed_full, own_columns(branch_grad), 1, 0).astype(low)
    g_inner = dims(normed_two, inner_grad, 0, 0).astype(low)
    g_outer = dims(active, cot, 0, 0).astype(low)

    def zero_rest(v):
        return by_core(v, jnp.zeros_like(v), 0)

    bias_sums = jnp.sum(dqkv_t.astype(wide), axis=1)
    halves = 0.5
    col = {
        "qb": zero_rest(bias_sums[:hw]),
        "vb": zero_rest(bias_sums[2 * hw :]),
        "ob": halves * jnp.sum(branch_grad.astype(wide), 0),
        "ub": halves * jnp.sum(cot.astype(wide), 0),
        "g1": jnp.sum(grad_one * own_xhat, (0, 1)),
        "s1": jnp.sum(grad_one, (0, 1)),
        "g2": halves * jnp.sum(grad_two * xhat_two, 0),
        "s2": halves * jnp.sum(grad_two, 0),
    }
    ib_sum = jnp.sum(inner_grad.astype(wide), 0).reshape(K, 1, f)
    small_grad = jnp.concatenate(
        [col[n].reshape(K, 2, r) for n in names]
        + [by_core(ib_sum, jnp.zeros_like(ib_sum), 1)],
        2,
    )
    small_grad = jnp.pad(small_grad, ((0, 0), (0, 0), (0, small_pad - n_small)))
    small_grad = small_grad.reshape(K, 2, small_pad // 128, 128).astype(low)
    g_outer, g_inner, g_out, g_qkv, g_small = (
        lax.psum_scatter(v, CHIPS, scatter_dimension=0, tiled=False).astype(wide)
        for v in (
            g_outer.reshape(K, 2, f // 2, D),
            g_inner.reshape(K, 2, r, FF // 2),
            g_out.reshape(K, 2, r, hw),
            g_qkv.reshape(K, 2, r, 3 * hw),
            small_grad,
        )
    )
    wide_rows = jnp.concatenate([g_qkv, g_out, g_inner], 2)
    mine = pick(wide_rows, core, 0)
    theirs = swap_core(pick(wide_rows, 1 - core, 0))

    def whole(a, b, parts):
        a, b = a.reshape(r, parts, 1, -1), b.reshape(r, parts, 1, -1)
        return by_core(a, b, 2).reshape(r, -1)

    outs = []
    for i in range(4):
        outs.append(whole(mine[:, i * hw : (i + 1) * hw], theirs[:, i * hw : (i + 1) * hw], 1))
    outs.append(whole(mine[:, 4 * hw :], theirs[:, 4 * hw :], K))
    outs.append(g_outer.reshape(f, D))
    g_small = g_small.reshape(2, small_pad)[:, :n_small]
    g_small = pick(g_small, core, 0) + swap_core(pick(g_small, 1 - core, 0))
    sv = {n: g_small[i * r : (i + 1) * r] for i, n in enumerate(names)}
    return (layer_out, frames_grad) + tuple(outs) + (
        sv["qb"], sv["vb"], sv["ob"], g_small[8 * r :], sv["ub"],
        sv["g1"], sv["s1"], sv["g2"], sv["s2"],
    )


VECTORS = ("qb", "vb", "ob", "ub", "g1", "s1", "g2", "s2")


def linked_body(
    Z,
    frames,
    clip_ids,
    query_weight,
    key_weight,
    value_weight,
    output_weight,
    inner_weight,
    outer_weight,
    query_bias,
    value_bias,
    output_bias,
    inner_bias,
    outer_bias,
    first_gain,
    first_shift,
    second_gain,
    second_shift,
    out_cotangent,
):
    K = 4 * Z
    R, D = frames.shape[2], frames.shape[3]
    FF = inner_weight.shape[1]
    r = query_weight.shape[0]
    f = outer_weight.shape[0]
    hw = D // 2
    heads = H // 2
    half = Z // 2
    core = lax.axis_index("core")
    first_core = core == 0
    zz = lax.axis_index("zz")
    micro = zz // half
    first_half = micro == 0
    place = zz % half
    tile = 256

    def swap_core(v):
        return lax.ppermute(v, "core", [(0, 1), (1, 0)])

    def by_core(own, other, axis):
        return jnp.where(
            first_core,
            jnp.concatenate([own, other], axis),
            jnp.concatenate([other, own], axis),
        )

    def pick(v, index, axis):
        return lax.dynamic_index_in_dim(v, index, axis, keepdims=False)

    def own_columns(v):
        return lax.dynamic_slice_in_dim(v, core * hw, hw, v.ndim - 1)

    small = jnp.concatenate(
        [
            jnp.stack(
                [
                    query_bias, value_bias, output_bias, outer_bias,
                    first_gain, first_shift, second_gain, second_shift,
                ]
            ),
            inner_bias.reshape(f // r, r),
        ]
    )
    small = jnp.pad(small, ((0, 16 - small.shape[0]), (0, 128 - r)))

    ids = pick(clip_ids[:, 0], micro, 0).reshape(2, half, 2 * R)
    ids_q = pick(ids, place, 1).reshape(4 * R)
    ids_far = pick(ids, 1 - place, 1).reshape(4 * R)
    tag = jnp.arange(TAGS, dtype=jnp.int32)[:, None]
    tags_q = jnp.where(ids_q[None, :] == tag, 0.0, masked_score).astype(low)
    tags_k = (jnp.stack([ids_q, ids_far])[:, None, :] == tag[None]).astype(low)

    weights = (query_weight, key_weight, value_weight, output_weight, inner_weight, outer_weight)
    fw = forward_linked(frames, out_cotangent, weights, small, tags_q, tags_k, Z, heads, tile)
    vec = {n: fw.vectors[i] for i, n in enumerate(VECTORS)}
    cot = fw.cot_rows.reshape(4 * R, D)
    active, slope, middle = fw.active, fw.slope, fw.middle
    normed, normed_two = fw.normed, fw.normed_two
    g_outer = dims(active, cot, 0, 0).astype(low)
    out_part = dims(active, fw.w_outer, 1, 0)

    def split_rows(v):
        return v.reshape(2, 2, R, D)

    def reduce_rows(v):
        v = split_rows(v)
        return pick(v, core, 1) + swap_core(pick(v, 1 - core, 1).astype(low)).astype(wide)

    own_middle = pick(split_rows(middle), core, 1)
    layer_rows = (own_middle + (reduce_rows(out_part) + vec["ub"])).astype(low)
    grad_active = dims(cot, fw.w_outer, 1, 1)
    inner_grad = (grad_active * slope).astype(low)
    part_two = dims(inner_grad, fw.w_inner, 1, 1)
    grad_two = part_two + swap_core(part_two.astype(low)).astype(wide)
    xhat_two, inverse_two = row_stats(middle)
    middle_grad = cot.astype(wide) + norm_pull(grad_two, vec["g2"], xhat_two, inverse_two)
    branch_grad = middle_grad.astype(low)
    w_heads = lax.dynamic_slice_in_dim(fw.w_out, core * hw, hw, 1)
    mixed_grad = sum(
        dims(w_heads[b], branch_grad[:, b * hw : (b + 1) * hw], 1, 1) for b in (0, 1)
    ).astype(low)
    g_inner = dims(normed_two, inner_grad, 0, 0).astype(low)

    halves = 0.5
    none = jnp.zeros((D,), wide)
    small_part = jnp.stack(
        [
            none,
            none,
            halves * jnp.sum(branch_grad.astype(wide), 0),
            halves * jnp.sum(cot.astype(wide), 0),
            none,
            none,
            halves * jnp.sum(grad_two * xhat_two, 0),
            halves * jnp.sum(grad_two, 0),
        ]
    )
    hidden_sums = jnp.sum(inner_grad.astype(wide), 0)[None]
    hidden_sums = by_core(hidden_sums, jnp.zeros_like(hidden_sums), 1)
    bw = backward_linked(
        (
            fw.qkv, fw.far, tags_q, tags_k, fw.mixed, fw.logs, mixed_grad, branch_grad,
            fw.vectors, small_part, hidden_sums,
        ),
        (
            fw.x_rows, middle_grad.reshape(4, R, D), fw.normed, fw.w_qkv, g_outer, g_inner,
            layer_rows,
        ),
        Z, heads, tile,
    )
    sv = {n: bw.small[i, :r] for i, n in enumerate(VECTORS)}
    ib = bw.small[8 : 8 + f // r, :r].reshape(f)
    return (
        bw.layer_out, bw.frames_grad, bw.query, bw.key, bw.value, bw.output, bw.inner, bw.outer,
        sv["qb"], sv["vb"], sv["ob"], ib, sv["ub"],
        sv["g1"], sv["s1"], sv["g2"], sv["s2"],
    )


def solution(mesh):
    C, S = mesh.shape["clip"], mesh.shape["seq"]
    fine = Mesh(mesh.devices.reshape(2, C // 2, S // 2, 2), ("cy", "cx", "zz", "core"))
    clip, seq = ("cy", "cx"), ("zz", "core")
    every = clip + seq
    rows, mat, vec = P(None, clip, seq, None), P(every, None), P(every)
    in_specs = (rows, P(None, clip, None)) + (mat,) * 6 + (vec,) * 9 + (rows,)
    out_specs = (rows, rows) + (mat,) * 6 + (vec,) * 9
    linked = C == 4 and S == 8
    run = functools.partial(linked_body, S // 2) if linked else functools.partial(general_body, C, S // 2)
    return jax.shard_map(
        run,
        mesh=fine,
        in_specs=in_specs,
        out_specs=out_specs,
        check_vma=False,
    )
```

```python
import functools
import math
from typing import Any, NamedTuple

import jax
import jax.numpy as jnp
from jax import lax
from jax.experimental import pallas as pl
from jax.experimental.pallas import tpu as pltpu
from jax.sharding import Mesh
from jax.sharding import PartitionSpec as P

H = 16
HD = 80
TAGS = 16
epsilon = 1e-05
masked_score = -1e30
low = jnp.bfloat16
wide = jnp.float32


def dims(left_side, right_side, left_dim, right_dim):
    return lax.dot_general(
        left_side,
        right_side,
        (((left_dim,), (right_dim,)), ((), ())),
        preferred_element_type=wide,
    )


def attend_forward_kernel(blocks, q_ref, qa_ref, k_ref, v_ref, ka_ref, out_ref, log_ref):
    factor = HD ** (-0.5) * math.log2(math.e)
    query = jnp.concatenate([q_ref[...], qa_ref[...]], axis=0)
    scores = []
    for b in range(blocks):
        key = jnp.concatenate([k_ref[b], ka_ref[b]], axis=0)
        scores.append(dims(key, query, 0, 0))
    top = functools.reduce(jnp.maximum, [jnp.max(s, axis=0, keepdims=True) for s in scores])
    top = top * factor
    total = jnp.zeros_like(top)
    mixed = jnp.zeros((HD, query.shape[1]), wide)
    for b in range(blocks):
        part = jnp.exp2(scores[b] * factor - top)
        total = total + jnp.sum(part, axis=0, keepdims=True)
        mixed = mixed + dims(v_ref[b], part.astype(low), 1, 0)
    out_ref[...] = (mixed / total).astype(low)
    log_ref[0] = top + jnp.log2(total)


def attend_forward(q_t, tags_q, kv, tags_k, heads, tile):
    blocks, _, width = kv.shape
    rows = q_t.shape[1]
    grid = (heads, rows // tile)
    return pl.pallas_call(
        functools.partial(attend_forward_kernel, blocks),
        grid=grid,
        out_shape=(
            jax.ShapeDtypeStruct((heads * HD, rows), low),
            jax.ShapeDtypeStruct((heads, 1, rows), wide),
        ),
        in_specs=[
            pl.BlockSpec((HD, tile), lambda h, t: (h, t)),
            pl.BlockSpec((TAGS, tile), lambda h, t: (0, t)),
            pl.BlockSpec((blocks, HD, width), lambda h, t: (0, h, 0)),
            pl.BlockSpec((blocks, HD, width), lambda h, t: (0, heads + h, 0)),
            pl.BlockSpec((blocks, TAGS, width), lambda h, t: (0, 0, 0)),
        ],
        out_specs=(
            pl.BlockSpec((HD, tile), lambda h, t: (h, t)),
            pl.BlockSpec((1, 1, tile), lambda h, t: (h, 0, t)),
        ),
        cost_estimate=pl.CostEstimate(
            flops=4 * heads * rows * blocks * width * HD,
            bytes_accessed=2 * kv.size,
            transcendentals=heads * rows * blocks * width,
        ),
    )(q_t, tags_q, kv, kv, tags_k)


def attend_backward_kernel(
    blocks, q_ref, qa_ref, k_ref, v_ref, ka_ref, o_ref, log_ref, g_ref, dq_ref, own_ref, far_ref, acc_k, acc_v
):
    factor = HD ** (-0.5) * math.log2(math.e)
    step, steps = pl.program_id(1), pl.num_programs(1)
    head_query = q_ref[...]
    grad = g_ref[...]
    query = jnp.concatenate([head_query, qa_ref[...]], axis=0)
    delta = jnp.sum(grad.astype(wide) * o_ref[...].astype(wide), axis=0, keepdims=True)
    logs = log_ref[0]
    query_rows = head_query.T
    grad_rows = grad.T
    dq = jnp.zeros(head_query.shape, wide)

    @pl.when(step == 0)
    def _():
        acc_k[...] = jnp.zeros_like(acc_k)
        acc_v[...] = jnp.zeros_like(acc_v)

    for b in range(blocks):
        key = jnp.concatenate([k_ref[b], ka_ref[b]], axis=0)
        probs = jnp.exp2(dims(key, query, 0, 0) * factor - logs)
        grad_probs = dims(v_ref[b], grad, 0, 0)
        score_grad = (probs * (grad_probs - delta)).astype(low)
        acc_v[b] += dims(probs.astype(low), grad_rows, 1, 0)
        acc_k[b] += dims(score_grad, query_rows, 1, 0)
        dq = dq + dims(k_ref[b], score_grad, 1, 0)
    dq_ref[...] = (dq * HD ** (-0.5)).astype(low)

    @pl.when(step == steps - 1)
    def _():
        for b in range(blocks):
            key_part = acc_k[b].T * HD ** (-0.5)
            value_part = acc_v[b].T
            if b == 0:
                own_ref[0] = key_part
                own_ref[1] = value_part
            else:
                far_ref[b - 1, 0] = key_part.astype(low)
                far_ref[b - 1, 1] = value_part.astype(low)


def attend_backward(q_t, tags_q, kv, tags_k, mixed_t, logs, grad_t, heads, tile):
    blocks, _, width = kv.shape
    rows = q_t.shape[1]
    grid = (heads, rows // tile)
    per_query = pl.BlockSpec((HD, tile), lambda h, t: (h, t))
    return pl.pallas_call(
        functools.partial(attend_backward_kernel, blocks),
        grid=grid,
        out_shape=(
            jax.ShapeDtypeStruct((heads * HD, rows), low),
            jax.ShapeDtypeStruct((2, heads * HD, width), wide),
            jax.ShapeDtypeStruct((blocks - 1, 2, heads * HD, width), low),
        ),
        in_specs=[
            per_query,
            pl.BlockSpec((TAGS, tile), lambda h, t: (0, t)),
            pl.BlockSpec((blocks, HD, width), lambda h, t: (0, h, 0)),
            pl.BlockSpec((blocks, HD, width), lambda h, t: (0, heads + h, 0)),
            pl.BlockSpec((blocks, TAGS, width), lambda h, t: (0, 0, 0)),
            per_query,
            pl.BlockSpec((1, 1, tile), lambda h, t: (h, 0, t)),
            per_query,
        ],
        out_specs=(
            per_query,
            pl.BlockSpec((2, HD, width), lambda h, t: (0, h, 0)),
            pl.BlockSpec((blocks - 1, 2, HD, width), lambda h, t: (0, 0, h, 0)),
        ),
        scratch_shapes=[
            pltpu.VMEM((blocks, width, HD), wide),
            pltpu.VMEM((blocks, width, HD), wide),
        ],
        cost_estimate=pl.CostEstimate(
            flops=10 * heads * rows * blocks * width * HD,
            bytes_accessed=4 * kv.size,
            transcendentals=heads * rows * blocks * width,
        ),
    )(q_t, tags_q, kv, kv, tags_k, mixed_t, logs, grad_t)


def row_stats(values):
    centre = jnp.mean(values, axis=-1, keepdims=True)
    centred = values - centre
    inverse = lax.rsqrt(jnp.mean(centred * centred, axis=-1, keepdims=True) + epsilon)
    return centred * inverse, inverse


def norm_pull(grad, gain, xhat, inverse):
    e = grad * gain
    return inverse * (
        e
        - jnp.mean(e, axis=-1, keepdims=True)
        - xhat * jnp.mean(e * xhat, axis=-1, keepdims=True)
    )


def gelu_parts(u):
    phi_sum = 0.5 * (1.0 + lax.erf(u * math.sqrt(0.5)))
    density = jnp.exp(-0.5 * u * u) * (1.0 / math.sqrt(2.0 * math.pi))
    return u * phi_sum, phi_sum + u * density


CHIPS = ("cy", "cx", "zz")
MESH = pl.DeviceIdType.MESH
BIG = 62 * 1024 * 1024


def offsets(Z):
    steps = []
    for d in range(1, Z):
        steps += [-d, d]
    return steps


def full(n, space=pltpu.VMEM):
    return [pl.BlockSpec(memory_space=space)] * n


class Links:
    def __init__(self, Z):
        self.Z = Z
        self.y, self.x, self.z = (lax.axis_index(a) for a in CHIPS)
        self.core = lax.axis_index("core")
        self.half = lax.div(self.z, Z // 2)
        self.crossed = lax.rem(self.y + self.core, 2)

    def sides(self, colour):
        return (("cx", "cy"), ("cy", "cx"))[colour]

    def coords(self, flips, z):
        y = 1 - self.y if "cy" in flips else self.y
        x = 1 - self.x if "cx" in flips else self.x
        return y, x, z

    def index(self, place):
        y, x, z = place
        return (y * 2 + x) * self.Z + z

    def at(self, flips, z):
        return self.index(self.coords(flips, z))

    def target(self, to):
        if to == "cy":
            return {"cy": 1 - self.y}
        if to == "cx":
            return {"cx": 1 - self.x}
        if to == "core":
            return {"core": 1 - self.core}
        if to == "pair":
            return {"zz": self.z + 1 - 2 * lax.rem(self.z, 2)}
        if to == "swap":
            return {"zz": self.z + (self.Z // 2) * (1 - 2 * self.half)}
        if to == "diagonal":
            return {"cy": self.core, "core": self.y}
        return {"zz": self.z + to}

    def has(self, step):
        there = self.z + step
        return jnp.logical_and(there >= 0, there < self.Z)

    def when(self, steps, run):
        steps = [s for s in steps if s]
        if steps:
            pl.when(functools.reduce(jnp.logical_and, [self.has(s) for s in steps]))(run)
        else:
            run()

    def barrier(self, *more):
        sem = pltpu.get_barrier_semaphore()
        for to in ("cy", "cx") + tuple(m for m in more if m != "diagonal"):
            pl.semaphore_signal(sem, inc=1, device_id=self.target(to), device_id_type=MESH)
        for step in (-1, 1):

            @pl.when(self.has(step))
            def _():
                pl.semaphore_signal(
                    sem, inc=1, device_id=self.target(step), device_id_type=MESH
                )

        count = 2 + len([m for m in more if m != "diagonal"])
        count = count + jnp.minimum(self.z, 1) + jnp.minimum(self.Z - 1 - self.z, 1)
        if "diagonal" in more:

            @pl.when(self.crossed == 1)
            def _():
                pl.semaphore_signal(
                    sem, inc=1, device_id=self.target("diagonal"), device_id_type=MESH
                )

            count = count + self.crossed
        pl.semaphore_wait(sem, count)


def remote(src, dst, send, recv, to):
    return pltpu.make_async_remote_copy(
        src_ref=src, dst_ref=dst, send_sem=send, recv_sem=recv, device_id=to, device_id_type=MESH
    )


class Gather:
    def __init__(self, links, block, sems):
        self.l, self.block, self.chunks = links, block, 7
        self.send_sem, self.recv_sem = sems

    def copy(self, i, colour, flips, step, base, to):
        place = self.l.coords(flips, self.l.z + step)
        block = self.block(i, colour, place)
        return remote(
            block,
            block,
            self.send_sem.at[i, colour, base + self.l.z + step],
            self.recv_sem.at[i, colour, self.l.index(place)],
            self.l.target(to),
        )

    def send(self, steps, *what):
        self.l.when(steps, lambda: self.copy(*what).start())

    def arrive(self, i, colour, flips, step):
        self.l.when([step], lambda: self.copy(i, colour, flips, step, 0, "cx").wait_recv())

    def own(self, i):
        for colour in (0, 1):
            for step, base in ((1, 0), (-1, self.l.Z)):
                self.send([step], i, colour, (), 0, base, step)

    def along(self, i, distance):
        for step in (-distance, distance):
            onward = 1 if step < 0 else -1
            for colour in (0, 1):
                self.arrive(i, colour, (), step)
                self.send([step, onward], i, colour, (), step, 0 if step < 0 else self.l.Z, onward)

    def aside(self, i, distance):
        for step in (-distance, distance) if distance else (0,):
            for colour in (0, 1):
                near, far = self.l.sides(colour)
                self.send([step], i, colour, (), step, 2 * self.l.Z, near)
                self.send([step], i, colour, (), step, 3 * self.l.Z, far)

    def across(self, i, distance):
        for step in (-distance, distance) if distance else (0,):
            for colour in (0, 1):
                near, far = self.l.sides(colour)
                self.arrive(i, colour, (near,), step)
                self.send([step], i, colour, (near,), step, 4 * self.l.Z, far)

    def last(self, i):
        def one(z, carry):
            for colour in (0, 1):
                near, far = self.l.sides(colour)
                for flips in ((far,), (far, near)):
                    self.copy(i, colour, flips, z - self.l.z, 0, "cx").wait_recv()
            return carry

        lax.fori_loop(0, self.l.Z, one, 0)

    def drain(self):
        l, Z = self.l, self.l.Z

        def sent(i, like, z):
            for colour in (0, 1):
                block = self.block(like, colour, l.coords((), l.z))

                def wait(slot):
                    remote(
                        block, block, self.send_sem.at[i, colour, slot],
                        self.recv_sem.at[i, colour, 0], l.target("cx"),
                    ).wait_send()

                for base in (2, 3, 4):
                    wait(base * Z + z)
                pl.when(jnp.logical_and(z <= l.z, l.z + 1 < Z))(lambda: wait(z))
                pl.when(jnp.logical_and(z >= l.z, l.z > 0))(lambda: wait(Z + z))

        def one(index, carry):
            sent(1 + lax.div(index, Z), 1, lax.rem(index, Z))
            return carry

        def small(z, carry):
            sent(0, 0, z)
            return carry

        lax.fori_loop(0, Z, small, 0)
        lax.fori_loop(0, (self.chunks - 1) * Z, one, 0)

    @staticmethod
    def semaphores(n, Z):
        return [
            pltpu.SemaphoreType.DMA((n, 2, 5 * Z)),
            pltpu.SemaphoreType.DMA((n, 2, 4 * Z)),
        ]


GROUP_HEADS = 2
PARTS = 4
class ForwardOuts(NamedTuple):
    vectors: Any
    w_qkv: Any
    w_out: Any
    w_inner: Any
    w_outer: Any
    cot_rows: Any
    x_rows: Any
    normed: Any
    qkv: Any
    far: Any
    mixed: Any
    logs: Any
    middle: Any
    normed_two: Any
    active: Any
    slope: Any


class ForwardScratch(NamedTuple):
    small_all: Any
    hidden_bias: Any
    x: Any
    norm_v: Any
    qkv_v: Any
    far_v: Any
    mix_v: Any
    wq_v: Any
    wo_v: Any
    wi_v: Any
    n2_v: Any
    mid_v: Any
    act_v: Any
    slo_v: Any
    cot_own: Any
    local: Any
    core_send: Any
    core_recv: Any
    row_sem: Any
    kv_send: Any
    kv_recv: Any
    mix_send: Any
    mix_recv: Any
    wo_sem: Any
    out_sem: Any
    load_sem: Any
    gather_send: Any
    gather_recv: Any


def norm_rows(values, gain, shift):
    xhat, _ = row_stats(values)
    return (xhat * gain + shift).astype(low)


def forward_kernel(Z, heads, tile, *refs):
    (frames, cot, wq, wk, wv, wo, wi, w2, small, tags_q, tags_k) = refs[:11]
    n_outs = len(ForwardOuts._fields)
    o = ForwardOuts(*refs[11 : 11 + n_outs])
    s = ForwardScratch(*refs[11 + n_outs :])
    l = Links(Z)
    core, K = l.core, 4 * Z
    here = l.at((), l.z)
    r, D = wq.shape
    hw = D // 2
    f = w2.shape[0]
    R = frames.shape[2]
    rows = 4 * R
    width = heads * HD
    tiles = rows // tile
    groups = heads // GROUP_HEADS
    span = GROUP_HEADS * HD
    factor = HD ** (-0.5) * math.log2(math.e)
    vectors = o.vectors

    def natural(place):
        y, x, z = place
        return (x * Z + z) * 2 + y

    def block(i, colour, place):
        k = l.index(place)
        rows80 = pl.ds(pl.multiple_of(k * 2 * r, 16), 2 * r)
        if i == 0:
            return s.small_all.at[k, colour]
        if i == 1:
            return o.w_qkv.at[rows80, pl.ds(colour * hw, hw)]
        if i == 2:
            if colour == 0:
                return o.w_qkv.at[rows80, pl.ds(2 * hw, hw)]
            return o.w_out.at[core, rows80, :]
        if i < 5:
            return o.w_inner.at[rows80, pl.ds(((i - 3) * 2 + colour) * hw, hw)]
        at = natural(place) * f + ((i - 5) * 2 + colour) * (f // 4)
        return o.w_outer.at[pl.ds(pl.multiple_of(at, 8), f // 4), :]

    gather = Gather(l, block, (s.gather_send, s.gather_recv))

    def my_rows():
        return pl.ds(pl.multiple_of(here * 2 * r + core * r, 8), r)

    sources = ((wq, hw), (wk, hw), (wv, hw), (wo, hw), (wi, 2 * D))

    def place_of(m, of_core):
        if m == 3:
            return o.w_out.at[of_core, my_rows(), :]
        if m == 4:
            return o.w_inner.at[my_rows(), :]
        return o.w_qkv.at[my_rows(), pl.ds(m * hw, hw)]

    def keep(m):
        if m == 5:
            return pltpu.make_async_copy(small, s.small_all.at[here, core], s.local.at[m])
        src, cols = sources[m]
        window = pl.ds(pl.multiple_of(core * cols, 128), cols)
        return pltpu.make_async_copy(src.at[:, window], place_of(m, core), s.local.at[m])

    def give(m):
        sems = s.core_send.at[m], s.core_recv.at[m]
        if m == 5:
            return remote(small, s.small_all.at[here, core], *sems, l.target("core"))
        src, cols = sources[m]
        window = pl.ds(pl.multiple_of((1 - core) * cols, 128), cols)
        return remote(src.at[:, window], place_of(m, 1 - core), *sems, l.target("core"))

    outer_rows = pl.ds(pl.multiple_of(((l.x * Z + l.z) * 2 + core) * f, 16), f)

    def outer_keep():
        return pltpu.make_async_copy(w2, o.w_outer.at[outer_rows, :], s.local.at[6])

    def outer_give():
        return remote(
            w2,
            o.w_outer.at[outer_rows, :],
            s.core_send.at[6],
            s.core_recv.at[6],
            l.target("diagonal"),
        )

    def begin(m):
        keep(m).start()
        give(m).start()

    def ready(m):
        keep(m).wait()
        give(m).wait_recv()

    def row_copies(source, target, base):
        m = l.half
        mine, theirs = m * 2 + core, (1 - m) * 2 + core
        swaps = []
        for p in range(PARTS):
            part = pl.ds(p * (R // PARTS), R // PARTS)
            swaps.append(
                remote(
                    source.at[1 - m, 0, part, :], target.at[mine, part, :],
                    s.row_sem.at[base, p], s.row_sem.at[base + 1, p], l.target("swap"),
                )
            )
        return (
            swaps,
            remote(
                source.at[m, 0], target.at[mine],
                s.row_sem.at[base, PARTS], s.row_sem.at[base + 1, PARTS], l.target("core"),
            ),
            remote(
                target.at[theirs], target.at[theirs],
                s.row_sem.at[base, PARTS + 1], s.row_sem.at[base + 1, PARTS + 1], l.target("core"),
            ),
        )

    frame_copies = lambda: row_copies(frames, s.x, 0)
    cot_copies = lambda: row_copies(cot, o.cot_rows, 2)
    frame_own = lambda: pltpu.make_async_copy(
        frames.at[l.half, 0], s.x.at[l.half * 2 + core], s.local.at[7]
    )
    cot_load = lambda: pltpu.make_async_copy(cot.at[l.half, 0], s.cot_own, s.local.at[8])
    cot_store = lambda: pltpu.make_async_copy(
        s.cot_own, o.cot_rows.at[l.half * 2 + core], s.local.at[8]
    )

    def kv_copy(g, which):
        at = which * width + g * span
        return remote(
            s.qkv_v.at[pl.ds(width + at, span)],
            s.far_v.at[pl.ds(at, span)],
            s.kv_send.at[g, which],
            s.kv_recv.at[g, which],
            l.target("pair"),
        )

    def mix_copy(g, of_core):
        at = pl.ds(pl.multiple_of(of_core * width + g * span, 16), span)
        return remote(
            s.mix_v.at[at],
            s.mix_v.at[at],
            s.mix_send.at[g],
            s.mix_recv.at[g],
            l.target("core"),
        )

    def wo_copy(of_core):
        return remote(
            o.w_out.at[of_core], o.w_out.at[of_core],
            s.wo_sem.at[0], s.wo_sem.at[1], l.target("core"),
        )

    def wide_load(which):
        return pltpu.make_async_copy(
            o.w_qkv.at[:, pl.ds(which * hw, hw)], s.wq_v.at[which], s.load_sem.at[which]
        )

    def wo_load():
        return pltpu.make_async_copy(o.w_out, s.wo_v, s.load_sem.at[3])

    inner_tile = 256

    def wi_load(c):
        cols = pl.ds(pl.multiple_of(c * inner_tile, inner_tile), inner_tile)
        slot = lax.rem(c, 2)
        return pltpu.make_async_copy(
            o.w_inner.at[:, cols], s.wi_v.at[slot], s.load_sem.at[4 + slot]
        )

    stores = (
        (s.x, o.x_rows), (s.norm_v, o.normed), (s.qkv_v, o.qkv), (s.far_v, o.far), (s.mix_v, o.mixed),
        (s.mid_v, o.middle), (s.n2_v, o.normed_two), (s.act_v, o.active), (s.slo_v, o.slope),
    )

    def store(i):
        return pltpu.make_async_copy(*stores[i], s.out_sem.at[i])

    big = rows // 2

    def big_rows(t):
        return pl.ds(pl.multiple_of(t * big, 128), big)

    def x_tile(t):
        return s.x[pl.ds(2 * t, 2)].reshape(big, D).astype(wide)

    def project(t, whiches):
        if 0 in whiches:
            s.norm_v[big_rows(t), :] = norm_rows(x_tile(t), vectors[4:5, :], vectors[5:6, :])
        source = s.norm_v[big_rows(t), :]
        mine = pl.ds(pl.multiple_of(core * hw, 128), hw)
        for which in whiches:
            part = dims(source, s.wq_v[which], 1, 0)
            if which == 0:
                part = part + vectors[0:1, mine]
            if which == 2:
                part = part + vectors[1:2, mine]
            s.qkv_v[pl.ds(which * hw, hw), big_rows(t)] = part.T.astype(low)

    def attend(index):
        head, part = index // tiles, lax.rem(index, tiles)
        row = head * HD
        columns = pl.ds(pl.multiple_of(part * tile, tile), tile)
        qkv, far = s.qkv_v, s.far_v

        def feature(base):
            return pl.ds(pl.multiple_of(base + row, 16), HD)

        query = jnp.concatenate([qkv[feature(0), columns], tags_q[:, columns]], axis=0)
        keys = (qkv[feature(width), :], far[feature(0), :])
        values = (qkv[feature(2 * width), :], far[feature(width), :])
        scores = [
            dims(jnp.concatenate([keys[b], tags_k[b]], axis=0), query, 0, 0) for b in (0, 1)
        ]
        top = jnp.maximum(*[jnp.max(v, axis=0, keepdims=True) for v in scores]) * factor
        total = jnp.zeros_like(top)
        sums = jnp.zeros((HD, tile), wide)
        for b in (0, 1):
            part_values = jnp.exp2(scores[b] * factor - top)
            total = total + jnp.sum(part_values, axis=0, keepdims=True)
            sums = sums + dims(values[b], part_values.astype(low), 1, 0)
        s.mix_v[feature(core * width), columns] = (sums / total).astype(low)
        o.logs[head, :, columns] = top + jnp.log2(total)

    def branch(t):
        parts = [dims(s.mix_v[:, big_rows(t)], s.wo_v[b], 0, 0) for b in (0, 1)]
        middle = x_tile(t) + (jnp.concatenate(parts, axis=1) + vectors[2:3, :])
        s.mid_v[big_rows(t), :] = middle
        s.n2_v[big_rows(t), :] = norm_rows(middle, vectors[6:7, :], vectors[7:8, :])

    column_tiles = 2 * D // inner_tile

    def inner(index):
        c, t = index // 2, lax.rem(index, 2)

        @pl.when(t == 0)
        def _():
            @pl.when(c + 1 < column_tiles)
            def _():
                wi_load(c + 1).start()

            wi_load(c).wait()

        cols = pl.ds(pl.multiple_of(c * inner_tile, inner_tile), inner_tile)
        bias_at = pl.ds(pl.multiple_of(core * 2 * D + c * inner_tile, inner_tile), inner_tile)
        value = dims(s.n2_v[big_rows(t), :], s.wi_v[lax.rem(c, 2)], 1, 0)
        active, slope = gelu_parts(value + s.hidden_bias[:, bias_at])
        s.act_v[big_rows(t), cols] = active.astype(low)
        s.slo_v[big_rows(t), cols] = slope

    def unpack():
        for k in range(K):
            for q in (0, 1):
                d = 2 * k + q
                vectors[:, d * r : (d + 1) * r] = s.small_all[k, q, 0:8, 0:r].astype(wide)
                per = f // r
                for j in range(per):
                    at = d * f + j * r
                    s.hidden_bias[:, at : at + r] = s.small_all[
                        k, q, 8 + j : 9 + j, 0:r
                    ].astype(wide)

    l.barrier("core", "swap", "diagonal")
    begin(5)
    begin(0)
    begin(1)
    _, own_f, _ = frame_copies()
    own_f.start()
    frame_own().start()
    for m in (2, 3, 4):
        begin(m)
    pl.when(l.crossed == 1)(lambda: outer_give().start())
    pl.when(l.crossed == 0)(lambda: outer_keep().start())
    cot_load().start()

    plan = {}

    def at(step, *runs):
        plan.setdefault(step, []).extend(runs)

    def own_outer():
        pl.when(l.crossed == 1)(lambda: outer_give().wait_recv())
        pl.when(l.crossed == 0)(lambda: outer_keep().wait())

    along = lambda i, d: functools.partial(gather.along, i, d)
    across = lambda i, d: functools.partial(gather.across, i, d)
    last = lambda i: functools.partial(gather.last, i)

    def rows_arrive():
        swaps, mine, pass_on = frame_copies()
        for swap in swaps:
            swap.wait_recv()
        pass_on.start()
        mine.wait_recv()
        pass_on.wait_recv()
        frame_own().wait()

    def kv_ready(g):
        for which in (0, 1):
            kv_copy(g, which).wait_recv()

    def cot_start():
        cot_load().wait()
        _, mine, _ = cot_copies()
        mine.start()
        cot_store().start()

    def cot_pass():
        swaps, _, pass_on = cot_copies()
        for swap in swaps:
            swap.wait_recv()
        pass_on.start()

    def after_v():
        wo_copy(1 - core).wait_recv()
        wo_load().start()

    def mix_ready():
        for g in range(groups):
            mix_copy(g, 1 - core).wait_recv()

    def kv_send(which, *gs):
        for g in gs:
            kv_copy(g, which).start()

    def swap_frames(*ps):
        for p in ps:
            frame_copies()[0][p].start()

    def swap_cot(*ps):
        for p in ps:
            cot_copies()[0][p].start()

    frames_go = lambda *ps: functools.partial(swap_frames, *ps)
    cot_go = lambda *ps: functools.partial(swap_cot, *ps)

    attends = heads * tiles
    v0, a0 = 2, 4
    b0 = a0 + attends
    i0 = b0 + 2
    end = i0 + 2 * column_tiles
    own = lambda i: functools.partial(gather.own, i)
    aside = lambda i, d: functools.partial(gather.aside, i, d)
    here_now = lambda *ms: (lambda: [ready(m) for m in ms])
    send_kv = lambda which, *gs: functools.partial(kv_send, which, *gs)

    at(0, here_now(5), own(0), aside(0, 0), here_now(0, 1), own(1), aside(1, 0))
    at(0, along(0, 1), aside(0, 1), here_now(2, 3), own(2), along(0, 2), aside(0, 2), along(0, 3), aside(0, 3))
    at(0, aside(2, 0), frames_go(0), across(0, 0), across(0, 1), across(0, 2), across(0, 3))
    at(0, along(1, 1), aside(1, 1), frames_go(1), along(1, 2), aside(1, 2), here_now(4), own(3), across(1, 0))
    at(0, frames_go(2), along(2, 1), aside(2, 1), along(1, 3), aside(1, 3), across(1, 1), frames_go(3))
    at(0, along(2, 2), aside(2, 2))
    at(0, own(4), across(1, 2), along(2, 3), aside(2, 3), across(1, 3), along(3, 1), last(0), unpack)
    at(0, aside(3, 0), across(2, 0), aside(3, 1), along(3, 2), rows_arrive, lambda: store(0).start())
    at(0, last(1), lambda: wide_load(0).start(), lambda: wide_load(1).start())
    at(0, lambda: wide_load(0).wait(), lambda: wide_load(1).wait())
    at(1, across(2, 1), along(4, 1), aside(3, 2), own_outer, own(5), along(3, 3))
    at(2, send_kv(0, 0), lambda: store(1).start(), across(2, 2), aside(3, 3), across(2, 3), aside(4, 0))
    at(2, along(4, 2), across(3, 0), own(6), send_kv(0, 1), aside(4, 1), across(3, 1), along(4, 3), last(2))
    at(2, lambda: wide_load(2).start(), lambda: wo_copy(core).start(), lambda: wide_load(2).wait())
    at(a0, send_kv(1, 0), lambda: store(2).start(), aside(4, 2))
    at(a0 + 1, across(3, 2), aside(4, 3), send_kv(1, 1))
    at(a0 + 3, along(5, 1), across(3, 3), send_kv(0, 2))
    at(a0 + 4, cot_start)
    at(a0 + 5, aside(5, 0), across(4, 0), along(5, 2), send_kv(1, 2))
    at(a0 + 7, aside(5, 1), across(4, 1))
    at(a0 + 9, along(6, 1), after_v, send_kv(0, 3))
    at(a0 + 11, aside(5, 2), across(4, 2), send_kv(1, 3))
    at(a0 + 13, along(5, 3), aside(5, 3), cot_go(0))
    at(a0 + 15, across(4, 3))
    at(a0 + 17, along(6, 2), aside(6, 0), cot_go(1))
    at(a0 + 19, across(5, 0), aside(6, 1))
    at(a0 + 20, across(5, 1), cot_go(2))
    at(a0 + 21, along(6, 3), aside(6, 2))
    at(a0 + 22, cot_go(3))
    at(a0 + 23, across(5, 2))
    at(i0 + 2, cot_pass)
    for g in range(groups):
        at(a0 + g * GROUP_HEADS * tiles, functools.partial(kv_ready, g))
        at(a0 + (g + 1) * GROUP_HEADS * tiles, lambda g=g: mix_copy(g, core).start())
    at(b0, aside(6, 3), across(5, 3), lambda: store(3).start())
    at(b0, lambda: wo_load().wait(), mix_ready, lambda: store(4).start())
    at(b0 + 1, across(6, 0))
    at(i0, across(6, 1), lambda: store(5).start(), lambda: store(6).start(), last(3))
    at(i0, lambda: wi_load(0).start())
    at(i0 + 3, across(6, 2))
    at(i0 + 7, across(6, 3))
    at(i0 + 8, last(4))

    def one(step, carry):
        for when in sorted(plan):

            def run():
                for tick in plan[when]:
                    tick()

            pl.when(step == when)(run)
        inside = lambda lo, n: jnp.logical_and(step >= lo, step < lo + n)
        pl.when(step < v0)(lambda: project(step, (0, 1)))
        pl.when(inside(v0, 2))(lambda: project(step - v0, (2,)))
        pl.when(inside(a0, attends))(lambda: attend(step - a0))
        pl.when(inside(b0, 2))(lambda: branch(step - b0))
        pl.when(inside(i0, 2 * column_tiles))(lambda: inner(step - i0))
        return carry

    lax.fori_loop(0, end, one, 0)
    store(7).start()
    store(8).start()
    gather.last(5)
    gather.last(6)
    gather.drain()
    for m in range(6):
        give(m).wait_send()
    pl.when(l.crossed == 1)(lambda: outer_give().wait_send())
    for swaps, mine, pass_on in (frame_copies(), cot_copies()):
        for copy in swaps + [mine, pass_on]:
            copy.wait_send()
    _, mine, pass_on = cot_copies()
    mine.wait_recv()
    pass_on.wait_recv()
    cot_store().wait()
    wo_copy(core).wait_send()
    for g in range(groups):
        mix_copy(g, core).wait_send()
        for which in (0, 1):
            kv_copy(g, which).wait_send()
    for i in range(len(stores)):
        store(i).wait()


def forward_linked(frames, cot, weights, small, tags_q, tags_k, Z, heads, tile):
    K = 4 * Z
    r, D = weights[0].shape
    FF2 = weights[4].shape[1] // 2
    R = frames.shape[2]
    rows = 4 * R
    hw = D // 2
    groups = heads // GROUP_HEADS
    shape = jax.ShapeDtypeStruct
    outs = ForwardOuts(
        vectors=shape((8, D), wide),
        w_qkv=shape((D, 3 * hw), low),
        w_out=shape((2, D, hw), low),
        w_inner=shape((D, FF2), low),
        w_outer=shape((FF2, D), low),
        cot_rows=shape((4, R, D), low),
        x_rows=shape((4, R, D), low),
        normed=shape((rows, D), low),
        qkv=shape((3 * hw, rows), low),
        far=shape((2 * hw, rows), low),
        mixed=shape((D, rows), low),
        logs=shape((heads, 1, rows), wide),
        middle=shape((rows, D), wide),
        normed_two=shape((rows, D), low),
        active=shape((rows, FF2), low),
        slope=shape((rows, FF2), wide),
    )
    dma = pltpu.SemaphoreType.DMA
    scratch = [
        pltpu.VMEM((K, 2) + small.shape, low),
        pltpu.VMEM((1, 2 * FF2), wide),
        pltpu.VMEM((4, R, D), low),
        pltpu.VMEM((rows, D), low),
        pltpu.VMEM((3 * hw, rows), low),
        pltpu.VMEM((2 * hw, rows), low),
        pltpu.VMEM((D, rows), low),
        pltpu.VMEM((3, D, hw), low),
        pltpu.VMEM((2, D, hw), low),
        pltpu.VMEM((2, D, 256), low),
        pltpu.VMEM((rows, D), low),
        pltpu.VMEM((rows, D), wide),
        pltpu.VMEM((rows, FF2), low),
        pltpu.VMEM((rows, FF2), wide),
        pltpu.VMEM((R, D), low),
        dma((9,)),
        dma((7,)),
        dma((7,)),
        dma((4, PARTS + 2)),
        dma((groups, 2)),
        dma((groups, 2)),
        dma((groups,)),
        dma((groups,)),
        dma((2,)),
        dma((9,)),
        dma((6,)),
    ]
    spaces = [pltpu.VMEM if v in (outs.vectors, outs.logs) else pl.ANY for v in outs]
    results = pl.pallas_call(
        functools.partial(forward_kernel, Z, heads, tile),
        out_shape=tuple(outs),
        in_specs=full(2, pl.ANY) + full(9),
        out_specs=tuple(pl.BlockSpec(memory_space=space) for space in spaces),
        scratch_shapes=scratch + Gather.semaphores(7, Z),
        compiler_params=pltpu.CompilerParams(
            collective_id=0, has_side_effects=True, vmem_limit_bytes=BIG
        ),
    )(frames, cot, *weights, small, tags_q, tags_k)
    return ForwardOuts(*results)


SETS = 3


class Scatter:
    def __init__(self, links, i, block, out, buffers, sems, credit):
        self.l, self.i, self.block, self.out = links, i, block, out
        self.held, self.from_far, self.from_near, self.from_line = buffers
        self.load_sem, self.send_sem, self.recv_sem = sems
        self.credit = credit
        self.drained = False

    def load(self, colour, side, step):
        l = self.l
        near, far = l.sides(colour)
        z = l.z + step
        return pltpu.make_async_copy(
            self.block(self.i, colour, l.coords((near,) if side else (), z)),
            self.held.at[colour, side, z],
            self.load_sem.at[self.i, colour, side * l.Z + z],
        )

    def remote(self, colour, kind, step, to):
        l, Z = self.l, self.l.Z
        near, far = l.sides(colour)
        z = l.z + step
        if kind < 2:
            src = self.block(self.i, colour, l.coords((near, far) if kind else (far,), z))
            dst = self.from_far.at[colour, kind, z]
        elif kind == 2:
            src, dst = self.held.at[colour, 1, z], self.from_near.at[colour, z]
        else:
            src, dst = self.held.at[colour, 0, z], self.from_line.at[colour, kind - 3, z]
        return remote(
            src,
            dst,
            self.send_sem.at[self.i, colour, min(kind, 3) * Z + z],
            self.recv_sem.at[self.i, colour, kind * Z + z],
            l.target(to),
        )

    def arrive(self, colour, kind, step):
        self.remote(colour, kind, step, "cx").wait_recv()

    def send(self, step, *what):
        self.remote(*what).start()

    def both(self, distance, run):
        for step in (-distance, distance) if distance else (0,):
            for colour in (0, 1):
                self.l.when([step], functools.partial(run, step, colour))

    def start(self):
        def run(step, colour):
            near, far = self.l.sides(colour)
            self.send(step, colour, 1, step, far)
            self.load(colour, 1, step).start()

        for distance in range(self.l.Z - 1, -1, -1):
            self.both(distance, run)

    def total(self, target, parts):
        rows, cols = target.shape
        pieces = 5 if cols % 640 == 0 else 1
        wide_cols = cols // pieces

        def one(p, carry):
            window = pl.ds(pl.multiple_of(p * wide_cols, 128), wide_cols)
            value = parts[0][:, window].astype(wide)
            for part in parts[1:]:
                value = value + part[:, window].astype(wide)
            target[:, window] = value.astype(target.dtype)
            return carry

        lax.fori_loop(0, pieces, one, 0)

    def near(self, distance):
        def run(step, colour):
            near, far = self.l.sides(colour)
            z = self.l.z + step
            self.load(colour, 1, step).wait()
            self.arrive(colour, 1, step)
            mine = self.held.at[colour, 1, z]
            self.total(mine, [mine, self.from_far.at[colour, 1, z]])
            self.send(step, colour, 2, step, near)

        def rest(step, colour):
            near, far = self.l.sides(colour)
            self.send(step, colour, 0, step, far)
            self.load(colour, 0, step).start()

        self.both(distance, run)
        self.both(distance, rest)

    def parts(self, colour, step):
        z = self.l.z + step
        self.load(colour, 0, step).wait()
        self.arrive(colour, 0, step)
        self.arrive(colour, 2, step)
        return [
            self.held.at[colour, 0, z],
            self.from_far.at[colour, 0, z],
            self.from_near.at[colour, z],
        ]

    def line(self, distance):
        l = self.l

        def run(step, colour):
            toward, kind = (1, 3) if step > 0 else (-1, 4)
            z = l.z + step
            behind = l.has(-toward)
            parts = self.parts(colour, step)
            mine = self.held.at[colour, 0, z]

            @pl.when(behind)
            def _():
                self.arrive(colour, kind, step)
                self.total(mine, parts + [self.from_line.at[colour, kind - 3, z]])

            @pl.when(jnp.logical_not(behind))
            def _():
                self.total(mine, parts)

            self.send(step, colour, kind, step, toward)

        self.both(distance, run)

    def finish(self):
        l = self.l
        for colour in (0, 1):
            z = l.z
            parts = self.parts(colour, 0)
            left, right = self.from_line.at[colour, 0, z], self.from_line.at[colour, 1, z]
            target = self.out.at[colour]
            l.when([-1], lambda: self.arrive(colour, 3, 0))
            l.when([1], lambda: self.arrive(colour, 4, 0))
            l.when([-1, 1], lambda: self.total(target, parts + [left, right]))
            pl.when(jnp.logical_not(l.has(-1)))(lambda: self.total(target, parts + [right]))
            pl.when(jnp.logical_not(l.has(1)))(lambda: self.total(target, parts + [left]))

    def free(self):
        for to in ("cy", "cx", -1, 1):

            def tell():
                pl.semaphore_signal(
                    self.credit.at[self.i], inc=1, device_id=self.l.target(to), device_id_type=MESH
                )

            self.l.when([] if to in ("cy", "cx") else [to], tell)

    def freed(self):
        ends = jnp.minimum(self.l.z, 1) + jnp.minimum(self.l.Z - 1 - self.l.z, 1)
        pl.semaphore_wait(self.credit.at[self.i], 2 + ends)
        self.drain()

    def drain(self):
        def one(z, carry):
            step = z - self.l.z
            for colour in (0, 1):
                for kind in (0, 1, 2):
                    self.remote(colour, kind, step, "cx").wait_send()
                pl.when(step != 0)(lambda: self.remote(colour, 3, step, "cx").wait_send())
            return carry

        if not self.drained:
            lax.fori_loop(0, self.l.Z, one, 0)
        self.drained = True

    @staticmethod
    def ticks(works, shared, settle):
        far_first = lambda w, run: [functools.partial(run(w), d) for d in range(w.l.Z - 1, -1, -1)]
        out = [(0, works[0].start)]
        for i, work in enumerate(works):
            out += [(i, t) for t in far_first(work, lambda w: w.near)]
            if i + 1 < len(works):
                if SETS <= i + 1 < shared:
                    out.append((i, works[i + 1 - SETS].freed))
                out.append((i + 1, works[i + 1].start))
            out += [(i, t) for t in far_first(work, lambda w: w.line)[:-1]]
            if i:
                out.append((i - 1, works[i - 1].finish))
                out.append((i - 1, functools.partial(settle, i - 1)))
                if i - 1 + SETS < shared:
                    out.append((i - 1, works[i - 1].free))
        out.append((len(works) - 1, works[-1].finish))
        out.append((len(works) - 1, functools.partial(settle, len(works) - 1)))
        return out


class BackwardOuts(NamedTuple):
    query: Any
    key: Any
    value: Any
    output: Any
    inner: Any
    outer: Any
    small: Any
    frames_grad: Any
    layer_out: Any
    qkv_blocks: Any
    out_blocks: Any
    inner_blocks: Any


class BackwardScratch(NamedTuple):
    dqkv: Any
    own: Any
    away: Any
    got: Any
    acc_k: Any
    acc_v: Any
    norm_v: Any
    half_v: Any
    act_t: Any
    act_sem: Any
    core_credit: Any
    wt: Any
    stage: Any
    stage_o: Any
    part: Any
    part_got: Any
    x_own: Any
    mg_own: Any
    home_out: Any
    home_in: Any
    vec: Any
    small_g: Any
    done: Any
    done_small: Any
    got_small: Any
    done_local: Any
    done_send: Any
    done_recv: Any
    layer_sem: Any
    home_sem: Any
    back_send: Any
    back_recv: Any
    pair_sem: Any
    load: Any
    wt_sem: Any
    stage_sem: Any
    credit: Any
    load_sem: Any
    send_sem: Any
    recv_sem: Any


RATE = 2.0


def backward_kernel(Z, heads, tile, *refs):
    (
        qkv, far, tags_q, tags_k, mixed, logs, grad_in, bg, vectors, small_part, hidden_sums,
        x_rows, middle_grad, normed, w_qkv, active, g_outer, inner_grad, normed_two, w_outer, middle,
    ) = refs[:21]
    n_outs, n_scratch = len(BackwardOuts._fields), len(BackwardScratch._fields)
    o = BackwardOuts(*refs[21 : 21 + n_outs])
    s = BackwardScratch(*refs[21 + n_outs : 21 + n_outs + n_scratch])
    buffers = refs[21 + n_outs + n_scratch :]
    l = Links(Z)
    core, K = l.core, 4 * Z
    width = heads * HD
    rows = qkv.shape[1]
    R = rows // 4
    D = bg.shape[1]
    hw = D // 2
    r2 = D // K
    r = r2 // 2
    f = w_outer.shape[0] // K
    tiles = rows // tile
    groups = heads // GROUP_HEADS
    span = GROUP_HEADS * HD
    scale = HD ** (-0.5)
    factor = scale * math.log2(math.e)

    def block(i, colour, place):
        y, x, z = place
        at = pl.ds(pl.multiple_of(l.index(place) * r2, 16), r2)
        if i < 2:
            first = ((x * Z + z) * 2 + y) * f + colour * (f // 2)
            return g_outer.at[pl.ds(pl.multiple_of(first, 16), f // 2), pl.ds(i * hw, hw)]
        if i < 4:
            return o.inner_blocks.at[at, pl.ds(((i - 2) * 2 + colour) * hw, hw)]
        if i == 4:
            return o.qkv_blocks.at[at, pl.ds(colour * hw, hw)]
        if i == 5:
            if colour == 0:
                return o.qkv_blocks.at[at, pl.ds(2 * hw, hw)]
            return o.out_blocks.at[at, :]
        return s.small_g.at[l.index(place), colour]

    outs = [s.done.at[i] for i in range(6)] + [s.done_small]
    works = [
        Scatter(
            l, i, block, outs[i],
            buffers[4 * (SETS if i == 6 else i % SETS) :][:4],
            (s.load_sem, s.send_sem, s.recv_sem), s.credit,
        )
        for i in range(7)
    ]

    row_tiles = D // 256

    finals = ((o.query, o.key), (o.value, o.output))

    def final_place(i, colour, of_core):
        if i < 2:
            return o.outer.at[pl.ds(colour * (f // 2), f // 2), pl.ds(i * hw, hw)]
        if i < 4:
            first = of_core * 2 * D + ((i - 2) * 2 + colour) * hw
            return o.inner.at[:, pl.ds(pl.multiple_of(first, 128), hw)]
        return finals[i - 4][colour].at[:, pl.ds(pl.multiple_of(of_core * hw, 128), hw)]

    def final_rows(i, colour, which):
        if i < 2:
            return s.done.at[i, colour]
        return s.done.at[i, colour, pl.ds(pl.multiple_of(which * r, 8), r), :]

    def final_keep(i, colour):
        return pltpu.make_async_copy(
            final_rows(i, colour, core), final_place(i, colour, core), s.done_local.at[i, colour]
        )

    def final_give(i, colour):
        return remote(
            final_rows(i, colour, 1 - core), final_place(i, colour, core),
            s.done_send.at[i, colour], s.done_recv.at[i, colour],
            l.target("diagonal" if i < 2 else "core"),
        )

    small_give = lambda: remote(
        s.done_small.at[1 - core], s.got_small,
        s.done_send.at[6, 0], s.done_recv.at[6, 0], l.target("core"),
    )

    def settle(i):
        if i == 6:
            small_give().start()
            return
        for colour in (0, 1):
            keep = lambda: final_keep(i, colour).start()
            give = lambda: final_give(i, colour).start()
            if i < 2:
                pl.when(l.crossed == 0)(keep)
                pl.when(l.crossed == 1)(give)
            else:
                keep()
                give()

    def settled():
        for i in range(6):
            for colour in (0, 1):
                keep = lambda: final_keep(i, colour).wait()

                def give():
                    final_give(i, colour).wait_send()
                    final_give(i, colour).wait_recv()

                if i < 2:
                    pl.when(l.crossed == 0)(keep)
                    pl.when(l.crossed == 1)(give)
                else:
                    keep()
                    give()
        small_give().wait_recv()
        o.small[...] = s.done_small[core] + s.got_small[...]
        small_give().wait_send()

    def layer_swap(p):
        part = pl.ds(p * (R // PARTS), R // PARTS)
        return remote(
            s.x_own.at[1 - l.half, part, :], o.layer_out.at[l.half, 0, part, :],
            s.home_sem.at[2, p], s.home_sem.at[3, p], l.target("swap"),
        )

    layer_store = lambda: pltpu.make_async_copy(
        s.x_own.at[l.half], o.layer_out.at[l.half, 0], s.layer_sem.at[2]
    )

    def back_copy(g, which):
        at = pl.ds(which * width + g * span, span)
        return remote(
            s.away.at[at], s.got.at[at],
            s.back_send.at[g, which], s.back_recv.at[g, which], l.target("pair"),
        )

    def send_back(g, which):
        back_copy(g, which).start()

    def add_back(g):
        for which in (0, 1):
            back_copy(g, which).wait_recv()
            for h in range(GROUP_HEADS):
                at = which * width + g * span + h * HD
                s.dqkv[pl.ds(width + at, HD), :] = (
                    s.own[pl.ds(at, HD), :] + s.got[pl.ds(at, HD), :].astype(wide)
                ).astype(low)

    def row_load(h, which):
        source, target = ((x_rows, s.x_own), (middle_grad, s.mg_own), (middle, s.mg_own))[which]
        return pltpu.make_async_copy(
            source.at[h * 2 + core], target.at[h], s.load.at[h * 3 + which]
        )

    def norm_load(which):
        return pltpu.make_async_copy(
            (normed_two, normed)[which], s.norm_v, s.load.at[6 + which]
        )

    def half_load(which):
        columns = pl.ds(which * D, D)
        return pltpu.make_async_copy(
            inner_grad.at[:, columns], s.half_v, s.load.at[9 + which]
        )

    hidden_tiles = 4 * hw // 256

    def act_load(index):
        slot = lax.rem(index, 2)
        at = pl.ds(pl.multiple_of(index * 256, 256), 256)
        return pltpu.make_async_copy(active.at[:, at], s.act_t.at[slot], s.act_sem.at[slot])

    def outer_load(c):
        at = pl.ds(pl.multiple_of(c * 256, 256), 256)
        slot = lax.rem(c, 2)
        return pltpu.make_async_copy(
            w_outer.at[at, :], s.wt.at[slot, :, pl.ds(0, D)], s.wt_sem.at[slot]
        )

    def wt_load(c):
        at = pl.ds(pl.multiple_of(c * 256, 256), 256)
        slot = lax.rem(c, 2)
        return pltpu.make_async_copy(w_qkv.at[at, :], s.wt.at[slot], s.wt_sem.at[slot])

    def stage_copy(c, which):
        slot = lax.rem(c, 2)
        if which < 2:
            at = pl.ds(pl.multiple_of(c * 256, 256), 256)
            source = (s.stage.at[slot], s.stage_o.at[slot])[which]
            target = (o.qkv_blocks, o.out_blocks)[which].at[at, :]
        else:
            at = pl.ds(pl.multiple_of(lax.rem(c, row_tiles) * 256, 256), 256)
            columns = pl.ds(pl.multiple_of(lax.div(c, row_tiles) * D, 128), D)
            source, target = s.stage.at[slot, :, pl.ds(0, D)], o.inner_blocks.at[at, columns]
        return pltpu.make_async_copy(source, target, s.stage_sem.at[which, slot])

    def drained(which, steps):
        for c in (steps - 2, steps - 1):
            stage_copy(c, which).wait()

    def part_copy(h, turn):
        return remote(
            s.part.at[h, 1 - core], s.part_got.at[h],
            s.pair_sem.at[turn, h], s.pair_sem.at[turn, 2 + h], l.target("core"),
        )

    def home_copy(p):
        part = pl.ds(p * (R // PARTS), R // PARTS)
        return remote(
            s.home_out.at[part, :], s.home_in.at[part, :],
            s.home_sem.at[0, p], s.home_sem.at[1, p], l.target("swap"),
        )

    def home_store(h):
        return pltpu.make_async_copy(s.mg_own.at[h], o.frames_grad.at[h, 0], s.load.at[11 + h])

    def attend(index):
        head, part = index // tiles, lax.rem(index, tiles)
        row = head * HD
        columns = pl.ds(pl.multiple_of(part * tile, tile), tile)

        def feature(base):
            return pl.ds(pl.multiple_of(base + row, 16), HD)

        head_query = qkv[feature(0), columns]
        grad = grad_in[feature(0), columns]
        query = jnp.concatenate([head_query, tags_q[:, columns]], axis=0)
        attended = mixed[feature(core * width), columns]
        delta = jnp.sum(grad.astype(wide) * attended.astype(wide), axis=0, keepdims=True)
        log_row = logs[head, :, columns]
        query_rows = head_query.T
        grad_rows = grad.T
        dq = jnp.zeros((HD, tile), wide)

        @pl.when(part == 0)
        def _():
            s.acc_k[...] = jnp.zeros_like(s.acc_k)
            s.acc_v[...] = jnp.zeros_like(s.acc_v)

        keys = (qkv[feature(width), :], far[feature(0), :])
        values = (qkv[feature(2 * width), :], far[feature(width), :])
        for b in (0, 1):
            key = jnp.concatenate([keys[b], tags_k[b]], axis=0)
            probs = jnp.exp2(dims(key, query, 0, 0) * factor - log_row)
            grad_probs = dims(values[b], grad, 0, 0)
            score_grad = (probs * (grad_probs - delta)).astype(low)
            s.acc_v[b] += dims(probs.astype(low), grad_rows, 1, 0)
            s.acc_k[b] += dims(score_grad, query_rows, 1, 0)
            dq = dq + dims(keys[b], score_grad, 1, 0)
        s.dqkv[feature(0), columns] = (dq * scale).astype(low)

        @pl.when(part == tiles - 1)
        def _():
            s.own[feature(0), :] = s.acc_k[0].T * scale
            s.own[feature(width), :] = s.acc_v[0].T
            s.away[feature(0), :] = (s.acc_k[1].T * scale).astype(low)
            s.away[feature(width), :] = s.acc_v[1].T.astype(low)

    own_cols = pl.ds(pl.multiple_of(core * hw, 128), hw)

    def staged(c, which, value):
        @pl.when(c >= 2)
        def _():
            stage_copy(c - 2, which).wait()

        if which == 2:
            s.stage[lax.rem(c, 2), :, 0:D] = value.astype(low)
        else:
            (s.stage, s.stage_o)[which][lax.rem(c, 2)] = value.astype(low)
        stage_copy(c, which).start()

    def out_part(c):
        @pl.when(c + 1 < hidden_tiles)
        def _():
            act_load(c + 1).start()
            outer_load(c + 1).start()

        act_load(c).wait()
        outer_load(c).wait()
        slot = lax.rem(c, 2)
        for h in (0, 1):
            value = dims(s.act_t[slot, pl.ds(h * 2 * R, 2 * R), :], s.wt[slot, :, 0:D], 1, 0)
            for q in (0, 1):
                s.part[h, q] = jnp.where(c == 0, 0.0, s.part[h, q]) + value[q * R : (q + 1) * R]

    def inner_step(index):
        c = lax.rem(index, row_tiles)
        at = pl.ds(pl.multiple_of(c * 256, 256), 256)
        staged(index, 2, dims(s.norm_v[:, at], s.half_v[...], 0, 0))

    def layer_parts():
        for h in (0, 1):
            part_copy(h, 0).start()
        for h in (0, 1):
            row_load(h, 2).wait()
            part_copy(h, 0).wait_recv()
            s.x_own[h] = (
                s.mg_own[h] + (s.part[h, core] + s.part_got[h] + vectors[3:4, :])
            ).astype(low)
            row_load(h, 1).start()
        for h in (0, 1):
            part_copy(h, 0).wait_send()
        pl.semaphore_signal(
            s.core_credit.at[0], inc=1, device_id=l.target("core"), device_id_type=MESH
        )
        layer_store().start()

    def layer_sent():
        layer_store().wait()
        for p in range(PARTS):
            layer_swap(p).wait_send()
        for h in (0, 1):
            row_load(h, 0).start()

    def out_grad(c):
        at = pl.ds(pl.multiple_of(c * 256, 256), 256)
        staged(c, 1, dims(mixed[at, :], bg[:, own_cols], 1, 0))

    def qkv_grad(c):
        at = pl.ds(pl.multiple_of(c * 256, 256), 256)
        staged(c, 0, dims(s.norm_v[:, at], s.dqkv[...], 0, 1))

    def norm_grad(index):
        c, h = index // 2, lax.rem(index, 2)

        @pl.when(h == 0)
        def _():
            @pl.when(c + 1 < row_tiles)
            def _():
                wt_load(c + 1).start()

            wt_load(c).wait()

        columns = pl.ds(pl.multiple_of(h * 2 * R, 128), 2 * R)
        value = dims(s.wt[lax.rem(c, 2)], s.dqkv[:, columns], 1, 0).T
        at = pl.ds(pl.multiple_of(c * 256, 256), 256)
        s.part[h, 0, :, at] = value[:R]
        s.part[h, 1, :, at] = value[R:]

    def frame_grad(h):
        grad = s.part[h, core] + s.part_got[h]
        xhat, inverse = row_stats(s.x_own[h].astype(wide))
        s.mg_own[h] = s.mg_own[h] + norm_pull(grad, vectors[4:5, :], xhat, inverse)
        s.vec[4:5, :] += jnp.sum(grad * xhat, axis=0, keepdims=True)
        s.vec[5:6, :] += jnp.sum(grad, axis=0, keepdims=True)

    def bias_sums():
        s.vec[...] = small_part[...]
        ones = jnp.ones((8, rows), low)
        s.vec[0:1, own_cols] = dims(ones, s.dqkv[pl.ds(0, hw), :], 1, 1)[0:1]
        s.vec[1:2, own_cols] = dims(ones, s.dqkv[pl.ds(2 * hw, hw), :], 1, 1)[0:1]

    def rows_home():
        s.home_out[...] = s.mg_own[1 - l.half].astype(low)
        for p in range(PARTS):
            home_copy(p).start()
        home_store(l.half).start()

    def pack():
        s.small_g[...] = jnp.zeros_like(s.small_g)
        for k in range(K):
            for q in (0, 1):
                d = 2 * k + q
                s.small_g[k, q, 0:8, 0:r] = s.vec[:, d * r : (d + 1) * r].astype(low)
                for j in range(f // r):
                    at = d * f + j * r
                    s.small_g[k, q, 8 + j : 9 + j, 0:r] = hidden_sums[:, at : at + r].astype(low)

    l.barrier("core", "swap", "diagonal")
    act_load(0).start()
    norm_load(0).start()
    half_load(0).start()
    for h in (0, 1):
        row_load(h, 2).start()
    outer_load(0).start()
    attends = heads * tiles
    layer_at = lambda p: (lambda: layer_swap(p).start())
    work = []
    for step in range(attends):
        work.append(None)
        if step % 3 == 2 and step >= GROUP_HEADS * tiles - 1:
            half_group = step // 3 - 1
            work.append(functools.partial(send_back, half_group // 2, half_group % 2))
    work += [functools.partial(send_back, groups - 1, 1)]
    work += [lambda: norm_load(0).wait(), lambda: half_load(0).wait()]
    work += [None] * row_tiles
    work += [lambda: half_load(1).start(), lambda: half_load(1).wait()]
    inner_ready = len(work) + 2
    work += [None] * row_tiles + [functools.partial(drained, 2, 2 * row_tiles)]
    inner_done = len(work)
    work += [lambda: norm_load(1).start()]
    work += [None] * hidden_tiles + [layer_parts, lambda: wt_load(0).start(), layer_at(0)]
    work += [None] * row_tiles + [layer_at(1)]
    work += [functools.partial(add_back, g) for g in range(groups)] + [bias_sums]
    work += [lambda: norm_load(1).wait()] + [None] * row_tiles + [layer_at(2)]
    work += [functools.partial(drained, 0, row_tiles), functools.partial(drained, 1, row_tiles)]
    qkv_ready = len(work)
    work += [None] * row_tiles + [layer_at(3)] + [None] * row_tiles + [layer_sent]

    def exchange_parts():
        pl.semaphore_wait(s.core_credit.at[0], 1)
        for h in (0, 1):
            part_copy(h, 1).start()
        for h in (0, 1):
            for which in (0, 1):
                row_load(h, which).wait()
        for h in (0, 1):
            part_copy(h, 1).wait_recv()

    work.append(exchange_parts)
    work += [None] * 2 + [rows_home, pack]

    ticks = Scatter.ticks(works, 6, settle)
    plan, now, done = {}, 0, 0
    starts = 0
    for j, (i, tick) in enumerate(ticks):
        need = int(j * RATE)
        for ready, first in enumerate((inner_ready, inner_done, qkv_ready)):
            if tick == works[ready + 2].start:
                need = max(need, first)
        if tick == works[6].start:
            need = len(work)
        while done < min(need, len(work)):
            if work[done] is None:
                now += 1
            else:
                plan.setdefault(now, []).append(work[done])
            done += 1
        plan.setdefault(now, []).append(tick)
    end = len([w for w in work if w is None])

    n0 = attends
    h0 = n0 + 2 * row_tiles
    o0 = h0 + hidden_tiles
    q0 = o0 + row_tiles
    d0 = q0 + row_tiles
    e0 = d0 + 2 * row_tiles

    def one(step, carry):
        for when in sorted(plan):
            if when < end:

                def run():
                    for tick in plan[when]:
                        tick()

                pl.when(step == when)(run)
        inside = lambda lo, n: jnp.logical_and(step >= lo, step < lo + n)
        pl.when(step < n0)(lambda: attend(step))
        pl.when(inside(n0, 2 * row_tiles))(lambda: inner_step(step - n0))
        pl.when(inside(h0, hidden_tiles))(lambda: out_part(step - h0))
        pl.when(inside(o0, row_tiles))(lambda: out_grad(step - o0))
        pl.when(inside(q0, row_tiles))(lambda: qkv_grad(step - q0))
        pl.when(inside(d0, 2 * row_tiles))(lambda: norm_grad(step - d0))
        pl.when(inside(e0, 2))(lambda: frame_grad(step - e0))
        return carry

    lax.fori_loop(0, end, one, 0)
    for tick in plan.get(end, []):
        tick()
    for p in range(PARTS):
        home_copy(p).wait_recv()
    home_store(l.half).wait()
    s.mg_own[1 - l.half] = s.home_in[...].astype(wide)
    home_store(1 - l.half).start()
    for w in works:
        w.drain()
    for g in range(groups):
        for which in (0, 1):
            back_copy(g, which).wait_send()
    for h in (0, 1):
        part_copy(h, 1).wait_send()
    for p in range(PARTS):
        home_copy(p).wait_send()
    home_store(1 - l.half).wait()
    for p in range(PARTS):
        layer_swap(p).wait_recv()
    settled()


def backward_linked(resident, streamed, Z, heads, tile):
    K = 4 * Z
    qkv_t = resident[0]
    rows = qkv_t.shape[1]
    R = rows // 4
    D = resident[7].shape[1]
    hw = D // 2
    r2 = D // K
    groups = heads // GROUP_HEADS
    shape = jax.ShapeDtypeStruct
    dma = pltpu.SemaphoreType.DMA
    outs = BackwardOuts(
        query=shape((r2 // 2, D), wide),
        key=shape((r2 // 2, D), wide),
        value=shape((r2 // 2, D), wide),
        output=shape((r2 // 2, D), wide),
        inner=shape((r2 // 2, 4 * D), wide),
        outer=shape((2 * r2, D), wide),
        small=shape((16, 128), wide),
        frames_grad=shape((2, 1, R, D), wide),
        layer_out=shape((2, 1, R, D), low),
        qkv_blocks=shape((D, 3 * hw), low),
        out_blocks=shape((D, hw), low),
        inner_blocks=shape((D, 4 * hw), low),
    )
    scratch = [
        pltpu.VMEM((3 * hw, rows), low),
        pltpu.VMEM((2 * hw, rows), wide),
        pltpu.VMEM((2 * hw, rows), low),
        pltpu.VMEM((2 * hw, rows), low),
        pltpu.VMEM((2, rows, HD), wide),
        pltpu.VMEM((2, rows, HD), wide),
        pltpu.VMEM((rows, D), low),
        pltpu.VMEM((rows, D), low),
        pltpu.VMEM((2, rows, 256), low),
        dma((2,)),
        pltpu.SemaphoreType.REGULAR((1,)),
        pltpu.VMEM((2, 256, 3 * hw), low),
        pltpu.VMEM((2, 256, 3 * hw), low),
        pltpu.VMEM((2, 256, hw), low),
        pltpu.VMEM((2, 2, R, D), wide),
        pltpu.VMEM((2, R, D), wide),
        pltpu.VMEM((2, R, D), low),
        pltpu.VMEM((2, R, D), wide),
        pltpu.VMEM((R, D), low),
        pltpu.VMEM((R, D), low),
        pltpu.VMEM((8, D), wide),
        pltpu.VMEM((K, 2, 16, 128), low),
        pltpu.VMEM((6, 2, r2, hw), wide),
        pltpu.VMEM((2, 16, 128), wide),
        pltpu.VMEM((16, 128), wide),
        dma((6, 2)),
        dma((7, 2)),
        dma((7, 2)),
        dma((3,)),
        dma((4, PARTS)),
        dma((groups, 2)),
        dma((groups, 2)),
        dma((2, 4)),
        dma((13,)),
        dma((2,)),
        dma((4, 2)),
        pltpu.SemaphoreType.REGULAR((SETS,)),
        dma((7, 2, 2 * Z)),
        dma((7, 2, 4 * Z)),
        dma((7, 2, 5 * Z)),
    ]
    for block in ((r2, hw),) * SETS + ((16, 128),):
        scratch += [pltpu.VMEM((2,) + lead + block, low) for lead in ((2, Z), (2, Z), (Z,), (2, Z))]
    results = pl.pallas_call(
        functools.partial(backward_kernel, Z, heads, tile),
        out_shape=tuple(outs),
        in_specs=full(len(resident)) + full(len(streamed), pl.ANY),
        out_specs=tuple(full(6, pl.ANY) + full(1) + full(5, pl.ANY)),
        scratch_shapes=scratch,
        compiler_params=pltpu.CompilerParams(
            collective_id=1, has_side_effects=True, vmem_limit_bytes=67043328
        ),
    )(*resident, *streamed)
    return BackwardOuts(*results)


def general_body(
    n_chip_rows,
    Z,
    frames,
    clip_ids,
    query_weight,
    key_weight,
    value_weight,
    output_weight,
    inner_weight,
    outer_weight,
    query_bias,
    value_bias,
    output_bias,
    inner_bias,
    outer_bias,
    first_gain,
    first_shift,
    second_gain,
    second_shift,
    out_cotangent,
):
    K = n_chip_rows * Z
    R, D = frames.shape[2], frames.shape[3]
    FF = inner_weight.shape[1]
    r = query_weight.shape[0]
    f = outer_weight.shape[0]
    hw = D // 2
    heads = H // 2
    half = Z // 2
    core = lax.axis_index("core")
    first_core = core == 0
    zz = lax.axis_index("zz")
    micro = zz // half
    first_half = micro == 0
    place = zz % half

    def swap_core(v):
        return lax.ppermute(v, "core", [(0, 1), (1, 0)])

    def swap_half(v):
        return lax.ppermute(v, "zz", [(z, (z + half) % Z) for z in range(Z)])

    def by_core(own, other, axis):
        return jnp.where(
            first_core,
            jnp.concatenate([own, other], axis),
            jnp.concatenate([other, own], axis),
        )

    def pick(v, index, axis):
        return lax.dynamic_index_in_dim(v, index, axis, keepdims=False)

    def take_rows(v):
        v = v[:, 0]
        own, away = pick(v, micro, 0), pick(v, 1 - micro, 0)
        got = swap_half(away)
        pair = jnp.where(first_half, jnp.stack([own, got]), jnp.stack([got, own]))
        both = by_core(pair[:, None], swap_core(pair)[:, None], 1)
        return both.reshape(4 * R, D)

    qkv = jnp.stack([query_weight, key_weight, value_weight], 1).reshape(r, 3, 2, hw)
    inner_split = inner_weight.reshape(r, K, 2, f)
    vectors = (
        query_bias, value_bias, output_bias, outer_bias,
        first_gain, first_shift, second_gain, second_shift, inner_bias,
    )
    small = jnp.concatenate(vectors)
    n_small = small.shape[0]

    def column_half(which):
        return jnp.concatenate(
            [
                pick(qkv, which, 2).reshape(r, 3 * hw),
                pick(inner_split, which, 2).reshape(r, FF // 2),
            ],
            1,
        )

    mine = column_half(core)
    theirs = swap_core(column_half(1 - core))
    both = by_core(mine[None], theirs[None], 0)
    small_both = by_core(small[None], swap_core(small)[None], 0)
    small_pad = -(-n_small // 1024) * 1024
    small_both = jnp.pad(small_both, ((0, 0), (0, small_pad - n_small)))
    shards = (
        small_both.reshape(2, small_pad // 128, 128),
        both[:, :, : 3 * hw],
        output_weight.reshape(r, 2, hw).transpose(1, 0, 2),
        both[:, :, 3 * hw :],
        outer_weight.reshape(2, f // 2, D),
    )
    small_all, qkv_all, out_all, inner_all, outer_all = (
        lax.all_gather(v, CHIPS, axis=0, tiled=False) for v in shards
    )
    x_rows = take_rows(frames)
    cot = take_rows(out_cotangent)

    w_qkv = qkv_all.reshape(D, 3 * hw)
    w_inner = inner_all.reshape(D, FF // 2)
    w_outer = outer_all.reshape(FF // 2, D)
    out_own = out_all.transpose(0, 2, 1, 3).reshape(K, 1, r, D)
    w_out = by_core(out_own, swap_core(out_own), 1).reshape(D, D)
    small_all = small_all.reshape(K, 2, small_pad)[:, :, :n_small].astype(wide)
    names = ("qb", "vb", "ob", "ub", "g1", "s1", "g2", "s2")
    vec = {n: small_all[:, :, i * r : (i + 1) * r].reshape(D) for i, n in enumerate(names)}
    ib_half = pick(small_all[:, :, 8 * r :], core, 1).reshape(FF // 2)

    def own_columns(v):
        return lax.dynamic_slice_in_dim(v, core * hw, hw, v.ndim - 1)

    ids = pick(clip_ids[:, 0], micro, 0).reshape(2, half, 2 * R)
    ids_q = pick(ids, place, 1).reshape(4 * R)
    order = (place - jnp.arange(half)) % half
    ids_k = jnp.take(ids, order, axis=1).transpose(1, 0, 2).reshape(half, 4 * R)
    tag = jnp.arange(TAGS, dtype=jnp.int32)[:, None]
    tags_q = jnp.where(ids_q[None, :] == tag, 0.0, masked_score).astype(low)
    tags_k = (ids_k[:, None, :] == tag[None]).astype(low)

    xf = x_rows.astype(wide)
    xhat, inverse = row_stats(xf)
    normed = (xhat * vec["g1"] + vec["s1"]).astype(low)
    bias_qkv = jnp.concatenate(
        [own_columns(vec["qb"]), jnp.zeros((hw,), wide), own_columns(vec["vb"])]
    )
    qkv_t = (dims(w_qkv, normed, 0, 1) + bias_qkv[:, None]).astype(low)
    q_t, kv_own = qkv_t[:hw], qkv_t[hw:]
    kv_parts = [kv_own]
    for o in range(1, half):
        kv_parts.append(
            lax.ppermute(
                kv_own, "zz", [(z, (z // half) * half + (z + o) % half) for z in range(Z)]
            )
        )
    kv = jnp.stack(kv_parts)
    tile = 256
    mixed_t, logs = attend_forward(q_t, tags_q, kv, tags_k, heads, tile)
    mixed_full = by_core(mixed_t, swap_core(mixed_t), 0)
    middle = xf + (dims(mixed_full, w_out, 0, 0) + vec["ob"])
    xhat_two, inverse_two = row_stats(middle)
    normed_two = (xhat_two * vec["g2"] + vec["s2"]).astype(low)
    inner = dims(normed_two, w_inner, 1, 0) + ib_half
    active, slope = gelu_parts(inner)
    active = active.astype(low)
    out_part = dims(active, w_outer, 1, 0)

    def split_rows(v):
        return v.reshape(2, 2, R, D)

    def reduce_rows(v):
        v = split_rows(v)
        return pick(v, core, 1) + swap_core(pick(v, 1 - core, 1).astype(low)).astype(wide)

    def home_rows(v):
        stay = pick(v, micro, 0)
        got = swap_half(pick(v, 1 - micro, 0))
        return jnp.where(first_half, jnp.stack([stay, got]), jnp.stack([got, stay]))[:, None]

    own_middle = pick(split_rows(middle), core, 1)
    layer_rows = (own_middle + (reduce_rows(out_part) + vec["ub"])).astype(low)
    layer_out = home_rows(layer_rows)

    grad_active = dims(cot, w_outer, 1, 1)
    inner_grad = (grad_active * slope).astype(low)
    part_two = dims(inner_grad, w_inner, 1, 1)
    grad_two = part_two + swap_core(part_two.astype(low)).astype(wide)
    middle_grad = cot.astype(wide) + norm_pull(grad_two, vec["g2"], xhat_two, inverse_two)
    branch_grad = middle_grad.astype(low)
    w_out_heads = lax.dynamic_slice_in_dim(w_out, core * hw, hw, 0)
    mixed_grad = dims(w_out_heads, branch_grad, 1, 1).astype(low)
    dq_t, own_kv, far_kv = attend_backward(
        q_t, tags_q, kv, tags_k, mixed_t, logs, mixed_grad, heads, tile
    )
    dkv = own_kv.reshape(2 * hw, 4 * R)
    for o in range(1, half):
        back = lax.ppermute(
            far_kv[o - 1], "zz", [(z, (z // half) * half + (z - o) % half) for z in range(Z)]
        )
        dkv = dkv + back.reshape(2 * hw, 4 * R).astype(wide)
    dqkv_t = jnp.concatenate([dq_t, dkv.astype(low)], 0)
    grad_one = reduce_rows(dims(dqkv_t, w_qkv, 0, 1))
    own_xhat = pick(split_rows(xhat), core, 1)
    own_inverse = pick(inverse.reshape(2, 2, R, 1), core, 1)
    frame_rows = pick(split_rows(middle_grad), core, 1) + norm_pull(
        grad_one, vec["g1"], own_xhat, own_inverse
    )
    sent = swap_half(pick(frame_rows, 1 - micro, 0).astype(low)).astype(wide)
    stay = pick(frame_rows, micro, 0)
    frames_grad = jnp.where(first_half, jnp.stack([stay, sent]), jnp.stack([sent, stay]))[:, None]

    g_qkv = dims(normed, dqkv_t, 0, 1).astype(low)
    g_out = dims(mixed_full, own_columns(branch_grad), 1, 0).astype(low)
    g_inner = dims(normed_two, inner_grad, 0, 0).astype(low)
    g_outer = dims(active, cot, 0, 0).astype(low)

    def zero_rest(v):
        return by_core(v, jnp.zeros_like(v), 0)

    bias_sums = jnp.sum(dqkv_t.astype(wide), axis=1)
    halves = 0.5
    col = {
        "qb": zero_rest(bias_sums[:hw]),
        "vb": zero_rest(bias_sums[2 * hw :]),
        "ob": halves * jnp.sum(branch_grad.astype(wide), 0),
        "ub": halves * jnp.sum(cot.astype(wide), 0),
        "g1": jnp.sum(grad_one * own_xhat, (0, 1)),
        "s1": jnp.sum(grad_one, (0, 1)),
        "g2": halves * jnp.sum(grad_two * xhat_two, 0),
        "s2": halves * jnp.sum(grad_two, 0),
    }
    ib_sum = jnp.sum(inner_grad.astype(wide), 0).reshape(K, 1, f)
    small_grad = jnp.concatenate(
        [col[n].reshape(K, 2, r) for n in names]
        + [by_core(ib_sum, jnp.zeros_like(ib_sum), 1)],
        2,
    )
    small_grad = jnp.pad(small_grad, ((0, 0), (0, 0), (0, small_pad - n_small)))
    small_grad = small_grad.reshape(K, 2, small_pad // 128, 128).astype(low)
    g_outer, g_inner, g_out, g_qkv, g_small = (
        lax.psum_scatter(v, CHIPS, scatter_dimension=0, tiled=False).astype(wide)
        for v in (
            g_outer.reshape(K, 2, f // 2, D),
            g_inner.reshape(K, 2, r, FF // 2),
            g_out.reshape(K, 2, r, hw),
            g_qkv.reshape(K, 2, r, 3 * hw),
            small_grad,
        )
    )
    wide_rows = jnp.concatenate([g_qkv, g_out, g_inner], 2)
    mine = pick(wide_rows, core, 0)
    theirs = swap_core(pick(wide_rows, 1 - core, 0))

    def whole(a, b, parts):
        a, b = a.reshape(r, parts, 1, -1), b.reshape(r, parts, 1, -1)
        return by_core(a, b, 2).reshape(r, -1)

    outs = []
    for i in range(4):
        outs.append(whole(mine[:, i * hw : (i + 1) * hw], theirs[:, i * hw : (i + 1) * hw], 1))
    outs.append(whole(mine[:, 4 * hw :], theirs[:, 4 * hw :], K))
    outs.append(g_outer.reshape(f, D))
    g_small = g_small.reshape(2, small_pad)[:, :n_small]
    g_small = pick(g_small, core, 0) + swap_core(pick(g_small, 1 - core, 0))
    sv = {n: g_small[i * r : (i + 1) * r] for i, n in enumerate(names)}
    return (layer_out, frames_grad) + tuple(outs) + (
        sv["qb"], sv["vb"], sv["ob"], g_small[8 * r :], sv["ub"],
        sv["g1"], sv["s1"], sv["g2"], sv["s2"],
    )


VECTORS = ("qb", "vb", "ob", "ub", "g1", "s1", "g2", "s2")


def linked_body(
    Z,
    frames,
    clip_ids,
    query_weight,
    key_weight,
    value_weight,
    output_weight,
    inner_weight,
    outer_weight,
    query_bias,
    value_bias,
    output_bias,
    inner_bias,
    outer_bias,
    first_gain,
    first_shift,
    second_gain,
    second_shift,
    out_cotangent,
):
    K = 4 * Z
    R, D = frames.shape[2], frames.shape[3]
    FF = inner_weight.shape[1]
    r = query_weight.shape[0]
    f = outer_weight.shape[0]
    hw = D // 2
    heads = H // 2
    half = Z // 2
    core = lax.axis_index("core")
    first_core = core == 0
    zz = lax.axis_index("zz")
    micro = zz // half
    first_half = micro == 0
    place = zz % half
    tile = 256

    def swap_core(v):
        return lax.ppermute(v, "core", [(0, 1), (1, 0)])

    def by_core(own, other, axis):
        return jnp.where(
            first_core,
            jnp.concatenate([own, other], axis),
            jnp.concatenate([other, own], axis),
        )

    def pick(v, index, axis):
        return lax.dynamic_index_in_dim(v, index, axis, keepdims=False)

    def own_columns(v):
        return lax.dynamic_slice_in_dim(v, core * hw, hw, v.ndim - 1)

    small = jnp.concatenate(
        [
            jnp.stack(
                [
                    query_bias, value_bias, output_bias, outer_bias,
                    first_gain, first_shift, second_gain, second_shift,
                ]
            ),
            inner_bias.reshape(f // r, r),
        ]
    )
    small = jnp.pad(small, ((0, 16 - small.shape[0]), (0, 128 - r)))

    ids = pick(clip_ids[:, 0], micro, 0).reshape(2, half, 2 * R)
    ids_q = pick(ids, place, 1).reshape(4 * R)
    ids_far = pick(ids, 1 - place, 1).reshape(4 * R)
    tag = jnp.arange(TAGS, dtype=jnp.int32)[:, None]
    tags_q = jnp.where(ids_q[None, :] == tag, 0.0, masked_score).astype(low)
    tags_k = (jnp.stack([ids_q, ids_far])[:, None, :] == tag[None]).astype(low)

    weights = (query_weight, key_weight, value_weight, output_weight, inner_weight, outer_weight)
    fw = forward_linked(frames, out_cotangent, weights, small, tags_q, tags_k, Z, heads, tile)
    vec = {n: fw.vectors[i] for i, n in enumerate(VECTORS)}
    cot = fw.cot_rows.reshape(4 * R, D)
    active, slope, middle = fw.active, fw.slope, fw.middle
    normed_two = fw.normed_two
    g_outer = dims(active, cot, 0, 0).astype(low)

    grad_active = dims(cot, fw.w_outer, 1, 1)
    inner_grad = (grad_active * slope).astype(low)
    part_two = dims(inner_grad, fw.w_inner, 1, 1)
    grad_two = part_two + swap_core(part_two.astype(low)).astype(wide)
    xhat_two, inverse_two = row_stats(middle)
    middle_grad = cot.astype(wide) + norm_pull(grad_two, vec["g2"], xhat_two, inverse_two)
    branch_grad = middle_grad.astype(low)
    w_heads = lax.dynamic_slice_in_dim(fw.w_out, core * hw, hw, 1)
    mixed_grad = sum(
        dims(w_heads[b], branch_grad[:, b * hw : (b + 1) * hw], 1, 1) for b in (0, 1)
    ).astype(low)
    halves = 0.5
    none = jnp.zeros((D,), wide)
    small_part = jnp.stack(
        [
            none,
            none,
            halves * jnp.sum(branch_grad.astype(wide), 0),
            halves * jnp.sum(cot.astype(wide), 0),
            none,
            none,
            halves * jnp.sum(grad_two * xhat_two, 0),
            halves * jnp.sum(grad_two, 0),
        ]
    )
    hidden_sums = jnp.sum(inner_grad.astype(wide), 0)[None]
    hidden_sums = by_core(hidden_sums, jnp.zeros_like(hidden_sums), 1)
    bw = backward_linked(
        (
            fw.qkv, fw.far, tags_q, tags_k, fw.mixed, fw.logs, mixed_grad, branch_grad,
            fw.vectors, small_part, hidden_sums,
        ),
        (
            fw.x_rows, middle_grad.reshape(4, R, D), fw.normed, fw.w_qkv, active, g_outer, inner_grad,
            normed_two, fw.w_outer, middle.reshape(4, R, D),
        ),
        Z, heads, tile,
    )
    sv = {n: bw.small[i, :r] for i, n in enumerate(VECTORS)}
    ib = bw.small[8 : 8 + f // r, :r].reshape(f)
    return (
        bw.layer_out, bw.frames_grad, bw.query, bw.key, bw.value, bw.output, bw.inner, bw.outer,
        sv["qb"], sv["vb"], sv["ob"], ib, sv["ub"],
        sv["g1"], sv["s1"], sv["g2"], sv["s2"],
    )


def solution(mesh):
    C, S = mesh.shape["clip"], mesh.shape["seq"]
    fine = Mesh(mesh.devices.reshape(2, C // 2, S // 2, 2), ("cy", "cx", "zz", "core"))
    clip, seq = ("cy", "cx"), ("zz", "core")
    every = clip + seq
    rows, mat, vec = P(None, clip, seq, None), P(every, None), P(every)
    in_specs = (rows, P(None, clip, None)) + (mat,) * 6 + (vec,) * 9 + (rows,)
    out_specs = (rows, rows) + (mat,) * 6 + (vec,) * 9
    linked = C == 4 and S == 8
    run = functools.partial(linked_body, S // 2) if linked else functools.partial(general_body, C, S // 2)
    return jax.shard_map(
        run,
        mesh=fine,
        in_specs=in_specs,
        out_specs=out_specs,
        check_vma=False,
    )
```

```python
import functools
import math
from typing import Any, NamedTuple

import jax
import jax.numpy as jnp
from jax import lax
from jax.experimental import pallas as pl
from jax.experimental.pallas import tpu as pltpu
from jax.sharding import Mesh
from jax.sharding import PartitionSpec as P

H = 16
HD = 80
TAGS = 16
epsilon = 1e-05
masked_score = -1e30
low = jnp.bfloat16
wide = jnp.float32


def dims(left_side, right_side, left_dim, right_dim):
    return lax.dot_general(
        left_side,
        right_side,
        (((left_dim,), (right_dim,)), ((), ())),
        preferred_element_type=wide,
    )


def attend_forward_kernel(blocks, q_ref, qa_ref, k_ref, v_ref, ka_ref, out_ref, log_ref):
    factor = HD ** (-0.5) * math.log2(math.e)
    query = jnp.concatenate([q_ref[...], qa_ref[...]], axis=0)
    scores = []
    for b in range(blocks):
        key = jnp.concatenate([k_ref[b], ka_ref[b]], axis=0)
        scores.append(dims(key, query, 0, 0))
    top = functools.reduce(jnp.maximum, [jnp.max(s, axis=0, keepdims=True) for s in scores])
    top = top * factor
    total = jnp.zeros_like(top)
    mixed = jnp.zeros((HD, query.shape[1]), wide)
    for b in range(blocks):
        part = jnp.exp2(scores[b] * factor - top)
        total = total + jnp.sum(part, axis=0, keepdims=True)
        mixed = mixed + dims(v_ref[b], part.astype(low), 1, 0)
    out_ref[...] = (mixed / total).astype(low)
    log_ref[0] = top + jnp.log2(total)


def attend_forward(q_t, tags_q, kv, tags_k, heads, tile):
    blocks, _, width = kv.shape
    rows = q_t.shape[1]
    grid = (heads, rows // tile)
    return pl.pallas_call(
        functools.partial(attend_forward_kernel, blocks),
        grid=grid,
        out_shape=(
            jax.ShapeDtypeStruct((heads * HD, rows), low),
            jax.ShapeDtypeStruct((heads, 1, rows), wide),
        ),
        in_specs=[
            pl.BlockSpec((HD, tile), lambda h, t: (h, t)),
            pl.BlockSpec((TAGS, tile), lambda h, t: (0, t)),
            pl.BlockSpec((blocks, HD, width), lambda h, t: (0, h, 0)),
            pl.BlockSpec((blocks, HD, width), lambda h, t: (0, heads + h, 0)),
            pl.BlockSpec((blocks, TAGS, width), lambda h, t: (0, 0, 0)),
        ],
        out_specs=(
            pl.BlockSpec((HD, tile), lambda h, t: (h, t)),
            pl.BlockSpec((1, 1, tile), lambda h, t: (h, 0, t)),
        ),
        cost_estimate=pl.CostEstimate(
            flops=4 * heads * rows * blocks * width * HD,
            bytes_accessed=2 * kv.size,
            transcendentals=heads * rows * blocks * width,
        ),
    )(q_t, tags_q, kv, kv, tags_k)


def attend_backward_kernel(
    blocks, q_ref, qa_ref, k_ref, v_ref, ka_ref, o_ref, log_ref, g_ref, dq_ref, own_ref, far_ref, acc_k, acc_v
):
    factor = HD ** (-0.5) * math.log2(math.e)
    step, steps = pl.program_id(1), pl.num_programs(1)
    head_query = q_ref[...]
    grad = g_ref[...]
    query = jnp.concatenate([head_query, qa_ref[...]], axis=0)
    delta = jnp.sum(grad.astype(wide) * o_ref[...].astype(wide), axis=0, keepdims=True)
    logs = log_ref[0]
    query_rows = head_query.T
    grad_rows = grad.T
    dq = jnp.zeros(head_query.shape, wide)

    @pl.when(step == 0)
    def _():
        acc_k[...] = jnp.zeros_like(acc_k)
        acc_v[...] = jnp.zeros_like(acc_v)

    for b in range(blocks):
        key = jnp.concatenate([k_ref[b], ka_ref[b]], axis=0)
        probs = jnp.exp2(dims(key, query, 0, 0) * factor - logs)
        grad_probs = dims(v_ref[b], grad, 0, 0)
        score_grad = (probs * (grad_probs - delta)).astype(low)
        acc_v[b] += dims(probs.astype(low), grad_rows, 1, 0)
        acc_k[b] += dims(score_grad, query_rows, 1, 0)
        dq = dq + dims(k_ref[b], score_grad, 1, 0)
    dq_ref[...] = (dq * HD ** (-0.5)).astype(low)

    @pl.when(step == steps - 1)
    def _():
        for b in range(blocks):
            key_part = acc_k[b].T * HD ** (-0.5)
            value_part = acc_v[b].T
            if b == 0:
                own_ref[0] = key_part
                own_ref[1] = value_part
            else:
                far_ref[b - 1, 0] = key_part.astype(low)
                far_ref[b - 1, 1] = value_part.astype(low)


def attend_backward(q_t, tags_q, kv, tags_k, mixed_t, logs, grad_t, heads, tile):
    blocks, _, width = kv.shape
    rows = q_t.shape[1]
    grid = (heads, rows // tile)
    per_query = pl.BlockSpec((HD, tile), lambda h, t: (h, t))
    return pl.pallas_call(
        functools.partial(attend_backward_kernel, blocks),
        grid=grid,
        out_shape=(
            jax.ShapeDtypeStruct((heads * HD, rows), low),
            jax.ShapeDtypeStruct((2, heads * HD, width), wide),
            jax.ShapeDtypeStruct((blocks - 1, 2, heads * HD, width), low),
        ),
        in_specs=[
            per_query,
            pl.BlockSpec((TAGS, tile), lambda h, t: (0, t)),
            pl.BlockSpec((blocks, HD, width), lambda h, t: (0, h, 0)),
            pl.BlockSpec((blocks, HD, width), lambda h, t: (0, heads + h, 0)),
            pl.BlockSpec((blocks, TAGS, width), lambda h, t: (0, 0, 0)),
            per_query,
            pl.BlockSpec((1, 1, tile), lambda h, t: (h, 0, t)),
            per_query,
        ],
        out_specs=(
            per_query,
            pl.BlockSpec((2, HD, width), lambda h, t: (0, h, 0)),
            pl.BlockSpec((blocks - 1, 2, HD, width), lambda h, t: (0, 0, h, 0)),
        ),
        scratch_shapes=[
            pltpu.VMEM((blocks, width, HD), wide),
            pltpu.VMEM((blocks, width, HD), wide),
        ],
        cost_estimate=pl.CostEstimate(
            flops=10 * heads * rows * blocks * width * HD,
            bytes_accessed=4 * kv.size,
            transcendentals=heads * rows * blocks * width,
        ),
    )(q_t, tags_q, kv, kv, tags_k, mixed_t, logs, grad_t)


def row_stats(values):
    centre = jnp.mean(values, axis=-1, keepdims=True)
    centred = values - centre
    inverse = lax.rsqrt(jnp.mean(centred * centred, axis=-1, keepdims=True) + epsilon)
    return centred * inverse, inverse


def norm_pull(grad, gain, xhat, inverse):
    e = grad * gain
    return inverse * (
        e
        - jnp.mean(e, axis=-1, keepdims=True)
        - xhat * jnp.mean(e * xhat, axis=-1, keepdims=True)
    )


def gelu_parts(u):
    phi_sum = 0.5 * (1.0 + lax.erf(u * math.sqrt(0.5)))
    density = jnp.exp(-0.5 * u * u) * (1.0 / math.sqrt(2.0 * math.pi))
    return u * phi_sum, phi_sum + u * density


CHIPS = ("cy", "cx", "zz")
MESH = pl.DeviceIdType.MESH
BIG = 62 * 1024 * 1024


def offsets(Z):
    steps = []
    for d in range(1, Z):
        steps += [-d, d]
    return steps


def full(n, space=pltpu.VMEM):
    return [pl.BlockSpec(memory_space=space)] * n


class Links:
    def __init__(self, Z):
        self.Z = Z
        self.y, self.x, self.z = (lax.axis_index(a) for a in CHIPS)
        self.core = lax.axis_index("core")
        self.half = lax.div(self.z, Z // 2)
        self.crossed = lax.rem(self.y + self.core, 2)

    def sides(self, colour):
        return (("cx", "cy"), ("cy", "cx"))[colour]

    def coords(self, flips, z):
        y = 1 - self.y if "cy" in flips else self.y
        x = 1 - self.x if "cx" in flips else self.x
        return y, x, z

    def index(self, place):
        y, x, z = place
        return (y * 2 + x) * self.Z + z

    def at(self, flips, z):
        return self.index(self.coords(flips, z))

    def target(self, to):
        if not isinstance(to, str):
            return {"zz": self.z + to}
        if to == "cy":
            return {"cy": 1 - self.y}
        if to == "cx":
            return {"cx": 1 - self.x}
        if to == "core":
            return {"core": 1 - self.core}
        if to == "pair":
            return {"zz": self.z + 1 - 2 * lax.rem(self.z, 2)}
        if to == "swap":
            return {"zz": self.z + (self.Z // 2) * (1 - 2 * self.half)}
        if to == "diagonal":
            return {"cy": self.core, "core": self.y}
        raise ValueError(to)

    def each_way(self, distance, run):
        def one(way, carry):
            step = distance * (2 * way - 1)
            pl.when(self.has(step))(lambda: run(step))
            return carry

        if distance:
            lax.fori_loop(0, 2, one, 0)
        else:
            run(0)

    def has(self, step):
        there = self.z + step
        return jnp.logical_and(there >= 0, there < self.Z)

    def when(self, steps, run):
        steps = [s for s in steps if s]
        if steps:
            pl.when(functools.reduce(jnp.logical_and, [self.has(s) for s in steps]))(run)
        else:
            run()

    def barrier(self, *more):
        sem = pltpu.get_barrier_semaphore()
        for to in ("cy", "cx") + tuple(m for m in more if m != "diagonal"):
            pl.semaphore_signal(sem, inc=1, device_id=self.target(to), device_id_type=MESH)
        for step in (-1, 1):

            @pl.when(self.has(step))
            def _():
                pl.semaphore_signal(
                    sem, inc=1, device_id=self.target(step), device_id_type=MESH
                )

        count = 2 + len([m for m in more if m != "diagonal"])
        count = count + jnp.minimum(self.z, 1) + jnp.minimum(self.Z - 1 - self.z, 1)
        if "diagonal" in more:

            @pl.when(self.crossed == 1)
            def _():
                pl.semaphore_signal(
                    sem, inc=1, device_id=self.target("diagonal"), device_id_type=MESH
                )

            count = count + self.crossed
        pl.semaphore_wait(sem, count)


def remote(src, dst, send, recv, to):
    return pltpu.make_async_remote_copy(
        src_ref=src, dst_ref=dst, send_sem=send, recv_sem=recv, device_id=to, device_id_type=MESH
    )


class Gather:
    def __init__(self, links, block, sems):
        self.l, self.block, self.chunks = links, block, 7
        self.send_sem, self.recv_sem = sems

    def copy(self, i, colour, flips, step, base, to):
        place = self.l.coords(flips, self.l.z + step)
        block = self.block(i, colour, place)
        return remote(
            block,
            block,
            self.send_sem.at[i, colour, base + self.l.z + step],
            self.recv_sem.at[i, colour, self.l.index(place)],
            self.l.target(to),
        )

    def send(self, steps, *what):
        self.l.when(steps, lambda: self.copy(*what).start())

    def arrive(self, i, colour, flips, step):
        self.l.when([step], lambda: self.copy(i, colour, flips, step, 0, "cx").wait_recv())

    def own(self, i):
        for colour in (0, 1):
            for step, base in ((1, 0), (-1, self.l.Z)):
                self.send([step], i, colour, (), 0, base, step)

    def along(self, i, distance):
        def run(step):
            toward = lax.div(step, distance)
            base = lax.div(1 + toward, 2) * self.l.Z
            for colour in (0, 1):
                self.copy(i, colour, (), step, 0, "cx").wait_recv()

                @pl.when(self.l.has(-toward))
                def _():
                    self.copy(i, colour, (), step, base, -toward).start()

        self.l.each_way(distance, run)

    def aside(self, i, distance):
        def run(step):
            for colour in (0, 1):
                near, far = self.l.sides(colour)
                self.copy(i, colour, (), step, 2 * self.l.Z, near).start()
                self.copy(i, colour, (), step, 3 * self.l.Z, far).start()

        self.l.each_way(distance, run)

    def across(self, i, distance):
        def run(step):
            for colour in (0, 1):
                near, far = self.l.sides(colour)
                self.copy(i, colour, (near,), step, 0, "cx").wait_recv()
                self.copy(i, colour, (near,), step, 4 * self.l.Z, far).start()

        self.l.each_way(distance, run)

    def last(self, i):
        def one(z, carry):
            for colour in (0, 1):
                near, far = self.l.sides(colour)
                for flips in ((far,), (far, near)):
                    self.copy(i, colour, flips, z - self.l.z, 0, "cx").wait_recv()
            return carry

        lax.fori_loop(0, self.l.Z, one, 0)

    def drain(self):
        l, Z = self.l, self.l.Z

        def sent(i, like, z):
            for colour in (0, 1):
                block = self.block(like, colour, l.coords((), l.z))

                def wait(slot):
                    remote(
                        block, block, self.send_sem.at[i, colour, slot],
                        self.recv_sem.at[i, colour, 0], l.target("cx"),
                    ).wait_send()

                for base in (2, 3, 4):
                    wait(base * Z + z)
                pl.when(jnp.logical_and(z <= l.z, l.z + 1 < Z))(lambda: wait(z))
                pl.when(jnp.logical_and(z >= l.z, l.z > 0))(lambda: wait(Z + z))

        def one(index, carry):
            sent(1 + lax.div(index, Z), 1, lax.rem(index, Z))
            return carry

        def small(z, carry):
            sent(0, 0, z)
            return carry

        lax.fori_loop(0, Z, small, 0)
        lax.fori_loop(0, (self.chunks - 1) * Z, one, 0)

    @staticmethod
    def semaphores(n, Z):
        return [
            pltpu.SemaphoreType.DMA((n, 2, 5 * Z)),
            pltpu.SemaphoreType.DMA((n, 2, 4 * Z)),
        ]


GROUP_HEADS = 2
PARTS = 4
class ForwardOuts(NamedTuple):
    vectors: Any
    w_qkv: Any
    w_out: Any
    w_inner: Any
    w_outer: Any
    cot_rows: Any
    x_rows: Any
    normed: Any
    qkv: Any
    far: Any
    mixed: Any
    logs: Any
    middle: Any
    normed_two: Any
    active: Any
    slope: Any


class ForwardScratch(NamedTuple):
    small_all: Any
    hidden_bias: Any
    x: Any
    norm_v: Any
    qkv_v: Any
    far_v: Any
    mix_v: Any
    wq_v: Any
    wo_v: Any
    wi_v: Any
    n2_v: Any
    mid_v: Any
    act_v: Any
    slo_v: Any
    cot_own: Any
    local: Any
    core_send: Any
    core_recv: Any
    row_sem: Any
    kv_send: Any
    kv_recv: Any
    mix_send: Any
    mix_recv: Any
    wo_sem: Any
    out_sem: Any
    load_sem: Any
    gather_send: Any
    gather_recv: Any


def norm_rows(values, gain, shift):
    xhat, _ = row_stats(values)
    return (xhat * gain + shift).astype(low)


def forward_kernel(Z, heads, tile, *refs):
    (frames, cot, wq, wk, wv, wo, wi, w2, small, tags_q, tags_k) = refs[:11]
    n_outs = len(ForwardOuts._fields)
    o = ForwardOuts(*refs[11 : 11 + n_outs])
    s = ForwardScratch(*refs[11 + n_outs :])
    l = Links(Z)
    core, K = l.core, 4 * Z
    here = l.at((), l.z)
    r, D = wq.shape
    hw = D // 2
    f = w2.shape[0]
    R = frames.shape[2]
    rows = 4 * R
    width = heads * HD
    tiles = rows // tile
    groups = heads // GROUP_HEADS
    span = GROUP_HEADS * HD
    factor = HD ** (-0.5) * math.log2(math.e)
    vectors = o.vectors

    def natural(place):
        y, x, z = place
        return (x * Z + z) * 2 + y

    def block(i, colour, place):
        k = l.index(place)
        rows80 = pl.ds(pl.multiple_of(k * 2 * r, 16), 2 * r)
        if i == 0:
            return s.small_all.at[k, colour]
        if i == 1:
            return o.w_qkv.at[rows80, pl.ds(colour * hw, hw)]
        if i == 2:
            if colour == 0:
                return o.w_qkv.at[rows80, pl.ds(2 * hw, hw)]
            return o.w_out.at[core, rows80, :]
        if i < 5:
            return o.w_inner.at[rows80, pl.ds(((i - 3) * 2 + colour) * hw, hw)]
        at = natural(place) * f + ((i - 5) * 2 + colour) * (f // 4)
        return o.w_outer.at[pl.ds(pl.multiple_of(at, 8), f // 4), :]

    gather = Gather(l, block, (s.gather_send, s.gather_recv))

    def my_rows():
        return pl.ds(pl.multiple_of(here * 2 * r + core * r, 8), r)

    sources = ((wq, hw), (wk, hw), (wv, hw), (wo, hw), (wi, 2 * D))

    def place_of(m, of_core):
        if m == 3:
            return o.w_out.at[of_core, my_rows(), :]
        if m == 4:
            return o.w_inner.at[my_rows(), :]
        return o.w_qkv.at[my_rows(), pl.ds(m * hw, hw)]

    def keep(m):
        if m == 5:
            return pltpu.make_async_copy(small, s.small_all.at[here, core], s.local.at[m])
        src, cols = sources[m]
        window = pl.ds(pl.multiple_of(core * cols, 128), cols)
        return pltpu.make_async_copy(src.at[:, window], place_of(m, core), s.local.at[m])

    def give(m):
        sems = s.core_send.at[m], s.core_recv.at[m]
        if m == 5:
            return remote(small, s.small_all.at[here, core], *sems, l.target("core"))
        src, cols = sources[m]
        window = pl.ds(pl.multiple_of((1 - core) * cols, 128), cols)
        return remote(src.at[:, window], place_of(m, 1 - core), *sems, l.target("core"))

    outer_rows = pl.ds(pl.multiple_of(((l.x * Z + l.z) * 2 + core) * f, 16), f)

    def outer_keep():
        return pltpu.make_async_copy(w2, o.w_outer.at[outer_rows, :], s.local.at[6])

    def outer_give():
        return remote(
            w2,
            o.w_outer.at[outer_rows, :],
            s.core_send.at[6],
            s.core_recv.at[6],
            l.target("diagonal"),
        )

    def begin(m):
        keep(m).start()
        give(m).start()

    def ready(m):
        keep(m).wait()
        give(m).wait_recv()

    def row_copies(source, target, base):
        m = l.half
        mine, theirs = m * 2 + core, (1 - m) * 2 + core
        swaps = []
        for p in range(PARTS):
            part = pl.ds(p * (R // PARTS), R // PARTS)
            swaps.append(
                remote(
                    source.at[1 - m, 0, part, :], target.at[mine, part, :],
                    s.row_sem.at[base, p], s.row_sem.at[base + 1, p], l.target("swap"),
                )
            )
        return (
            swaps,
            remote(
                source.at[m, 0], target.at[mine],
                s.row_sem.at[base, PARTS], s.row_sem.at[base + 1, PARTS], l.target("core"),
            ),
            remote(
                target.at[theirs], target.at[theirs],
                s.row_sem.at[base, PARTS + 1], s.row_sem.at[base + 1, PARTS + 1], l.target("core"),
            ),
        )

    frame_copies = lambda: row_copies(frames, s.x, 0)
    cot_copies = lambda: row_copies(cot, o.cot_rows, 2)
    frame_own = lambda: pltpu.make_async_copy(
        frames.at[l.half, 0], s.x.at[l.half * 2 + core], s.local.at[7]
    )
    cot_load = lambda: pltpu.make_async_copy(cot.at[l.half, 0], s.cot_own, s.local.at[8])
    cot_store = lambda: pltpu.make_async_copy(
        s.cot_own, o.cot_rows.at[l.half * 2 + core], s.local.at[8]
    )

    def kv_copy(g, which):
        at = which * width + g * span
        return remote(
            s.qkv_v.at[pl.ds(width + at, span)],
            s.far_v.at[pl.ds(at, span)],
            s.kv_send.at[g, which],
            s.kv_recv.at[g, which],
            l.target("pair"),
        )

    def mix_copy(g, of_core):
        at = pl.ds(pl.multiple_of(of_core * width + g * span, 16), span)
        return remote(
            s.mix_v.at[at],
            s.mix_v.at[at],
            s.mix_send.at[g],
            s.mix_recv.at[g],
            l.target("core"),
        )

    def wo_copy(of_core):
        return remote(
            o.w_out.at[of_core], o.w_out.at[of_core],
            s.wo_sem.at[0], s.wo_sem.at[1], l.target("core"),
        )

    def wide_load(which):
        return pltpu.make_async_copy(
            o.w_qkv.at[:, pl.ds(which * hw, hw)], s.wq_v.at[which], s.load_sem.at[which]
        )

    def wo_load():
        return pltpu.make_async_copy(o.w_out, s.wo_v, s.load_sem.at[3])

    inner_tile = 256

    def wi_load(c):
        cols = pl.ds(pl.multiple_of(c * inner_tile, inner_tile), inner_tile)
        slot = lax.rem(c, 2)
        return pltpu.make_async_copy(
            o.w_inner.at[:, cols], s.wi_v.at[slot], s.load_sem.at[4 + slot]
        )

    stores = (
        (s.x, o.x_rows), (s.norm_v, o.normed), (s.qkv_v, o.qkv), (s.far_v, o.far), (s.mix_v, o.mixed),
        (s.mid_v, o.middle), (s.n2_v, o.normed_two), (s.act_v, o.active), (s.slo_v, o.slope),
    )

    def store(i):
        return pltpu.make_async_copy(*stores[i], s.out_sem.at[i])

    big = rows // 2

    def big_rows(t):
        return pl.ds(pl.multiple_of(t * big, 128), big)

    def x_tile(t):
        return s.x[pl.ds(2 * t, 2)].reshape(big, D).astype(wide)

    slices = 4

    def by_rows(t, run):
        def one(part, carry):
            run(pl.ds(pl.multiple_of(t * big + part * (big // slices), 16), big // slices))
            return carry

        lax.fori_loop(0, slices, one, 0)

    def project(step):
        t = lax.rem(step, 2)

        def norm(at):
            values = s.norm_v[at, :].astype(wide)
            s.norm_v[at, :] = norm_rows(values, vectors[4:5, :], vectors[5:6, :])

        @pl.when(step < 2)
        def _():
            s.norm_v[big_rows(t), :] = s.x[pl.ds(2 * t, 2)].reshape(big, D)
            by_rows(t, norm)

        mine = pl.ds(pl.multiple_of(core * hw, 128), hw)

        def one(which, carry):
            part = dims(s.norm_v[big_rows(t), :], s.wq_v[which], 1, 0)
            bias = jnp.where(which == 1, 0.0, vectors[pl.ds(lax.div(which, 2), 1), mine])
            at = pl.ds(pl.multiple_of(which * hw, 16), hw)
            s.qkv_v[at, big_rows(t)] = (part + bias).T.astype(low)
            return carry

        values = lax.div(step, 2)
        lax.fori_loop(2 * values, 2 + values, one, 0)

    def attend(index):
        head, part = index // tiles, lax.rem(index, tiles)
        row = head * HD
        columns = pl.ds(pl.multiple_of(part * tile, tile), tile)
        qkv, far = s.qkv_v, s.far_v

        def feature(base):
            return pl.ds(pl.multiple_of(base + row, 16), HD)

        query = jnp.concatenate([qkv[feature(0), columns], tags_q[:, columns]], axis=0)
        keys = (qkv[feature(width), :], far[feature(0), :])
        values = (qkv[feature(2 * width), :], far[feature(width), :])
        scores = [
            dims(jnp.concatenate([keys[b], tags_k[b]], axis=0), query, 0, 0) for b in (0, 1)
        ]
        top = jnp.maximum(*[jnp.max(v, axis=0, keepdims=True) for v in scores]) * factor
        total = jnp.zeros_like(top)
        sums = jnp.zeros((HD, tile), wide)
        for b in (0, 1):
            part_values = jnp.exp2(scores[b] * factor - top)
            total = total + jnp.sum(part_values, axis=0, keepdims=True)
            sums = sums + dims(values[b], part_values.astype(low), 1, 0)
        s.mix_v[feature(core * width), columns] = (sums / total).astype(low)
        o.logs[head, :, columns] = top + jnp.log2(total)

    def branch(t):
        parts = [dims(s.mix_v[:, big_rows(t)], s.wo_v[b], 0, 0) for b in (0, 1)]
        middle = x_tile(t) + (jnp.concatenate(parts, axis=1) + vectors[2:3, :])
        s.mid_v[big_rows(t), :] = middle

        def norm(at):
            s.n2_v[at, :] = norm_rows(s.mid_v[at, :], vectors[6:7, :], vectors[7:8, :])

        by_rows(t, norm)

    column_tiles = 2 * D // inner_tile

    def inner(index):
        c, t = index // 2, lax.rem(index, 2)

        @pl.when(t == 0)
        def _():
            @pl.when(c + 1 < column_tiles)
            def _():
                wi_load(c + 1).start()

            wi_load(c).wait()

        cols = pl.ds(pl.multiple_of(c * inner_tile, inner_tile), inner_tile)
        bias_at = pl.ds(pl.multiple_of(core * 2 * D + c * inner_tile, inner_tile), inner_tile)
        value = dims(s.n2_v[big_rows(t), :], s.wi_v[lax.rem(c, 2)], 1, 0)
        active, slope = gelu_parts(value + s.hidden_bias[:, bias_at])
        s.act_v[big_rows(t), cols] = active.astype(low)
        s.slo_v[big_rows(t), cols] = slope

    def unpack():
        for k in range(K):
            for q in (0, 1):
                d = 2 * k + q
                vectors[:, d * r : (d + 1) * r] = s.small_all[k, q, 0:8, 0:r].astype(wide)
                per = f // r
                for j in range(per):
                    at = d * f + j * r
                    s.hidden_bias[:, at : at + r] = s.small_all[
                        k, q, 8 + j : 9 + j, 0:r
                    ].astype(wide)

    l.barrier("core", "swap", "diagonal")
    begin(5)
    begin(0)
    begin(1)
    _, own_f, _ = frame_copies()
    own_f.start()
    frame_own().start()
    for m in (2, 3, 4):
        begin(m)
    pl.when(l.crossed == 1)(lambda: outer_give().start())
    pl.when(l.crossed == 0)(lambda: outer_keep().start())
    cot_load().start()

    plan = {}

    def at(step, *runs):
        plan.setdefault(step, []).extend(runs)

    def own_outer():
        pl.when(l.crossed == 1)(lambda: outer_give().wait_recv())
        pl.when(l.crossed == 0)(lambda: outer_keep().wait())

    along = lambda i, d: functools.partial(gather.along, i, d)
    across = lambda i, d: functools.partial(gather.across, i, d)
    last = lambda i: functools.partial(gather.last, i)

    def rows_arrive():
        swaps, mine, pass_on = frame_copies()
        for swap in swaps:
            swap.wait_recv()
        pass_on.start()
        mine.wait_recv()
        pass_on.wait_recv()
        frame_own().wait()

    def kv_ready(g):
        for which in (0, 1):
            kv_copy(g, which).wait_recv()

    def cot_start():
        cot_load().wait()
        _, mine, _ = cot_copies()
        mine.start()
        cot_store().start()

    def cot_pass():
        swaps, _, pass_on = cot_copies()
        for swap in swaps:
            swap.wait_recv()
        pass_on.start()

    def after_v():
        wo_copy(1 - core).wait_recv()
        wo_load().start()

    def mix_ready():
        for g in range(groups):
            mix_copy(g, 1 - core).wait_recv()

    def kv_send(which, *gs):
        for g in gs:
            kv_copy(g, which).start()

    def swap_frames(*ps):
        for p in ps:
            frame_copies()[0][p].start()

    def swap_cot(*ps):
        for p in ps:
            cot_copies()[0][p].start()

    frames_go = lambda *ps: functools.partial(swap_frames, *ps)
    cot_go = lambda *ps: functools.partial(swap_cot, *ps)

    attends = heads * tiles
    a0 = 4
    b0 = a0 + attends
    i0 = b0 + 2
    end = i0 + 2 * column_tiles
    own = lambda i: functools.partial(gather.own, i)
    aside = lambda i, d: functools.partial(gather.aside, i, d)
    here_now = lambda *ms: (lambda: [ready(m) for m in ms])
    send_kv = lambda which, *gs: functools.partial(kv_send, which, *gs)

    at(0, here_now(5), own(0), aside(0, 0), here_now(0, 1), own(1), aside(1, 0))
    at(0, along(0, 1), aside(0, 1), here_now(2, 3), own(2), along(0, 2), aside(0, 2), along(0, 3), aside(0, 3))
    at(0, aside(2, 0), frames_go(0), across(0, 0), across(0, 1), across(0, 2), across(0, 3))
    at(0, along(1, 1), aside(1, 1), frames_go(1), along(1, 2), aside(1, 2), here_now(4), own(3), across(1, 0))
    at(0, frames_go(2), along(2, 1), aside(2, 1), along(1, 3), aside(1, 3), across(1, 1), frames_go(3))
    at(0, along(2, 2), aside(2, 2))
    at(0, own(4), across(1, 2), along(2, 3), aside(2, 3), across(1, 3), along(3, 1), last(0), unpack)
    at(0, aside(3, 0), across(2, 0), aside(3, 1), along(3, 2), rows_arrive, lambda: store(0).start())
    at(0, last(1), lambda: wide_load(0).start(), lambda: wide_load(1).start())
    at(0, lambda: wide_load(0).wait(), lambda: wide_load(1).wait())
    at(1, across(2, 1), along(4, 1), aside(3, 2), own_outer, own(5), along(3, 3))
    at(2, send_kv(0, 0), lambda: store(1).start(), across(2, 2), aside(3, 3), across(2, 3), aside(4, 0))
    at(2, along(4, 2), across(3, 0), own(6), send_kv(0, 1), aside(4, 1), across(3, 1), along(4, 3), last(2))
    at(2, lambda: wide_load(2).start(), lambda: wo_copy(core).start(), lambda: wide_load(2).wait())
    at(a0, send_kv(1, 0), lambda: store(2).start(), aside(4, 2))
    at(a0 + 1, across(3, 2), aside(4, 3), send_kv(1, 1))
    at(a0 + 3, along(5, 1), across(3, 3), send_kv(0, 2))
    at(a0 + 4, cot_start)
    at(a0 + 5, aside(5, 0), across(4, 0), along(5, 2), send_kv(1, 2))
    at(a0 + 7, aside(5, 1), across(4, 1))
    at(a0 + 9, along(6, 1), after_v, send_kv(0, 3))
    at(a0 + 11, aside(5, 2), across(4, 2), send_kv(1, 3))
    at(a0 + 13, along(5, 3), aside(5, 3), cot_go(0))
    at(a0 + 15, across(4, 3))
    at(a0 + 17, along(6, 2), aside(6, 0), cot_go(1))
    at(a0 + 19, across(5, 0), aside(6, 1))
    at(a0 + 20, across(5, 1), cot_go(2))
    at(a0 + 21, along(6, 3), aside(6, 2))
    at(a0 + 22, cot_go(3))
    at(a0 + 23, across(5, 2))
    at(i0 + 2, cot_pass)
    for g in range(groups):
        at(a0 + g * GROUP_HEADS * tiles, functools.partial(kv_ready, g))
        at(a0 + (g + 1) * GROUP_HEADS * tiles, lambda g=g: mix_copy(g, core).start())
    at(b0, aside(6, 3), across(5, 3), lambda: store(3).start())
    at(b0, lambda: wo_load().wait(), mix_ready, lambda: store(4).start())
    at(b0 + 1, across(6, 0))
    at(i0, across(6, 1), lambda: store(5).start(), lambda: store(6).start(), last(3))
    at(i0, lambda: wi_load(0).start())
    at(i0 + 3, across(6, 2))
    at(i0 + 7, across(6, 3))
    at(i0 + 8, last(4))

    def one(step, carry):
        for when in sorted(plan):

            def run():
                for tick in plan[when]:
                    tick()

            pl.when(step == when)(run)
        inside = lambda lo, n: jnp.logical_and(step >= lo, step < lo + n)
        pl.when(step < a0)(lambda: project(step))
        pl.when(inside(a0, attends))(lambda: attend(step - a0))
        pl.when(inside(b0, 2))(lambda: branch(step - b0))
        pl.when(inside(i0, 2 * column_tiles))(lambda: inner(step - i0))
        return carry

    lax.fori_loop(0, end, one, 0)
    store(7).start()
    store(8).start()
    gather.last(5)
    gather.last(6)
    gather.drain()
    for m in range(6):
        give(m).wait_send()
    pl.when(l.crossed == 1)(lambda: outer_give().wait_send())
    for swaps, mine, pass_on in (frame_copies(), cot_copies()):
        for copy in swaps + [mine, pass_on]:
            copy.wait_send()
    _, mine, pass_on = cot_copies()
    mine.wait_recv()
    pass_on.wait_recv()
    cot_store().wait()
    wo_copy(core).wait_send()
    for g in range(groups):
        mix_copy(g, core).wait_send()
        for which in (0, 1):
            kv_copy(g, which).wait_send()
    for i in range(len(stores)):
        store(i).wait()


def forward_linked(frames, cot, weights, small, tags_q, tags_k, Z, heads, tile):
    K = 4 * Z
    r, D = weights[0].shape
    FF2 = weights[4].shape[1] // 2
    R = frames.shape[2]
    rows = 4 * R
    hw = D // 2
    groups = heads // GROUP_HEADS
    shape = jax.ShapeDtypeStruct
    outs = ForwardOuts(
        vectors=shape((8, D), wide),
        w_qkv=shape((D, 3 * hw), low),
        w_out=shape((2, D, hw), low),
        w_inner=shape((D, FF2), low),
        w_outer=shape((FF2, D), low),
        cot_rows=shape((4, R, D), low),
        x_rows=shape((4, R, D), low),
        normed=shape((rows, D), low),
        qkv=shape((3 * hw, rows), low),
        far=shape((2 * hw, rows), low),
        mixed=shape((D, rows), low),
        logs=shape((heads, 1, rows), wide),
        middle=shape((rows, D), wide),
        normed_two=shape((rows, D), low),
        active=shape((rows, FF2), low),
        slope=shape((rows, FF2), wide),
    )
    dma = pltpu.SemaphoreType.DMA
    scratch = [
        pltpu.VMEM((K, 2) + small.shape, low),
        pltpu.VMEM((1, 2 * FF2), wide),
        pltpu.VMEM((4, R, D), low),
        pltpu.VMEM((rows, D), low),
        pltpu.VMEM((3 * hw, rows), low),
        pltpu.VMEM((2 * hw, rows), low),
        pltpu.VMEM((D, rows), low),
        pltpu.VMEM((3, D, hw), low),
        pltpu.VMEM((2, D, hw), low),
        pltpu.VMEM((2, D, 256), low),
        pltpu.VMEM((rows, D), low),
        pltpu.VMEM((rows, D), wide),
        pltpu.VMEM((rows, FF2), low),
        pltpu.VMEM((rows, FF2), wide),
        pltpu.VMEM((R, D), low),
        dma((9,)),
        dma((7,)),
        dma((7,)),
        dma((4, PARTS + 2)),
        dma((groups, 2)),
        dma((groups, 2)),
        dma((groups,)),
        dma((groups,)),
        dma((2,)),
        dma((9,)),
        dma((6,)),
    ]
    spaces = [pltpu.VMEM if v in (outs.vectors, outs.logs) else pl.ANY for v in outs]
    results = pl.pallas_call(
        functools.partial(forward_kernel, Z, heads, tile),
        out_shape=tuple(outs),
        in_specs=full(2, pl.ANY) + full(9),
        out_specs=tuple(pl.BlockSpec(memory_space=space) for space in spaces),
        scratch_shapes=scratch + Gather.semaphores(7, Z),
        compiler_params=pltpu.CompilerParams(
            collective_id=0, has_side_effects=True, vmem_limit_bytes=BIG
        ),
    )(frames, cot, *weights, small, tags_q, tags_k)
    return ForwardOuts(*results)


SETS = 3


class Scatter:
    def __init__(self, links, i, block, out, buffers, sems, credit):
        self.l, self.i, self.block, self.out = links, i, block, out
        self.held, self.from_far, self.from_near, self.from_line = buffers
        self.load_sem, self.send_sem, self.recv_sem = sems
        self.credit = credit
        self.drained = False

    def load(self, colour, side, step):
        l = self.l
        near, far = l.sides(colour)
        z = l.z + step
        return pltpu.make_async_copy(
            self.block(self.i, colour, l.coords((near,) if side else (), z)),
            self.held.at[colour, side, z],
            self.load_sem.at[self.i, colour, side * l.Z + z],
        )

    def remote(self, colour, kind, step, to, way=0):
        l, Z = self.l, self.l.Z
        near, far = l.sides(colour)
        z = l.z + step
        if kind < 2:
            src = self.block(self.i, colour, l.coords((near, far) if kind else (far,), z))
            dst = self.from_far.at[colour, kind, z]
        elif kind == 2:
            src, dst = self.held.at[colour, 1, z], self.from_near.at[colour, z]
        else:
            src, dst = self.held.at[colour, 0, z], self.from_line.at[colour, way, z]
        return remote(
            src,
            dst,
            self.send_sem.at[self.i, colour, kind * Z + z],
            self.recv_sem.at[self.i, colour, (kind + way) * Z + z],
            l.target(to),
        )

    def arrive(self, colour, kind, step, way=0):
        self.remote(colour, kind, step, "cx", way).wait_recv()

    def send(self, step, *what):
        self.remote(*what).start()

    def both(self, distance, run):
        def here(step):
            for colour in (0, 1):
                run(step, colour)

        self.l.each_way(distance, here)

    def start(self):
        def run(step, colour):
            near, far = self.l.sides(colour)
            self.send(step, colour, 1, step, far)
            self.load(colour, 1, step).start()

        for distance in range(self.l.Z - 1, -1, -1):
            self.both(distance, run)

    def total(self, target, parts):
        rows, cols = target.shape
        pieces = 5 if cols % 640 == 0 else 1
        wide_cols = cols // pieces

        def one(p, carry):
            window = pl.ds(pl.multiple_of(p * wide_cols, 128), wide_cols)
            value = parts[0][:, window].astype(wide)
            for part in parts[1:]:
                value = value + part[:, window].astype(wide)
            target[:, window] = value.astype(target.dtype)
            return carry

        lax.fori_loop(0, pieces, one, 0)

    def near(self, distance):
        def run(step, colour):
            near, far = self.l.sides(colour)
            z = self.l.z + step
            self.load(colour, 1, step).wait()
            self.arrive(colour, 1, step)
            mine = self.held.at[colour, 1, z]
            self.total(mine, [mine, self.from_far.at[colour, 1, z]])
            self.send(step, colour, 2, step, near)

        def rest(step, colour):
            near, far = self.l.sides(colour)
            self.send(step, colour, 0, step, far)
            self.load(colour, 0, step).start()

        self.both(distance, run)
        self.both(distance, rest)

    def parts(self, colour, step):
        z = self.l.z + step
        self.load(colour, 0, step).wait()
        self.arrive(colour, 0, step)
        self.arrive(colour, 2, step)
        return [
            self.held.at[colour, 0, z],
            self.from_far.at[colour, 0, z],
            self.from_near.at[colour, z],
        ]

    def line(self, distance):
        l = self.l

        def run(step, colour):
            toward = lax.div(step, distance)
            way = lax.div(1 - toward, 2)
            z = l.z + step
            behind = l.has(-toward)
            parts = self.parts(colour, step)
            mine = self.held.at[colour, 0, z]

            @pl.when(behind)
            def _():
                self.arrive(colour, 3, step, way)
                self.total(mine, parts + [self.from_line.at[colour, way, z]])

            @pl.when(jnp.logical_not(behind))
            def _():
                self.total(mine, parts)

            self.send(step, colour, 3, step, toward, way)

        self.both(distance, run)

    def finish(self):
        l = self.l
        for colour in (0, 1):
            z = l.z
            parts = self.parts(colour, 0)
            left, right = self.from_line.at[colour, 0, z], self.from_line.at[colour, 1, z]
            target = self.out.at[colour]
            l.when([-1], lambda: self.arrive(colour, 3, 0))
            l.when([1], lambda: self.arrive(colour, 3, 0, 1))
            l.when([-1, 1], lambda: self.total(target, parts + [left, right]))
            pl.when(jnp.logical_not(l.has(-1)))(lambda: self.total(target, parts + [right]))
            pl.when(jnp.logical_not(l.has(1)))(lambda: self.total(target, parts + [left]))

    def free(self):
        for to in ("cy", "cx", -1, 1):

            def tell():
                pl.semaphore_signal(
                    self.credit.at[self.i], inc=1, device_id=self.l.target(to), device_id_type=MESH
                )

            self.l.when([] if to in ("cy", "cx") else [to], tell)

    def freed(self):
        ends = jnp.minimum(self.l.z, 1) + jnp.minimum(self.l.Z - 1 - self.l.z, 1)
        pl.semaphore_wait(self.credit.at[self.i], 2 + ends)
        self.drain()

    def drain(self):
        def one(z, carry):
            step = z - self.l.z
            for colour in (0, 1):
                for kind in (0, 1, 2):
                    self.remote(colour, kind, step, "cx").wait_send()
                pl.when(step != 0)(lambda: self.remote(colour, 3, step, "cx").wait_send())
            return carry

        if not self.drained:
            lax.fori_loop(0, self.l.Z, one, 0)
        self.drained = True

    @staticmethod
    def ticks(works, shared, settle):
        far_first = lambda w, run: [functools.partial(run(w), d) for d in range(w.l.Z - 1, -1, -1)]
        out = [(0, works[0].start)]
        for i, work in enumerate(works):
            out += [(i, t) for t in far_first(work, lambda w: w.near)]
            if i + 1 < len(works):
                if SETS <= i + 1 < shared:
                    out.append((i, works[i + 1 - SETS].freed))
                out.append((i + 1, works[i + 1].start))
            out += [(i, t) for t in far_first(work, lambda w: w.line)[:-1]]
            if i:
                out.append((i - 1, works[i - 1].finish))
                out.append((i - 1, functools.partial(settle, i - 1)))
                if i - 1 + SETS < shared:
                    out.append((i - 1, works[i - 1].free))
        out.append((len(works) - 1, works[-1].finish))
        out.append((len(works) - 1, functools.partial(settle, len(works) - 1)))
        return out


class BackwardOuts(NamedTuple):
    query: Any
    key: Any
    value: Any
    output: Any
    inner: Any
    outer: Any
    small: Any
    frames_grad: Any
    layer_out: Any
    qkv_blocks: Any
    out_blocks: Any
    inner_blocks: Any


class BackwardScratch(NamedTuple):
    dqkv: Any
    own: Any
    away: Any
    got: Any
    acc_k: Any
    acc_v: Any
    norm_v: Any
    half_v: Any
    act_t: Any
    act_sem: Any
    core_credit: Any
    wt: Any
    stage: Any
    stage_o: Any
    part: Any
    part_got: Any
    x_own: Any
    mg_own: Any
    home_out: Any
    home_in: Any
    vec: Any
    small_g: Any
    done: Any
    done_small: Any
    got_small: Any
    done_local: Any
    done_send: Any
    done_recv: Any
    layer_sem: Any
    home_sem: Any
    back_send: Any
    back_recv: Any
    pair_sem: Any
    load: Any
    wt_sem: Any
    stage_sem: Any
    credit: Any
    load_sem: Any
    send_sem: Any
    recv_sem: Any


RATES = (2.0, 2.0, 2.0, 2.0, 1.0, 1.0)


def backward_kernel(Z, heads, tile, *refs):
    (
        qkv, far, tags_q, tags_k, mixed, logs, grad_in, bg, vectors, small_part, hidden_sums,
        x_rows, middle_grad, normed, w_qkv, active, g_outer, inner_grad, normed_two, w_outer, middle,
    ) = refs[:21]
    n_outs, n_scratch = len(BackwardOuts._fields), len(BackwardScratch._fields)
    o = BackwardOuts(*refs[21 : 21 + n_outs])
    s = BackwardScratch(*refs[21 + n_outs : 21 + n_outs + n_scratch])
    buffers = refs[21 + n_outs + n_scratch :]
    l = Links(Z)
    core, K = l.core, 4 * Z
    width = heads * HD
    rows = qkv.shape[1]
    R = rows // 4
    D = bg.shape[1]
    hw = D // 2
    r2 = D // K
    r = r2 // 2
    f = w_outer.shape[0] // K
    tiles = rows // tile
    groups = heads // GROUP_HEADS
    span = GROUP_HEADS * HD
    scale = HD ** (-0.5)
    factor = scale * math.log2(math.e)

    def block(i, colour, place):
        y, x, z = place
        at = pl.ds(pl.multiple_of(l.index(place) * r2, 16), r2)
        if i < 2:
            first = ((x * Z + z) * 2 + y) * f + colour * (f // 2)
            return g_outer.at[pl.ds(pl.multiple_of(first, 16), f // 2), pl.ds(i * hw, hw)]
        if i < 4:
            return o.inner_blocks.at[at, pl.ds(((i - 2) * 2 + colour) * hw, hw)]
        if i == 4:
            return o.qkv_blocks.at[at, pl.ds(colour * hw, hw)]
        if i == 5:
            if colour == 0:
                return o.qkv_blocks.at[at, pl.ds(2 * hw, hw)]
            return o.out_blocks.at[at, :]
        return s.small_g.at[l.index(place), colour]

    outs = [s.done.at[i] for i in range(6)] + [s.done_small]
    works = [
        Scatter(
            l, i, block, outs[i],
            buffers[4 * (SETS if i == 6 else i % SETS) :][:4],
            (s.load_sem, s.send_sem, s.recv_sem), s.credit,
        )
        for i in range(7)
    ]

    row_tiles = D // 256

    finals = ((o.query, o.key), (o.value, o.output))

    def final_place(i, colour, of_core):
        if i < 2:
            return o.outer.at[pl.ds(colour * (f // 2), f // 2), pl.ds(i * hw, hw)]
        if i < 4:
            first = of_core * 2 * D + ((i - 2) * 2 + colour) * hw
            return o.inner.at[:, pl.ds(pl.multiple_of(first, 128), hw)]
        return finals[i - 4][colour].at[:, pl.ds(pl.multiple_of(of_core * hw, 128), hw)]

    def final_rows(i, colour, which):
        if i < 2:
            return s.done.at[i, colour]
        return s.done.at[i, colour, pl.ds(pl.multiple_of(which * r, 8), r), :]

    def final_keep(i, colour):
        return pltpu.make_async_copy(
            final_rows(i, colour, core), final_place(i, colour, core), s.done_local.at[i, colour]
        )

    def final_give(i, colour):
        return remote(
            final_rows(i, colour, 1 - core), final_place(i, colour, core),
            s.done_send.at[i, colour], s.done_recv.at[i, colour],
            l.target("diagonal" if i < 2 else "core"),
        )

    small_give = lambda: remote(
        s.done_small.at[1 - core], s.got_small,
        s.done_send.at[6, 0], s.done_recv.at[6, 0], l.target("core"),
    )

    def settle(i):
        if i == 6:
            small_give().start()
            return
        for colour in (0, 1):
            keep = lambda: final_keep(i, colour).start()
            give = lambda: final_give(i, colour).start()
            if i < 2:
                pl.when(l.crossed == 0)(keep)
                pl.when(l.crossed == 1)(give)
            else:
                keep()
                give()

    def settled():
        for i in range(6):
            for colour in (0, 1):
                keep = lambda: final_keep(i, colour).wait()

                def give():
                    final_give(i, colour).wait_send()
                    final_give(i, colour).wait_recv()

                if i < 2:
                    pl.when(l.crossed == 0)(keep)
                    pl.when(l.crossed == 1)(give)
                else:
                    keep()
                    give()
        small_give().wait_recv()
        o.small[...] = s.done_small[core] + s.got_small[...]
        small_give().wait_send()

    def layer_swap(p):
        part = pl.ds(p * (R // PARTS), R // PARTS)
        return remote(
            s.x_own.at[1 - l.half, part, :], o.layer_out.at[l.half, 0, part, :],
            s.home_sem.at[2, p], s.home_sem.at[3, p], l.target("swap"),
        )

    layer_store = lambda: pltpu.make_async_copy(
        s.x_own.at[l.half], o.layer_out.at[l.half, 0], s.layer_sem.at[2]
    )

    def back_copy(g, which):
        at = pl.ds(which * width + g * span, span)
        return remote(
            s.away.at[at], s.got.at[at],
            s.back_send.at[g, which], s.back_recv.at[g, which], l.target("pair"),
        )

    def send_back(g, which):
        back_copy(g, which).start()

    def add_back(g):
        for which in (0, 1):
            back_copy(g, which).wait_recv()
            for h in range(GROUP_HEADS):
                at = which * width + g * span + h * HD
                s.dqkv[pl.ds(width + at, HD), :] = (
                    s.own[pl.ds(at, HD), :] + s.got[pl.ds(at, HD), :].astype(wide)
                ).astype(low)

    def row_load(h, which):
        source, target = ((x_rows, s.x_own), (middle_grad, s.mg_own), (middle, s.mg_own))[which]
        return pltpu.make_async_copy(
            source.at[h * 2 + core], target.at[h], s.load.at[h * 3 + which]
        )

    def norm_load(which):
        return pltpu.make_async_copy(
            (normed_two, normed)[which], s.norm_v, s.load.at[6 + which]
        )

    def half_load(which):
        columns = pl.ds(which * D, D)
        return pltpu.make_async_copy(
            inner_grad.at[:, columns], s.half_v, s.load.at[9 + which]
        )

    hidden_tiles = 4 * hw // 256

    def act_load(index):
        slot = lax.rem(index, 2)
        at = pl.ds(pl.multiple_of(index * 256, 256), 256)
        return pltpu.make_async_copy(active.at[:, at], s.act_t.at[slot], s.act_sem.at[slot])

    def outer_load(c):
        at = pl.ds(pl.multiple_of(c * 256, 256), 256)
        slot = lax.rem(c, 2)
        return pltpu.make_async_copy(
            w_outer.at[at, :], s.wt.at[slot, :, pl.ds(0, D)], s.wt_sem.at[slot]
        )

    def wt_load(c):
        at = pl.ds(pl.multiple_of(c * 256, 256), 256)
        slot = lax.rem(c, 2)
        return pltpu.make_async_copy(w_qkv.at[at, :], s.wt.at[slot], s.wt_sem.at[slot])

    def stage_copy(c, which):
        slot = lax.rem(c, 2)
        if which < 2:
            at = pl.ds(pl.multiple_of(c * 256, 256), 256)
            source = (s.stage.at[slot], s.stage_o.at[slot])[which]
            target = (o.qkv_blocks, o.out_blocks)[which].at[at, :]
        else:
            at = pl.ds(pl.multiple_of(lax.rem(c, row_tiles) * 256, 256), 256)
            columns = pl.ds(pl.multiple_of(lax.div(c, row_tiles) * D, 128), D)
            source, target = s.stage.at[slot, :, pl.ds(0, D)], o.inner_blocks.at[at, columns]
        return pltpu.make_async_copy(source, target, s.stage_sem.at[which, slot])

    def drained(which, steps):
        for c in (steps - 2, steps - 1):
            stage_copy(c, which).wait()

    def part_copy(h, turn):
        return remote(
            s.part.at[h, 1 - core], s.part_got.at[h],
            s.pair_sem.at[turn, h], s.pair_sem.at[turn, 2 + h], l.target("core"),
        )

    def home_copy(p):
        part = pl.ds(p * (R // PARTS), R // PARTS)
        return remote(
            s.home_out.at[part, :], s.home_in.at[part, :],
            s.home_sem.at[0, p], s.home_sem.at[1, p], l.target("swap"),
        )

    def home_store(h):
        return pltpu.make_async_copy(s.mg_own.at[h], o.frames_grad.at[h, 0], s.load.at[11 + h])

    def attend(index):
        head, part = index // tiles, lax.rem(index, tiles)
        row = head * HD
        columns = pl.ds(pl.multiple_of(part * tile, tile), tile)

        def feature(base):
            return pl.ds(pl.multiple_of(base + row, 16), HD)

        head_query = qkv[feature(0), columns]
        grad = grad_in[feature(0), columns]
        query = jnp.concatenate([head_query, tags_q[:, columns]], axis=0)
        attended = mixed[feature(core * width), columns]
        delta = jnp.sum(grad.astype(wide) * attended.astype(wide), axis=0, keepdims=True)
        log_row = logs[head, :, columns]
        query_rows = head_query.T
        grad_rows = grad.T
        dq = jnp.zeros((HD, tile), wide)

        @pl.when(part == 0)
        def _():
            s.acc_k[...] = jnp.zeros_like(s.acc_k)
            s.acc_v[...] = jnp.zeros_like(s.acc_v)

        keys = (qkv[feature(width), :], far[feature(0), :])
        values = (qkv[feature(2 * width), :], far[feature(width), :])
        for b in (0, 1):
            key = jnp.concatenate([keys[b], tags_k[b]], axis=0)
            probs = jnp.exp2(dims(key, query, 0, 0) * factor - log_row)
            grad_probs = dims(values[b], grad, 0, 0)
            score_grad = (probs * (grad_probs - delta)).astype(low)
            s.acc_v[b] += dims(probs.astype(low), grad_rows, 1, 0)
            s.acc_k[b] += dims(score_grad, query_rows, 1, 0)
            dq = dq + dims(keys[b], score_grad, 1, 0)
        s.dqkv[feature(0), columns] = (dq * scale).astype(low)

        @pl.when(part == tiles - 1)
        def _():
            s.own[feature(0), :] = s.acc_k[0].T * scale
            s.own[feature(width), :] = s.acc_v[0].T
            s.away[feature(0), :] = (s.acc_k[1].T * scale).astype(low)
            s.away[feature(width), :] = s.acc_v[1].T.astype(low)

    own_cols = pl.ds(pl.multiple_of(core * hw, 128), hw)

    def staged(c, which, value):
        @pl.when(c >= 2)
        def _():
            stage_copy(c - 2, which).wait()

        if which == 2:
            s.stage[lax.rem(c, 2), :, 0:D] = value.astype(low)
        else:
            (s.stage, s.stage_o)[which][lax.rem(c, 2)] = value.astype(low)
        stage_copy(c, which).start()

    def out_part(c):
        @pl.when(c + 1 < hidden_tiles)
        def _():
            act_load(c + 1).start()
            outer_load(c + 1).start()

        act_load(c).wait()
        outer_load(c).wait()
        slot = lax.rem(c, 2)
        for h in (0, 1):
            value = dims(s.act_t[slot, pl.ds(h * 2 * R, 2 * R), :], s.wt[slot, :, 0:D], 1, 0)
            for q in (0, 1):
                s.part[h, q] = jnp.where(c == 0, 0.0, s.part[h, q]) + value[q * R : (q + 1) * R]

    def inner_step(index):
        c = lax.rem(index, row_tiles)
        at = pl.ds(pl.multiple_of(c * 256, 256), 256)
        staged(index, 2, dims(s.norm_v[:, at], s.half_v[...], 0, 0))

    def layer_parts():
        for h in (0, 1):
            part_copy(h, 0).start()
        for h in (0, 1):
            row_load(h, 2).wait()
            part_copy(h, 0).wait_recv()
            s.x_own[h] = (
                s.mg_own[h] + (s.part[h, core] + s.part_got[h] + vectors[3:4, :])
            ).astype(low)
            row_load(h, 1).start()
        for h in (0, 1):
            part_copy(h, 0).wait_send()
        pl.semaphore_signal(
            s.core_credit.at[0], inc=1, device_id=l.target("core"), device_id_type=MESH
        )
        layer_store().start()

    def layer_sent():
        layer_store().wait()
        for p in range(PARTS):
            layer_swap(p).wait_send()
        for h in (0, 1):
            row_load(h, 0).start()

    def out_grad(c):
        at = pl.ds(pl.multiple_of(c * 256, 256), 256)
        staged(c, 1, dims(mixed[at, :], bg[:, own_cols], 1, 0))

    def qkv_grad(c):
        at = pl.ds(pl.multiple_of(c * 256, 256), 256)
        staged(c, 0, dims(s.norm_v[:, at], s.dqkv[...], 0, 1))

    def norm_grad(index):
        c, h = index // 2, lax.rem(index, 2)

        @pl.when(h == 0)
        def _():
            @pl.when(c + 1 < row_tiles)
            def _():
                wt_load(c + 1).start()

            wt_load(c).wait()

        columns = pl.ds(pl.multiple_of(h * 2 * R, 128), 2 * R)
        value = dims(s.wt[lax.rem(c, 2)], s.dqkv[:, columns], 1, 0).T
        at = pl.ds(pl.multiple_of(c * 256, 256), 256)
        s.part[h, 0, :, at] = value[:R]
        s.part[h, 1, :, at] = value[R:]

    def frame_grad(h):
        def one(part, carry):
            at = pl.ds(pl.multiple_of(part * 48, 16), 48)
            grad = s.part[h, core, at, :] + s.part_got[h, at, :]
            xhat, inverse = row_stats(s.x_own[h, at, :].astype(wide))
            s.mg_own[h, at, :] = s.mg_own[h, at, :] + norm_pull(grad, vectors[4:5, :], xhat, inverse)
            s.vec[4:5, :] += jnp.sum(grad * xhat, axis=0, keepdims=True)
            s.vec[5:6, :] += jnp.sum(grad, axis=0, keepdims=True)
            return carry

        lax.fori_loop(0, R // 48, one, 0)

    def bias_sums():
        s.vec[...] = small_part[...]
        ones = jnp.ones((8, rows), low)
        s.vec[0:1, own_cols] = dims(ones, s.dqkv[pl.ds(0, hw), :], 1, 1)[0:1]
        s.vec[1:2, own_cols] = dims(ones, s.dqkv[pl.ds(2 * hw, hw), :], 1, 1)[0:1]

    def rows_home():
        s.home_out[...] = s.mg_own[1 - l.half].astype(low)
        for p in range(PARTS):
            home_copy(p).start()
        home_store(l.half).start()

    def pack():
        s.small_g[...] = jnp.zeros_like(s.small_g)
        for k in range(K):
            for q in (0, 1):
                d = 2 * k + q
                s.small_g[k, q, 0:8, 0:r] = s.vec[:, d * r : (d + 1) * r].astype(low)
                for j in range(f // r):
                    at = d * f + j * r
                    s.small_g[k, q, 8 + j : 9 + j, 0:r] = hidden_sums[:, at : at + r].astype(low)

    l.barrier("core", "swap", "diagonal")
    act_load(0).start()
    norm_load(0).start()
    half_load(0).start()
    for h in (0, 1):
        row_load(h, 2).start()
    outer_load(0).start()
    attends = heads * tiles
    layer_at = lambda p: (lambda: layer_swap(p).start())
    work = []
    for step in range(attends):
        work.append(None)
        if step % 3 == 2 and step >= GROUP_HEADS * tiles - 1:
            half_group = step // 3 - 1
            work.append(functools.partial(send_back, half_group // 2, half_group % 2))
    work += [functools.partial(send_back, groups - 1, 1)]
    work += [lambda: norm_load(0).wait(), lambda: half_load(0).wait()]
    work += [None] * row_tiles
    work += [lambda: half_load(1).start(), lambda: half_load(1).wait()]
    inner_ready = len(work) + 2
    work += [None] * row_tiles + [functools.partial(drained, 2, 2 * row_tiles)]
    inner_done = len(work)
    work += [lambda: norm_load(1).start()]
    work += [None] * hidden_tiles + [layer_parts, lambda: wt_load(0).start(), layer_at(0)]
    work += [None] * row_tiles + [layer_at(1)]
    work += [functools.partial(add_back, g) for g in range(groups)] + [bias_sums]
    work += [lambda: norm_load(1).wait()] + [None] * row_tiles + [layer_at(2)]
    work += [functools.partial(drained, 0, row_tiles), functools.partial(drained, 1, row_tiles)]
    qkv_ready = len(work)
    work += [None] * row_tiles + [layer_at(3)] + [None] * row_tiles + [layer_sent]

    def exchange_parts():
        pl.semaphore_wait(s.core_credit.at[0], 1)
        for h in (0, 1):
            part_copy(h, 1).start()
        for h in (0, 1):
            for which in (0, 1):
                row_load(h, which).wait()
        for h in (0, 1):
            part_copy(h, 1).wait_recv()

    work.append(exchange_parts)
    work += [None] * 2 + [rows_home, pack]

    ticks = Scatter.ticks(works, 6, settle)
    plan, now, done = {}, 0, 0
    starts = 0
    place, started = 0.0, 0
    for i, tick in ticks:
        if started < 7 and tick == works[started].start:
            started += 1
        need = int(place)
        for ready, first in enumerate((inner_ready, inner_done, qkv_ready)):
            if tick == works[ready + 2].start:
                need = max(need, first)
        if tick == works[6].start:
            need = len(work)
        while done < min(need, len(work)):
            if work[done] is None:
                now += 1
            else:
                plan.setdefault(now, []).append(work[done])
            done += 1
        plan.setdefault(now, []).append(tick)
        place += RATES[min(max(started - 1, 0), 5)]
    end = len([w for w in work if w is None])

    n0 = attends
    h0 = n0 + 2 * row_tiles
    o0 = h0 + hidden_tiles
    q0 = o0 + row_tiles
    d0 = q0 + row_tiles
    e0 = d0 + 2 * row_tiles

    def one(step, carry):
        for when in sorted(plan):
            if when < end:

                def run():
                    for tick in plan[when]:
                        tick()

                pl.when(step == when)(run)
        inside = lambda lo, n: jnp.logical_and(step >= lo, step < lo + n)
        pl.when(step < n0)(lambda: attend(step))
        pl.when(inside(n0, 2 * row_tiles))(lambda: inner_step(step - n0))
        pl.when(inside(h0, hidden_tiles))(lambda: out_part(step - h0))
        pl.when(inside(o0, row_tiles))(lambda: out_grad(step - o0))
        pl.when(inside(q0, row_tiles))(lambda: qkv_grad(step - q0))
        pl.when(inside(d0, 2 * row_tiles))(lambda: norm_grad(step - d0))
        pl.when(inside(e0, 2))(lambda: frame_grad(step - e0))
        return carry

    lax.fori_loop(0, end, one, 0)
    for tick in plan.get(end, []):
        tick()
    for p in range(PARTS):
        home_copy(p).wait_recv()
    home_store(l.half).wait()
    s.mg_own[1 - l.half] = s.home_in[...].astype(wide)
    home_store(1 - l.half).start()
    for w in works:
        w.drain()
    for g in range(groups):
        for which in (0, 1):
            back_copy(g, which).wait_send()
    for h in (0, 1):
        part_copy(h, 1).wait_send()
    for p in range(PARTS):
        home_copy(p).wait_send()
    home_store(1 - l.half).wait()
    for p in range(PARTS):
        layer_swap(p).wait_recv()
    settled()


def backward_linked(resident, streamed, Z, heads, tile):
    K = 4 * Z
    qkv_t = resident[0]
    rows = qkv_t.shape[1]
    R = rows // 4
    D = resident[7].shape[1]
    hw = D // 2
    r2 = D // K
    groups = heads // GROUP_HEADS
    shape = jax.ShapeDtypeStruct
    dma = pltpu.SemaphoreType.DMA
    outs = BackwardOuts(
        query=shape((r2 // 2, D), wide),
        key=shape((r2 // 2, D), wide),
        value=shape((r2 // 2, D), wide),
        output=shape((r2 // 2, D), wide),
        inner=shape((r2 // 2, 4 * D), wide),
        outer=shape((2 * r2, D), wide),
        small=shape((16, 128), wide),
        frames_grad=shape((2, 1, R, D), wide),
        layer_out=shape((2, 1, R, D), low),
        qkv_blocks=shape((D, 3 * hw), low),
        out_blocks=shape((D, hw), low),
        inner_blocks=shape((D, 4 * hw), low),
    )
    scratch = [
        pltpu.VMEM((3 * hw, rows), low),
        pltpu.VMEM((2 * hw, rows), wide),
        pltpu.VMEM((2 * hw, rows), low),
        pltpu.VMEM((2 * hw, rows), low),
        pltpu.VMEM((2, rows, HD), wide),
        pltpu.VMEM((2, rows, HD), wide),
        pltpu.VMEM((rows, D), low),
        pltpu.VMEM((rows, D), low),
        pltpu.VMEM((2, rows, 256), low),
        dma((2,)),
        pltpu.SemaphoreType.REGULAR((1,)),
        pltpu.VMEM((2, 256, 3 * hw), low),
        pltpu.VMEM((2, 256, 3 * hw), low),
        pltpu.VMEM((2, 256, hw), low),
        pltpu.VMEM((2, 2, R, D), wide),
        pltpu.VMEM((2, R, D), wide),
        pltpu.VMEM((2, R, D), low),
        pltpu.VMEM((2, R, D), wide),
        pltpu.VMEM((R, D), low),
        pltpu.VMEM((R, D), low),
        pltpu.VMEM((8, D), wide),
        pltpu.VMEM((K, 2, 16, 128), low),
        pltpu.VMEM((6, 2, r2, hw), wide),
        pltpu.VMEM((2, 16, 128), wide),
        pltpu.VMEM((16, 128), wide),
        dma((6, 2)),
        dma((7, 2)),
        dma((7, 2)),
        dma((3,)),
        dma((4, PARTS)),
        dma((groups, 2)),
        dma((groups, 2)),
        dma((2, 4)),
        dma((13,)),
        dma((2,)),
        dma((4, 2)),
        pltpu.SemaphoreType.REGULAR((SETS,)),
        dma((7, 2, 2 * Z)),
        dma((7, 2, 4 * Z)),
        dma((7, 2, 5 * Z)),
    ]
    for block in ((r2, hw),) * SETS + ((16, 128),):
        scratch += [pltpu.VMEM((2,) + lead + block, low) for lead in ((2, Z), (2, Z), (Z,), (2, Z))]
    results = pl.pallas_call(
        functools.partial(backward_kernel, Z, heads, tile),
        out_shape=tuple(outs),
        in_specs=full(len(resident)) + full(len(streamed), pl.ANY),
        out_specs=tuple(full(6, pl.ANY) + full(1) + full(5, pl.ANY)),
        scratch_shapes=scratch,
        compiler_params=pltpu.CompilerParams(
            collective_id=1, has_side_effects=True, vmem_limit_bytes=67043328
        ),
    )(*resident, *streamed)
    return BackwardOuts(*results)


def general_body(
    n_chip_rows,
    Z,
    frames,
    clip_ids,
    query_weight,
    key_weight,
    value_weight,
    output_weight,
    inner_weight,
    outer_weight,
    query_bias,
    value_bias,
    output_bias,
    inner_bias,
    outer_bias,
    first_gain,
    first_shift,
    second_gain,
    second_shift,
    out_cotangent,
):
    K = n_chip_rows * Z
    R, D = frames.shape[2], frames.shape[3]
    FF = inner_weight.shape[1]
    r = query_weight.shape[0]
    f = outer_weight.shape[0]
    hw = D // 2
    heads = H // 2
    half = Z // 2
    core = lax.axis_index("core")
    first_core = core == 0
    zz = lax.axis_index("zz")
    micro = zz // half
    first_half = micro == 0
    place = zz % half

    def swap_core(v):
        return lax.ppermute(v, "core", [(0, 1), (1, 0)])

    def swap_half(v):
        return lax.ppermute(v, "zz", [(z, (z + half) % Z) for z in range(Z)])

    def by_core(own, other, axis):
        return jnp.where(
            first_core,
            jnp.concatenate([own, other], axis),
            jnp.concatenate([other, own], axis),
        )

    def pick(v, index, axis):
        return lax.dynamic_index_in_dim(v, index, axis, keepdims=False)

    def take_rows(v):
        v = v[:, 0]
        own, away = pick(v, micro, 0), pick(v, 1 - micro, 0)
        got = swap_half(away)
        pair = jnp.where(first_half, jnp.stack([own, got]), jnp.stack([got, own]))
        both = by_core(pair[:, None], swap_core(pair)[:, None], 1)
        return both.reshape(4 * R, D)

    qkv = jnp.stack([query_weight, key_weight, value_weight], 1).reshape(r, 3, 2, hw)
    inner_split = inner_weight.reshape(r, K, 2, f)
    vectors = (
        query_bias, value_bias, output_bias, outer_bias,
        first_gain, first_shift, second_gain, second_shift, inner_bias,
    )
    small = jnp.concatenate(vectors)
    n_small = small.shape[0]

    def column_half(which):
        return jnp.concatenate(
            [
                pick(qkv, which, 2).reshape(r, 3 * hw),
                pick(inner_split, which, 2).reshape(r, FF // 2),
            ],
            1,
        )

    mine = column_half(core)
    theirs = swap_core(column_half(1 - core))
    both = by_core(mine[None], theirs[None], 0)
    small_both = by_core(small[None], swap_core(small)[None], 0)
    small_pad = -(-n_small // 1024) * 1024
    small_both = jnp.pad(small_both, ((0, 0), (0, small_pad - n_small)))
    shards = (
        small_both.reshape(2, small_pad // 128, 128),
        both[:, :, : 3 * hw],
        output_weight.reshape(r, 2, hw).transpose(1, 0, 2),
        both[:, :, 3 * hw :],
        outer_weight.reshape(2, f // 2, D),
    )
    small_all, qkv_all, out_all, inner_all, outer_all = (
        lax.all_gather(v, CHIPS, axis=0, tiled=False) for v in shards
    )
    x_rows = take_rows(frames)
    cot = take_rows(out_cotangent)

    w_qkv = qkv_all.reshape(D, 3 * hw)
    w_inner = inner_all.reshape(D, FF // 2)
    w_outer = outer_all.reshape(FF // 2, D)
    out_own = out_all.transpose(0, 2, 1, 3).reshape(K, 1, r, D)
    w_out = by_core(out_own, swap_core(out_own), 1).reshape(D, D)
    small_all = small_all.reshape(K, 2, small_pad)[:, :, :n_small].astype(wide)
    names = ("qb", "vb", "ob", "ub", "g1", "s1", "g2", "s2")
    vec = {n: small_all[:, :, i * r : (i + 1) * r].reshape(D) for i, n in enumerate(names)}
    ib_half = pick(small_all[:, :, 8 * r :], core, 1).reshape(FF // 2)

    def own_columns(v):
        return lax.dynamic_slice_in_dim(v, core * hw, hw, v.ndim - 1)

    ids = pick(clip_ids[:, 0], micro, 0).reshape(2, half, 2 * R)
    ids_q = pick(ids, place, 1).reshape(4 * R)
    order = (place - jnp.arange(half)) % half
    ids_k = jnp.take(ids, order, axis=1).transpose(1, 0, 2).reshape(half, 4 * R)
    tag = jnp.arange(TAGS, dtype=jnp.int32)[:, None]
    tags_q = jnp.where(ids_q[None, :] == tag, 0.0, masked_score).astype(low)
    tags_k = (ids_k[:, None, :] == tag[None]).astype(low)

    xf = x_rows.astype(wide)
    xhat, inverse = row_stats(xf)
    normed = (xhat * vec["g1"] + vec["s1"]).astype(low)
    bias_qkv = jnp.concatenate(
        [own_columns(vec["qb"]), jnp.zeros((hw,), wide), own_columns(vec["vb"])]
    )
    qkv_t = (dims(w_qkv, normed, 0, 1) + bias_qkv[:, None]).astype(low)
    q_t, kv_own = qkv_t[:hw], qkv_t[hw:]
    kv_parts = [kv_own]
    for o in range(1, half):
        kv_parts.append(
            lax.ppermute(
                kv_own, "zz", [(z, (z // half) * half + (z + o) % half) for z in range(Z)]
            )
        )
    kv = jnp.stack(kv_parts)
    tile = 256
    mixed_t, logs = attend_forward(q_t, tags_q, kv, tags_k, heads, tile)
    mixed_full = by_core(mixed_t, swap_core(mixed_t), 0)
    middle = xf + (dims(mixed_full, w_out, 0, 0) + vec["ob"])
    xhat_two, inverse_two = row_stats(middle)
    normed_two = (xhat_two * vec["g2"] + vec["s2"]).astype(low)
    inner = dims(normed_two, w_inner, 1, 0) + ib_half
    active, slope = gelu_parts(inner)
    active = active.astype(low)
    out_part = dims(active, w_outer, 1, 0)

    def split_rows(v):
        return v.reshape(2, 2, R, D)

    def reduce_rows(v):
        v = split_rows(v)
        return pick(v, core, 1) + swap_core(pick(v, 1 - core, 1).astype(low)).astype(wide)

    def home_rows(v):
        stay = pick(v, micro, 0)
        got = swap_half(pick(v, 1 - micro, 0))
        return jnp.where(first_half, jnp.stack([stay, got]), jnp.stack([got, stay]))[:, None]

    own_middle = pick(split_rows(middle), core, 1)
    layer_rows = (own_middle + (reduce_rows(out_part) + vec["ub"])).astype(low)
    layer_out = home_rows(layer_rows)

    grad_active = dims(cot, w_outer, 1, 1)
    inner_grad = (grad_active * slope).astype(low)
    part_two = dims(inner_grad, w_inner, 1, 1)
    grad_two = part_two + swap_core(part_two.astype(low)).astype(wide)
    middle_grad = cot.astype(wide) + norm_pull(grad_two, vec["g2"], xhat_two, inverse_two)
    branch_grad = middle_grad.astype(low)
    w_out_heads = lax.dynamic_slice_in_dim(w_out, core * hw, hw, 0)
    mixed_grad = dims(w_out_heads, branch_grad, 1, 1).astype(low)
    dq_t, own_kv, far_kv = attend_backward(
        q_t, tags_q, kv, tags_k, mixed_t, logs, mixed_grad, heads, tile
    )
    dkv = own_kv.reshape(2 * hw, 4 * R)
    for o in range(1, half):
        back = lax.ppermute(
            far_kv[o - 1], "zz", [(z, (z // half) * half + (z - o) % half) for z in range(Z)]
        )
        dkv = dkv + back.reshape(2 * hw, 4 * R).astype(wide)
    dqkv_t = jnp.concatenate([dq_t, dkv.astype(low)], 0)
    grad_one = reduce_rows(dims(dqkv_t, w_qkv, 0, 1))
    own_xhat = pick(split_rows(xhat), core, 1)
    own_inverse = pick(inverse.reshape(2, 2, R, 1), core, 1)
    frame_rows = pick(split_rows(middle_grad), core, 1) + norm_pull(
        grad_one, vec["g1"], own_xhat, own_inverse
    )
    sent = swap_half(pick(frame_rows, 1 - micro, 0).astype(low)).astype(wide)
    stay = pick(frame_rows, micro, 0)
    frames_grad = jnp.where(first_half, jnp.stack([stay, sent]), jnp.stack([sent, stay]))[:, None]

    g_qkv = dims(normed, dqkv_t, 0, 1).astype(low)
    g_out = dims(mixed_full, own_columns(branch_grad), 1, 0).astype(low)
    g_inner = dims(normed_two, inner_grad, 0, 0).astype(low)
    g_outer = dims(active, cot, 0, 0).astype(low)

    def zero_rest(v):
        return by_core(v, jnp.zeros_like(v), 0)

    bias_sums = jnp.sum(dqkv_t.astype(wide), axis=1)
    halves = 0.5
    col = {
        "qb": zero_rest(bias_sums[:hw]),
        "vb": zero_rest(bias_sums[2 * hw :]),
        "ob": halves * jnp.sum(branch_grad.astype(wide), 0),
        "ub": halves * jnp.sum(cot.astype(wide), 0),
        "g1": jnp.sum(grad_one * own_xhat, (0, 1)),
        "s1": jnp.sum(grad_one, (0, 1)),
        "g2": halves * jnp.sum(grad_two * xhat_two, 0),
        "s2": halves * jnp.sum(grad_two, 0),
    }
    ib_sum = jnp.sum(inner_grad.astype(wide), 0).reshape(K, 1, f)
    small_grad = jnp.concatenate(
        [col[n].reshape(K, 2, r) for n in names]
        + [by_core(ib_sum, jnp.zeros_like(ib_sum), 1)],
        2,
    )
    small_grad = jnp.pad(small_grad, ((0, 0), (0, 0), (0, small_pad - n_small)))
    small_grad = small_grad.reshape(K, 2, small_pad // 128, 128).astype(low)
    g_outer, g_inner, g_out, g_qkv, g_small = (
        lax.psum_scatter(v, CHIPS, scatter_dimension=0, tiled=False).astype(wide)
        for v in (
            g_outer.reshape(K, 2, f // 2, D),
            g_inner.reshape(K, 2, r, FF // 2),
            g_out.reshape(K, 2, r, hw),
            g_qkv.reshape(K, 2, r, 3 * hw),
            small_grad,
        )
    )
    wide_rows = jnp.concatenate([g_qkv, g_out, g_inner], 2)
    mine = pick(wide_rows, core, 0)
    theirs = swap_core(pick(wide_rows, 1 - core, 0))

    def whole(a, b, parts):
        a, b = a.reshape(r, parts, 1, -1), b.reshape(r, parts, 1, -1)
        return by_core(a, b, 2).reshape(r, -1)

    outs = []
    for i in range(4):
        outs.append(whole(mine[:, i * hw : (i + 1) * hw], theirs[:, i * hw : (i + 1) * hw], 1))
    outs.append(whole(mine[:, 4 * hw :], theirs[:, 4 * hw :], K))
    outs.append(g_outer.reshape(f, D))
    g_small = g_small.reshape(2, small_pad)[:, :n_small]
    g_small = pick(g_small, core, 0) + swap_core(pick(g_small, 1 - core, 0))
    sv = {n: g_small[i * r : (i + 1) * r] for i, n in enumerate(names)}
    return (layer_out, frames_grad) + tuple(outs) + (
        sv["qb"], sv["vb"], sv["ob"], g_small[8 * r :], sv["ub"],
        sv["g1"], sv["s1"], sv["g2"], sv["s2"],
    )


VECTORS = ("qb", "vb", "ob", "ub", "g1", "s1", "g2", "s2")


def linked_body(
    Z,
    frames,
    clip_ids,
    query_weight,
    key_weight,
    value_weight,
    output_weight,
    inner_weight,
    outer_weight,
    query_bias,
    value_bias,
    output_bias,
    inner_bias,
    outer_bias,
    first_gain,
    first_shift,
    second_gain,
    second_shift,
    out_cotangent,
):
    K = 4 * Z
    R, D = frames.shape[2], frames.shape[3]
    FF = inner_weight.shape[1]
    r = query_weight.shape[0]
    f = outer_weight.shape[0]
    hw = D // 2
    heads = H // 2
    half = Z // 2
    core = lax.axis_index("core")
    first_core = core == 0
    zz = lax.axis_index("zz")
    micro = zz // half
    first_half = micro == 0
    place = zz % half
    tile = 256

    def swap_core(v):
        return lax.ppermute(v, "core", [(0, 1), (1, 0)])

    def by_core(own, other, axis):
        return jnp.where(
            first_core,
            jnp.concatenate([own, other], axis),
            jnp.concatenate([other, own], axis),
        )

    def pick(v, index, axis):
        return lax.dynamic_index_in_dim(v, index, axis, keepdims=False)

    def own_columns(v):
        return lax.dynamic_slice_in_dim(v, core * hw, hw, v.ndim - 1)

    small = jnp.concatenate(
        [
            jnp.stack(
                [
                    query_bias, value_bias, output_bias, outer_bias,
                    first_gain, first_shift, second_gain, second_shift,
                ]
            ),
            inner_bias.reshape(f // r, r),
        ]
    )
    small = jnp.pad(small, ((0, 16 - small.shape[0]), (0, 128 - r)))

    ids = pick(clip_ids[:, 0], micro, 0).reshape(2, half, 2 * R)
    ids_q = pick(ids, place, 1).reshape(4 * R)
    ids_far = pick(ids, 1 - place, 1).reshape(4 * R)
    tag = jnp.arange(TAGS, dtype=jnp.int32)[:, None]
    tags_q = jnp.where(ids_q[None, :] == tag, 0.0, masked_score).astype(low)
    tags_k = (jnp.stack([ids_q, ids_far])[:, None, :] == tag[None]).astype(low)

    weights = (query_weight, key_weight, value_weight, output_weight, inner_weight, outer_weight)
    fw = forward_linked(frames, out_cotangent, weights, small, tags_q, tags_k, Z, heads, tile)
    vec = {n: fw.vectors[i] for i, n in enumerate(VECTORS)}
    cot = fw.cot_rows.reshape(4 * R, D)
    active, slope, middle = fw.active, fw.slope, fw.middle
    normed_two = fw.normed_two
    g_outer = dims(active, cot, 0, 0).astype(low)

    grad_active = dims(cot, fw.w_outer, 1, 1)
    inner_grad = (grad_active * slope).astype(low)
    part_two = dims(inner_grad, fw.w_inner, 1, 1)
    grad_two = part_two + swap_core(part_two.astype(low)).astype(wide)
    xhat_two, inverse_two = row_stats(middle)
    middle_grad = cot.astype(wide) + norm_pull(grad_two, vec["g2"], xhat_two, inverse_two)
    branch_grad = middle_grad.astype(low)
    w_heads = lax.dynamic_slice_in_dim(fw.w_out, core * hw, hw, 1)
    mixed_grad = sum(
        dims(w_heads[b], branch_grad[:, b * hw : (b + 1) * hw], 1, 1) for b in (0, 1)
    ).astype(low)
    halves = 0.5
    none = jnp.zeros((D,), wide)
    small_part = jnp.stack(
        [
            none,
            none,
            halves * jnp.sum(branch_grad.astype(wide), 0),
            halves * jnp.sum(cot.astype(wide), 0),
            none,
            none,
            halves * jnp.sum(grad_two * xhat_two, 0),
            halves * jnp.sum(grad_two, 0),
        ]
    )
    hidden_sums = jnp.sum(inner_grad.astype(wide), 0)[None]
    hidden_sums = by_core(hidden_sums, jnp.zeros_like(hidden_sums), 1)
    bw = backward_linked(
        (
            fw.qkv, fw.far, tags_q, tags_k, fw.mixed, fw.logs, mixed_grad, branch_grad,
            fw.vectors, small_part, hidden_sums,
        ),
        (
            fw.x_rows, middle_grad.reshape(4, R, D), fw.normed, fw.w_qkv, active, g_outer, inner_grad,
            normed_two, fw.w_outer, middle.reshape(4, R, D),
        ),
        Z, heads, tile,
    )
    sv = {n: bw.small[i, :r] for i, n in enumerate(VECTORS)}
    ib = bw.small[8 : 8 + f // r, :r].reshape(f)
    return (
        bw.layer_out, bw.frames_grad, bw.query, bw.key, bw.value, bw.output, bw.inner, bw.outer,
        sv["qb"], sv["vb"], sv["ob"], ib, sv["ub"],
        sv["g1"], sv["s1"], sv["g2"], sv["s2"],
    )


def solution(mesh):
    C, S = mesh.shape["clip"], mesh.shape["seq"]
    fine = Mesh(mesh.devices.reshape(2, C // 2, S // 2, 2), ("cy", "cx", "zz", "core"))
    clip, seq = ("cy", "cx"), ("zz", "core")
    every = clip + seq
    rows, mat, vec = P(None, clip, seq, None), P(every, None), P(every)
    in_specs = (rows, P(None, clip, None)) + (mat,) * 6 + (vec,) * 9 + (rows,)
    out_specs = (rows, rows) + (mat,) * 6 + (vec,) * 9
    linked = C == 4 and S == 8
    run = functools.partial(linked_body, S // 2) if linked else functools.partial(general_body, C, S // 2)
    return jax.shard_map(
        run,
        mesh=fine,
        in_specs=in_specs,
        out_specs=out_specs,
        check_vma=False,
    )
```
